256 devices in a mesh: dp: 4 (over z_lo), context: 64 (over z_hi, x, y, core).
Axes of the slice: x: 4, y: 4, z: 8 (z_hi: 2, z_lo: 4; z = z_hi * 4 + z_lo), core: 2. Of those that a mesh axis runs over, the one named last changes fastest.
Arguments:
- queries: bfloat16 [4, 12288, 4096], P('dp', 'context'), may hold values from -6 to 6
- key_rows: bfloat16 [4, 12288, 4096], P('dp', 'context'), may hold values from -6 to 6
- value_rows: bfloat16 [4, 12288, 4096], P('dp', 'context'), may hold values from -6 to 6
- out_grad: bfloat16 [4, 12288, 4096], P('dp', 'context'), may hold values from -16 to 16
- log_decay: float32 [4, 12288, 32], P('dp', 'context'), may hold values from -0.8 to 0
- norm_gain: float32 [4096], replicated, may hold values from 0.1 to 1.9
Outputs:
- query_grad: bfloat16 [4, 12288, 4096], P('dp', 'context')
- key_grad: bfloat16 [4, 12288, 4096], P('dp', 'context')
- value_grad: bfloat16 [4, 12288, 4096], P('dp', 'context')
- gain_grad: float32 [4096], P(('dp', 'context'))
The draws below stay inside these ranges and needn't reach their ends.
All inputs are finite; a program needn't handle non-finite values.
Results may differ from the reference program's by a relative error of at most 0.0058.
Values sent between devices are 32-bit elements; how exact they have to be, the bound alone decides.
No kernel may reach another device: no remote copies, remote signals or barrier semaphores. Data moves between devices by JAX's collectives and lax.ppermute only.
A program may use at most 128 MiB of HBM per device.

```python
import jax
import jax.numpy as jnp
from jax import lax

LOCAL_HEADS = 32
HD = 128
TOK_DEV = 192
SEQUENCE_COUNT = 4
SEQUENCE_LENGTH = 12288
FEAT = 4096


def draw_log_decay(key, part):
    random_key_quick, random_key_jitter, random_key_block, random_key_locate, random_key_spike = jax.random.split(key, 5)
    fast_share = 0.5
    fast_heads = jax.random.uniform(random_key_quick, (SEQUENCE_COUNT, 1, LOCAL_HEADS)) < fast_share
    jitter_amount = jax.random.uniform(random_key_jitter, (SEQUENCE_COUNT, SEQUENCE_LENGTH, LOCAL_HEADS), minval=0.5, maxval=1.5)
    block_count = SEQUENCE_LENGTH // TOK_DEV
    per_block_values = jnp.exp(jax.random.uniform(random_key_block, (SEQUENCE_COUNT, block_count, 1, LOCAL_HEADS), minval=-0.7, maxval=0.7))
    per_block_values = jnp.broadcast_to(per_block_values, (SEQUENCE_COUNT, block_count, TOK_DEV, LOCAL_HEADS)).reshape(SEQUENCE_COUNT, SEQUENCE_LENGTH, LOCAL_HEADS)
    baseline_rate = jnp.where(fast_heads, 1.0 / 40.0, 0.5 / SEQUENCE_LENGTH)
    locations = jax.random.randint(random_key_locate, (SEQUENCE_COUNT, 3, LOCAL_HEADS), 0, SEQUENCE_LENGTH)
    token_position = lax.broadcasted_iota(jnp.int32, (SEQUENCE_COUNT, SEQUENCE_LENGTH, LOCAL_HEADS), 1)
    spike_count = (token_position == locations[:, 0:1, :]) | (token_position == locations[:, 1:2, :]) | (token_position == locations[:, 2:3, :])
    spike_logits = jnp.log(jax.random.uniform(random_key_spike, (SEQUENCE_COUNT, SEQUENCE_LENGTH, LOCAL_HEADS), minval=0.5, maxval=0.8))
    return (-(baseline_rate * jitter_amount * per_block_values) + jnp.where(spike_count, spike_logits, 0.0)).astype(jnp.float32)


def spiked(values, own_key, source, target, shards_of, factor):
    def block_of(axis_at):
        return (jnp.arange(values.shape[axis_at]) // (values.shape[axis_at] // shards_of)).reshape((-1,) + (1,) * (values.ndim - 1 - axis_at))

    first = jax.random.permutation(own_key, shards_of)[block_of(target)]
    far = (block_of(target) + shards_of // 2) % shards_of
    return jnp.where((block_of(source) == first) | (block_of(source) == far), factor * values, values)


def shard_levels(own_key, shape, cuts, low, largest):
    def one(axis_at, shards_of):
        heights = jax.random.uniform(jax.random.fold_in(jax.random.fold_in(own_key, 6), axis_at), (shards_of,), jnp.float32, low / len(cuts), largest / len(cuts))
        return jnp.repeat(jnp.exp(heights), shape[axis_at] // shards_of).reshape((-1,) + (1,) * (len(shape) - axis_at - 1))

    level = one(*cuts[0])
    for cut in cuts[1:]:
        level = level * one(*cut)
    return level


def centred(stream_key, shape, scale, most, cuts=(), kind=jnp.bfloat16):
    loudness = shard_levels(stream_key, shape, cuts, -0.22, 0.18) if cuts else 1.0
    array = jax.random.normal(stream_key, shape, jnp.float32) * scale * loudness
    return jnp.minimum(jnp.maximum(array, -most), most).astype(kind)


def noise_with(stream_key, extent, scale, bound, pieces, heavy, held_as=jnp.bfloat16):
    result = scale * jax.random.normal(stream_key, extent, jnp.float32)
    if pieces:
        result = result * shard_levels(stream_key, extent, pieces, -0.22, 0.18)
    return jnp.clip(spiked(result, jax.random.fold_in(stream_key, 3), *heavy), -bound, bound).astype(held_as)


def setup_inputs(seed: int = 0) -> dict:
    seeds = jax.random.split(jax.random.key(seed), 7)
    return {
        "queries": centred(seeds[0], (SEQUENCE_COUNT, SEQUENCE_LENGTH, FEAT), 1.0, 6.0, ((0, 4), (1, 64))),
        "key_rows": centred(seeds[1], (SEQUENCE_COUNT, SEQUENCE_LENGTH, FEAT), 1.0, 6.0, ((0, 4), (1, 64))),
        "value_rows": centred(seeds[2], (SEQUENCE_COUNT, SEQUENCE_LENGTH, FEAT), 1.0, 6.0, ((0, 4), (1, 64))),
        "out_grad": noise_with(seeds[3], (SEQUENCE_COUNT, SEQUENCE_LENGTH, FEAT), 1.0, 16.0, ((0, 4), (1, 64)), (1, 2, 64, 4.0)),
        "log_decay": draw_log_decay(jax.random.fold_in(seeds[6], 71), 0),
        "norm_gain": jnp.clip(1.0 + 0.18 * jax.random.normal(seeds[5], (FEAT,), jnp.float32), 0.1, 1.9),
    }


EPSILON = 1e-06
HIGHEST = lax.Precision.HIGHEST

def rounded(values_in):
    return lax.optimization_barrier(values_in.astype(jnp.bfloat16)).astype(jnp.float32)

def decay_table(cumulative):
    positions = cumulative.shape[0]
    turned = jnp.transpose(cumulative)
    exponent = turned[:, :, None] - turned[:, None, :]
    row_ids = lax.broadcasted_iota(jnp.int32, (positions, positions), 0)
    col_ids = lax.broadcasted_iota(jnp.int32, (positions, positions), 1)
    return jnp.exp(jnp.where((row_ids >= col_ids)[None], exponent, -jnp.inf))

def ref_state(random_key_block, value_block, decay_block):
    cumulative = jnp.cumsum(decay_block, axis=0)
    block_log = cumulative[-1]
    shrink = jnp.exp(block_log[None, :] - cumulative)[:, :, None]
    key_late = rounded(random_key_block.astype(jnp.float32) * shrink)
    state_local = jnp.einsum('uhk,uhd->hkd', key_late, value_block.astype(jnp.float32), precision=HIGHEST)
    return (block_log, state_local)

def ref_main(query_block, random_key_block, value_block, grad_block, decay_block, incoming, norm_gain):
    positions, head_count, head_size = query_block.shape
    query_wide = query_block.astype(jnp.float32)
    key_wide = random_key_block.astype(jnp.float32)
    value_wide = value_block.astype(jnp.float32)
    cumulative = jnp.cumsum(decay_block, axis=0)
    growth = jnp.exp(cumulative)[:, :, None]
    decay = decay_table(cumulative)
    scores = jnp.einsum('thd,uhd->htu', query_wide, key_wide, precision=HIGHEST)
    fwd_weights = rounded(scores * decay)
    attended = jnp.einsum('htu,uhd->thd', fwd_weights, value_wide, precision=HIGHEST)
    attended = attended + jnp.einsum('thk,hkd->thd', query_wide * growth, incoming, precision=HIGHEST)
    attended = attended.reshape(positions, head_count * head_size)
    inverse = lax.rsqrt(lax.optimization_barrier(jnp.mean(attended * attended, axis=1, keepdims=True)) + EPSILON)
    normed = attended * inverse
    grad_wide = grad_block.astype(jnp.float32)
    scaled = norm_gain[None, :] * grad_wide
    projected = lax.optimization_barrier(jnp.mean(scaled * normed, axis=1, keepdims=True))
    out_delta = rounded(inverse * (scaled - normed * projected)).reshape(positions, head_count, head_size)
    delta_scores = jnp.einsum('thd,uhd->htu', out_delta, value_wide, precision=HIGHEST)
    bwd_weights = rounded(delta_scores * decay)
    query_early = rounded(query_wide * growth)
    moment = jnp.einsum('thk,thd->hkd', query_early, out_delta, precision=HIGHEST)
    query_grad = jnp.einsum('htu,uhd->thd', bwd_weights, key_wide, precision=HIGHEST)
    query_grad = query_grad + jnp.einsum('thd,hkd->thk', out_delta * growth, incoming, precision=HIGHEST)
    key_local = jnp.einsum('htu,thd->uhd', bwd_weights, query_wide, precision=HIGHEST)
    value_local = jnp.einsum('htu,thd->uhd', fwd_weights, out_delta, precision=HIGHEST)
    gain_term = lax.optimization_barrier(jnp.sum(grad_wide * normed, axis=0))
    return (query_grad.astype(jnp.bfloat16), key_local, value_local, moment, gain_term)

def ref_finish(random_key_block, value_block, decay_block, key_local, value_local, later):
    cumulative = jnp.cumsum(decay_block, axis=0)
    block_log = cumulative[-1]
    shrink = jnp.exp(block_log[None, :] - cumulative)[:, :, None]
    key_grad = key_local + jnp.einsum('uhd,hkd->uhk', value_block.astype(jnp.float32) * shrink, later, precision=HIGHEST)
    value_grad = value_local + jnp.einsum('uhk,hkd->uhd', random_key_block.astype(jnp.float32) * shrink, later, precision=HIGHEST)
    return (key_grad.astype(jnp.bfloat16), value_grad.astype(jnp.bfloat16))

def reference(queries, key_rows, value_rows, out_grad, log_decay, norm_gain):
    block_count = SEQUENCE_LENGTH // TOK_DEV
    query_list, key_list, value_list = ([], [], [])
    gain_total = jnp.zeros((FEAT,), jnp.float32)
    zeros_state = jnp.zeros((LOCAL_HEADS, HD, HD), jnp.float32)
    for sequence in range(SEQUENCE_COUNT):
        query_blocks = queries[sequence].reshape(block_count, TOK_DEV, LOCAL_HEADS, HD)
        key_blocks = key_rows[sequence].reshape(block_count, TOK_DEV, LOCAL_HEADS, HD)
        value_blocks = value_rows[sequence].reshape(block_count, TOK_DEV, LOCAL_HEADS, HD)
        grad_blocks = out_grad[sequence].reshape(block_count, TOK_DEV, FEAT)
        decay_blocks = log_decay[sequence].reshape(block_count, TOK_DEV, LOCAL_HEADS)
        block_logs, local_states = lax.map(lambda inputs: ref_state(*inputs), (key_blocks, value_blocks, decay_blocks))

        def forward_step(running, element):
            block_log, state_local = element
            return (jnp.exp(block_log)[:, None, None] * running + state_local, running)
        unused_end, incoming = lax.scan(forward_step, zeros_state, (block_logs, local_states))
        query_grad, key_local, value_local, moments, gain_terms = lax.map(lambda inputs: ref_main(*inputs, norm_gain), (query_blocks, key_blocks, value_blocks, grad_blocks, decay_blocks, incoming))

        def backward_step(running, element):
            block_log, moment = element
            return (moment + jnp.exp(block_log)[:, None, None] * running, running)
        unused_start, later = lax.scan(backward_step, zeros_state, (block_logs, moments), reverse=True)
        key_grad, value_grad = lax.map(lambda inputs: ref_finish(*inputs), (key_blocks, value_blocks, decay_blocks, key_local, value_local, later))
        query_list.append(query_grad.reshape(SEQUENCE_LENGTH, FEAT))
        key_list.append(key_grad.reshape(SEQUENCE_LENGTH, FEAT))
        value_list.append(value_grad.reshape(SEQUENCE_LENGTH, FEAT))
        gain_total = gain_total + lax.optimization_barrier(jnp.sum(gain_terms, axis=0))
    gain_grad = gain_total / jnp.sqrt(jnp.float32(SEQUENCE_COUNT * SEQUENCE_LENGTH))
    return (jnp.stack(query_list), jnp.stack(key_list), jnp.stack(value_list), gain_grad)
```

```python
import functools
import math

import jax
import jax.numpy as jnp
from jax import lax
from jax.experimental import pallas as pl
from jax.experimental.pallas import tpu as pltpu
from jax.sharding import Mesh, PartitionSpec as P

EPSILON = 1e-06
HIGHEST = lax.Precision.HIGHEST
F32 = jnp.float32
BF16 = jnp.bfloat16
T = 192
HD = 128
GH = 8
GW = GH * HD
NG = 4
HALF = NG // 2
NC = 16
ALL = ("dp", "zh", "x", "y", "core")


def dot(a, b, ca, cb):
    return lax.dot_general(a, b, (((ca,), (cb,)), ((), ())), preferred_element_type=F32)


def lanes(j):
    return slice(j * HD, (j + 1) * HD)


def split_state(state, axis):
    high = state.astype(BF16)
    low = (state - high.astype(F32)).astype(BF16)
    return jnp.concatenate([high, low], axis)


def rows_by_state(rows, state):
    return dot(jnp.concatenate([rows, rows], 1), split_state(state, 0), 1, 0)


def rows_by_state_t(rows, state):
    return dot(jnp.concatenate([rows, rows], 1), split_state(state, 1), 1, 1)


def decay_table(col, row):
    row_ids = lax.broadcasted_iota(jnp.int32, (T, T), 0)
    col_ids = lax.broadcasted_iota(jnp.int32, (T, T), 1)
    return jnp.exp(jnp.where(row_ids >= col_ids, col - row, -jnp.inf))


def states_of(k_ref, v_ref, cum, s_ref):
    last = cum[T - 1 : T, :]
    shrink = jnp.exp(last - cum)
    for j in range(GH):
        late = (k_ref[:, lanes(j)].astype(F32) * shrink[:, j : j + 1]).astype(BF16)
        s_ref[j, :HD, :] = dot(late, v_ref[:, lanes(j)], 0, 0)
        s_ref[j, HD:, :] = jnp.broadcast_to(last[:, j : j + 1], (8, HD))


def state_first_kernel(c_ref, k_ref, v_ref, ld_ref, s_ref, col_ref, row_ref):
    i = pl.program_id(0)

    @pl.when(i == 0)
    def _():
        upper = (
            lax.broadcasted_iota(jnp.int32, (T, T), 0) <= lax.broadcasted_iota(jnp.int32, (T, T), 1)
        ).astype(F32)
        logs = ld_ref[...]
        row_ref[...] = lax.dot_general(
            logs, upper, (((1,), (0,)), ((), ())), precision=HIGHEST, preferred_element_type=F32
        )
        col = lax.dot_general(
            upper, logs, (((0,), (1,)), ((), ())), precision=HIGHEST, preferred_element_type=F32
        )
        for g in range(NG):
            col_ref[g] = col[:, g * GH : (g + 1) * GH]

    states_of(k_ref, v_ref, col_ref[(1 - c_ref[0]) * HALF + i], s_ref)


def state_second_kernel(c_ref, k_ref, v_ref, col_ref, s_ref):
    states_of(k_ref, v_ref, col_ref[c_ref[0] * HALF + pl.program_id(0)], s_ref)


def combine_kernel(upward, c_ref, own_ref, got_ref, lo_ref, lg_ref, p_ref):
    first = c_ref[0] == 0 if upward else c_ref[0] == 1
    for j in range(GH):
        log_own, log_got = lo_ref[j, 0:1, :], lg_ref[j, 0:1, :]
        scale_own = jnp.where(first, jnp.exp(log_got), 1.0)
        scale_got = jnp.where(first, 1.0, jnp.exp(log_own))
        p_ref[j, :HD, :] = scale_own * own_ref[j] + scale_got * got_ref[j]
        if upward:
            p_ref[j, HD:, :] = jnp.broadcast_to(log_own + log_got, (8, HD))


def total_kernel(upward, m_ref, l_ref, t_ref):
    run = jnp.zeros((HD, HD), F32)
    for i in range(NC) if upward else reversed(range(NC)):
        run = jnp.exp(l_ref[i, 0:1, :]) * run + m_ref[i]
    t_ref[...] = run


def scan_kernel(upward, m_ref, l_ref, t_ref, o_ref):
    run = t_ref[...]
    for i in range(NC) if upward else reversed(range(NC)):
        o_ref[i] = run
        run = jnp.exp(l_ref[i, 0:1, :]) * run + m_ref[i]


def send_kernel(upward, c_ref, d_ref, own_ref, lo_ref, o_ref):
    step_on = c_ref[0] == 0 if upward else c_ref[0] == 1
    for j in range(GH):
        scale = jnp.where(step_on, jnp.exp(lo_ref[j, 0:1, :]), 1.0)
        keep = jnp.where(step_on, 1.0, 0.0)
        o_ref[j] = scale * d_ref[j] + keep * own_ref[j]


def own_state(upward, c_ref, d_ref, got_ref, lg_ref, j):
    at_edge = c_ref[0] == 0 if upward else c_ref[0] == 1
    scale = jnp.where(at_edge, 1.0, jnp.exp(lg_ref[j, 0:1, :]))
    keep = jnp.where(at_edge, 0.0, 1.0)
    return scale * d_ref[j] + keep * got_ref[j]


def forward_kernel(own, c_ref, q_ref, k_ref, v_ref, col_ref, row_ref, fw_ref, in_ref):
    half = c_ref[0] if own else 1 - c_ref[0]
    cum = col_ref[half * HALF + pl.program_id(0)]
    for j in range(GH):
        decay = decay_table(cum[:, j : j + 1], row_ref[j : j + 1, :])
        scores = dot(q_ref[:, lanes(j)], k_ref[:, lanes(j)], 1, 1)
        weights = (scores * decay).astype(BF16)
        fw_ref[j] = weights
        in_ref[:, lanes(j)] = dot(weights, v_ref[:, lanes(j)], 1, 0)


def attend_group(q_ref, g_ref, gain_ref, cum, in_ref, state_at, att_ref, sq_ref, pr_ref):
    growth = jnp.exp(cum)
    squares = jnp.zeros((T, HD), F32)
    products = jnp.zeros((T, HD), F32)
    for j in range(GH):
        att = in_ref[:, lanes(j)] + growth[:, j : j + 1] * rows_by_state(q_ref[:, lanes(j)], state_at(j))
        att_ref[:, lanes(j)] = att
        squares += att * att
        products += att * (gain_ref[:, lanes(j)] * g_ref[:, lanes(j)].astype(F32))
    sq_ref[...] += squares
    pr_ref[...] += products


def attend_own_kernel(
    c_ref, q_ref, g_ref, gain_ref, col_ref, in_ref, d_ref, got_ref, lg_ref,
    att_ref, i_ref, sq_ref, pr_ref,
):
    @pl.when(pl.program_id(0) == 0)
    def _():
        sq_ref[...] = jnp.zeros_like(sq_ref)
        pr_ref[...] = jnp.zeros_like(pr_ref)

    def state_at(j):
        state = own_state(True, c_ref, d_ref, got_ref, lg_ref, j)
        i_ref[j] = state
        return state

    cum = col_ref[c_ref[0] * HALF + pl.program_id(0)]
    attend_group(q_ref, g_ref, gain_ref, cum, in_ref, state_at, att_ref, sq_ref, pr_ref)


def delta_group(q_ref, g_ref, gain_ref, cum, att_ref, inverse, mean, od_ref, m_ref, gt_ref):
    growth = jnp.exp(cum)
    for j in range(GH):
        grad = g_ref[:, lanes(j)].astype(F32)
        normed = att_ref[:, lanes(j)] * inverse
        delta = (inverse * (gain_ref[:, lanes(j)] * grad - normed * mean)).astype(BF16)
        od_ref[:, lanes(j)] = delta
        gt_ref[:, lanes(j)] = jnp.sum(grad * normed, axis=0, keepdims=True)
        early = (q_ref[:, lanes(j)].astype(F32) * growth[:, j : j + 1]).astype(BF16)
        m_ref[j] = dot(early, delta, 0, 0)


def attend_other_kernel(
    c_ref, q_ref, g_ref, gain_ref, col_ref, in_ref, i_ref, sq_in, pr_in,
    od_ref, m_ref, gt_ref, inv_ref, mean_ref, att_ref, sq_ref, pr_ref,
):
    step = pl.program_id(0)
    group = jnp.where(step < HALF, step, 2 * HALF - 1 - step)
    cum = col_ref[(1 - c_ref[0]) * HALF + group]

    @pl.when(step == 0)
    def _():
        sq_ref[...] = sq_in[...]
        pr_ref[...] = pr_in[...]

    @pl.when(step < HALF)
    def _():
        attend_group(
            q_ref, g_ref, gain_ref, cum, in_ref, lambda j: i_ref[j], att_ref.at[group], sq_ref, pr_ref
        )

    @pl.when(step == HALF)
    def _():
        features = NG * GW
        inverse = lax.rsqrt(jnp.sum(sq_ref[...], axis=1, keepdims=True) * (1.0 / features) + EPSILON)
        mean = inverse * (jnp.sum(pr_ref[...], axis=1, keepdims=True) * (1.0 / features))
        inv_ref[...] = jnp.broadcast_to(inverse, (T, HD))
        mean_ref[...] = jnp.broadcast_to(mean, (T, HD))

    @pl.when(step >= HALF)
    def _():
        delta_group(
            q_ref, g_ref, gain_ref, cum, att_ref.at[group], inv_ref[...], mean_ref[...],
            od_ref, m_ref, gt_ref,
        )


def delta_own_kernel(
    c_ref, q_ref, g_ref, gain_ref, col_ref, att_ref, inv_ref, mean_ref, od_ref, m_ref, gt_ref
):
    cum = col_ref[c_ref[0] * HALF + pl.program_id(0)]
    delta_group(
        q_ref, g_ref, gain_ref, cum, att_ref, inv_ref[...], mean_ref[...], od_ref, m_ref, gt_ref
    )


def backward_kernel(
    own, c_ref, od_ref, q_ref, k_ref, v_ref, fw_ref, col_ref, row_ref, i_ref, *rest
):
    qg_ref, ki_ref, vi_ref = rest[-3:]
    half = c_ref[0] if own else 1 - c_ref[0]
    cum = col_ref[half * HALF + pl.program_id(0)]
    growth = jnp.exp(cum)
    for j in range(GH):
        at = lanes(j)
        decay = decay_table(cum[:, j : j + 1], row_ref[j : j + 1, :])
        delta = od_ref[:, at]
        weights = (dot(delta, v_ref[:, at], 1, 1) * decay).astype(BF16)
        inter = growth[:, j : j + 1] * rows_by_state_t(delta, i_ref[j])
        qg_ref[:, at] = (dot(weights, k_ref[:, at], 1, 0) + inter).astype(BF16)
        ki_ref[:, at] = dot(weights, q_ref[:, at], 0, 0)
        vi_ref[:, at] = dot(fw_ref[j], delta, 0, 0)


def finish_group(k_ref, v_ref, cum, ki_ref, vi_ref, state_at, kg_ref, vg_ref):
    shrink = jnp.exp(cum[T - 1 : T, :] - cum)
    for j in range(GH):
        at = lanes(j)
        state = state_at(j)
        scale = shrink[:, j : j + 1]
        kg_ref[:, at] = (ki_ref[:, at] + scale * rows_by_state_t(v_ref[:, at], state)).astype(BF16)
        vg_ref[:, at] = (vi_ref[:, at] + scale * rows_by_state(k_ref[:, at], state)).astype(BF16)


def finish_own_kernel(
    c_ref, k_ref, v_ref, col_ref, ki_ref, vi_ref, d_ref, got_ref, lg_ref, kg_ref, vg_ref
):
    cum = col_ref[c_ref[0] * HALF + pl.program_id(0)]
    finish_group(
        k_ref, v_ref, cum, ki_ref, vi_ref,
        lambda j: own_state(False, c_ref, d_ref, got_ref, lg_ref, j), kg_ref, vg_ref,
    )


def finish_other_kernel(
    c_ref, k_ref, v_ref, col_ref, ki_ref, vi_ref, x_ref, kg_in, vg_in, kg_ref, vg_ref
):
    cum = col_ref[(1 - c_ref[0]) * HALF + pl.program_id(0)]
    finish_group(k_ref, v_ref, cum, ki_ref, vi_ref, lambda j: x_ref[j], kg_ref, vg_ref)


def call(kernel, name, grid, in_specs, out_specs, out_shape, args, flops, scratch=(), aliases=None):
    nbytes = sum(math.prod(s.shape) * s.dtype.itemsize for s in out_shape)
    nbytes += sum(math.prod(a.shape) * a.dtype.itemsize for a in args[1:])
    return pl.pallas_call(
        kernel,
        name=name,
        grid_spec=pltpu.PrefetchScalarGridSpec(
            num_scalar_prefetch=1,
            grid=grid,
            in_specs=in_specs,
            out_specs=out_specs,
            scratch_shapes=scratch,
        ),
        out_shape=out_shape,
        input_output_aliases=aliases or {},
        compiler_params=pltpu.CompilerParams(vmem_limit_bytes=24 << 20),
        cost_estimate=pl.CostEstimate(flops=flops, bytes_accessed=nbytes, transcendentals=0),
    )(*args)


def shape(dims, dtype=F32):
    return jax.ShapeDtypeStruct(dims, dtype)


def half_of(own, c_ref):
    return c_ref[0] if own else 1 - c_ref[0]


def wide(own, group=lambda i: i):
    return pl.BlockSpec((None, T, GW), lambda i, c: (0, 0, half_of(own, c) * HALF + group(i)))


def narrow(group=lambda i: i):
    return pl.BlockSpec((T, GW), lambda i, c: (0, group(i)))


def gain_block(own, group=lambda i: i):
    return pl.BlockSpec((1, GW), lambda i, c: (0, half_of(own, c) * HALF + group(i)))


def row_block(own):
    return pl.BlockSpec((GH, T), lambda i, c: (half_of(own, c) * HALF + i, 0))


def state_block(rows=HD, group=lambda i: i):
    return pl.BlockSpec((GH, rows, HD), lambda i, c: (group(i), 0, 0))


LOG_BLOCK = pl.BlockSpec((GH, 8, HD), lambda i, c: (i, HD // 8, 0))
COL_WHOLE = pl.BlockSpec((NG, T, GH), lambda i, c: (0, 0, 0))
STAT_WHOLE = pl.BlockSpec((T, HD), lambda i, c: (0, 0))
ANY = pl.BlockSpec(memory_space=pl.ANY)
STATES = shape((NC, HD, HD))
LOGGED = shape((NC, HD + 8, HD))
HALF_F32 = shape((T, HALF * GW))
HALF_BF16 = shape((T, HALF * GW), BF16)
WHOLE_BF16 = shape((1, T, NG * GW), BF16)
STAT = shape((T, HD))
GAIN_ROW = shape((1, HALF * GW))
MM = 2 * T * HD * HD * NC
SM = 2 * T * T * HD * NC


def swap_cores(values):
    return lax.ppermute(values, "core", [(0, 1), (1, 0)])


def chips_all_to_all(values):
    return lax.all_to_all(values, ("x", "y"), split_axis=0, concat_axis=0, tiled=True)


def scan_over_chips(upward, got, logs):
    whole_m = pl.BlockSpec((NC, HD, HD), lambda i: (0, 0, 0))
    whole_l = pl.BlockSpec((NC, 8, HD), lambda i: (0, HD // 8, 0))
    whole_t = pl.BlockSpec((HD, HD), lambda i: (0, 0))
    params = pltpu.CompilerParams(vmem_limit_bytes=24 << 20)
    total = pl.pallas_call(
        functools.partial(total_kernel, upward),
        name="half_total",
        grid=(1,),
        in_specs=[whole_m, whole_l],
        out_specs=whole_t,
        out_shape=shape((HD, HD)),
        compiler_params=params,
    )(got, logs)
    before = lax.ppermute(total, "zh", [(0, 1)] if upward else [(1, 0)])
    return pl.pallas_call(
        functools.partial(scan_kernel, upward),
        name="chip_scan",
        grid=(1,),
        in_specs=[whole_m, whole_l, whole_t],
        out_specs=whole_m,
        out_shape=STATES,
        compiler_params=params,
    )(got, logs, before)


def per_device(queries, key_rows, value_rows, out_grad, log_decay, norm_gain):
    core = lax.axis_index("core").astype(jnp.int32).reshape(1)
    q, k, v, g = queries, key_rows, value_rows, out_grad
    gain = norm_gain.reshape(1, NG * GW)
    logs = jnp.transpose(log_decay[0])

    sent, col, row = call(
        state_first_kernel, "states_other", (HALF,),
        [wide(False), wide(False), pl.BlockSpec((NG * GH, T), lambda i, c: (0, 0))],
        [state_block(HD + 8), COL_WHOLE, pl.BlockSpec((NG * GH, T), lambda i, c: (0, 0))],
        [LOGGED, shape((NG, T, GH)), shape((NG * GH, T))],
        (core, k, v, logs), MM,
    )
    got = swap_cores(sent)
    (own,) = call(
        state_second_kernel, "states_own", (HALF,),
        [wide(True), wide(True), COL_WHOLE], [state_block(HD + 8)], [LOGGED],
        (core, k, v, col), MM,
    )
    (chip_total,) = call(
        functools.partial(combine_kernel, True), "chip_total", (HALF,),
        [state_block(), state_block(), LOG_BLOCK, LOG_BLOCK], [state_block(HD + 8)], [LOGGED],
        (core, own, got, own, got), 0,
    )
    gathered = chips_all_to_all(chip_total)

    weights, inside = {}, {}
    for mine in (True, False):
        weights[mine], inside[mine] = call(
            functools.partial(forward_kernel, mine), "forward_inside", (HALF,),
            [wide(mine), wide(mine), wide(mine), COL_WHOLE, row_block(mine)],
            [pl.BlockSpec((GH, T, T), lambda i, c: (i, 0, 0)), narrow()],
            [shape((NC, T, T), BF16), HALF_F32],
            (core, q, k, v, col, row), 2 * SM,
        )

    scanned = chips_all_to_all(scan_over_chips(True, gathered, gathered))
    (onward,) = call(
        functools.partial(send_kernel, True), "onward", (HALF,),
        [state_block(), state_block(), LOG_BLOCK], [state_block()], [STATES],
        (core, scanned, own, own), 0,
    )
    state_other = swap_cores(onward)
    att_own, state_own, squares, products = call(
        attend_own_kernel, "attend_own", (HALF,),
        [wide(True), wide(True), gain_block(True), COL_WHOLE, narrow(), state_block(), state_block(),
         LOG_BLOCK],
        [narrow(), state_block(), STAT_WHOLE, STAT_WHOLE],
        [HALF_F32, STATES, STAT, STAT],
        (core, q, g, gain, col, inside[True], scanned, got, got), 2 * MM,
    )

    def turn(i):
        return jnp.where(i < HALF, i, 2 * HALF - 1 - i)

    def first(i):
        return jnp.minimum(i, HALF - 1)

    def second(i):
        return jnp.minimum(2 * HALF - 1 - i, HALF - 1)

    delta_other, moment_sent, gain_other, inverse, mean = call(
        attend_other_kernel, "attend_other", (2 * HALF,),
        [wide(False, turn), wide(False, turn), gain_block(False, turn), COL_WHOLE, narrow(first),
         state_block(HD, first), STAT_WHOLE, STAT_WHOLE],
        [narrow(second), state_block(HD, second), pl.BlockSpec((1, GW), lambda i, c: (0, second(i))),
         STAT_WHOLE, STAT_WHOLE],
        [HALF_BF16, STATES, GAIN_ROW, STAT, STAT],
        (core, q, g, gain, col, inside[False], state_other, squares, products), 3 * MM,
        scratch=[pltpu.VMEM((HALF, T, GW), F32), pltpu.VMEM((T, HD), F32), pltpu.VMEM((T, HD), F32)],
    )
    moment_got = swap_cores(moment_sent)
    delta_own, moment_own, gain_own = call(
        delta_own_kernel, "delta_own", (HALF,),
        [wide(True), wide(True), gain_block(True), COL_WHOLE, narrow(), STAT_WHOLE, STAT_WHOLE],
        [narrow(), state_block(), pl.BlockSpec((1, GW), lambda i, c: (0, i))],
        [HALF_BF16, STATES, GAIN_ROW],
        (core, q, g, gain, col, att_own, inverse, mean), MM,
    )
    (chip_moment,) = call(
        functools.partial(combine_kernel, False), "chip_moment", (HALF,),
        [state_block(), state_block(), LOG_BLOCK, LOG_BLOCK], [state_block()], [STATES],
        (core, moment_own, moment_got, own, got), 0,
    )
    gathered_back = chips_all_to_all(chip_moment)

    gain_halves = jnp.where(
        core[0] == 0,
        jnp.concatenate([gain_own, gain_other], 1),
        jnp.concatenate([gain_other, gain_own], 1),
    )
    members = lax.axis_size(ALL)
    gain_parts = lax.all_to_all(
        gain_halves.reshape(members, -1), ALL, split_axis=0, concat_axis=0, tiled=True
    )
    gain_grad = jnp.sum(gain_parts, axis=0) * (1.0 / math.sqrt(T * members))

    delta = {True: delta_own, False: delta_other}
    state = {True: state_own, False: state_other}
    query_grad, key_inside, value_inside = (), {}, {}
    for mine in (True, False):
        *query_grad, key_inside[mine], value_inside[mine] = call(
            functools.partial(backward_kernel, mine), "backward_inside", (HALF,),
            [narrow(), wide(mine), wide(mine), wide(mine),
             pl.BlockSpec((GH, T, T), lambda i, c: (i, 0, 0)), COL_WHOLE, row_block(mine), state_block()]
            + [ANY] * len(query_grad),
            [wide(mine), narrow(), narrow()],
            [WHOLE_BF16, HALF_F32, HALF_F32],
            (core, delta[mine], q, k, v, weights[mine], col, row, state[mine], *query_grad),
            4 * SM + 2 * MM,
            aliases={9: 0} if query_grad else None,
        )

    scanned_back = chips_all_to_all(scan_over_chips(False, gathered_back, gathered))
    (onward_back,) = call(
        functools.partial(send_kernel, False), "onward_back", (HALF,),
        [state_block(), state_block(), LOG_BLOCK], [state_block()], [STATES],
        (core, scanned_back, moment_own, own), 0,
    )
    later_other = swap_cores(onward_back)
    key_grad, value_grad = call(
        finish_own_kernel, "finish_own", (HALF,),
        [wide(True), wide(True), COL_WHOLE, narrow(), narrow(), state_block(), state_block(), LOG_BLOCK],
        [wide(True), wide(True)], [WHOLE_BF16, WHOLE_BF16],
        (core, k, v, col, key_inside[True], value_inside[True], scanned_back, moment_got, got), 4 * MM,
    )
    key_grad, value_grad = call(
        finish_other_kernel, "finish_other", (HALF,),
        [wide(False), wide(False), COL_WHOLE, narrow(), narrow(), state_block(), ANY, ANY],
        [wide(False), wide(False)], [WHOLE_BF16, WHOLE_BF16],
        (core, k, v, col, key_inside[False], value_inside[False], later_other, key_grad, value_grad),
        4 * MM, aliases={7: 0, 8: 1},
    )
    return query_grad[0], key_grad, value_grad, gain_grad


def solution(mesh):
    fine = Mesh(mesh.devices.reshape(4, 2, 4, 4, 2), ALL)
    rows = P("dp", ("zh", "x", "y", "core"), None)
    return jax.shard_map(
        per_device,
        mesh=fine,
        in_specs=(rows,) * 5 + (P(),),
        out_specs=(rows, rows, rows, P(ALL)),
        check_vma=False,
    )
```

```python
import functools
import math

import jax
import jax.numpy as jnp
from jax import lax
from jax.experimental import pallas as pl
from jax.experimental.pallas import tpu as pltpu
from jax.sharding import Mesh, PartitionSpec as P

EPSILON = 1e-06
HIGHEST = lax.Precision.HIGHEST
F32 = jnp.float32
BF16 = jnp.bfloat16
T = 192
HD = 128
GH = 8
GW = GH * HD
NG = 4
HALF = NG // 2
NC = 16
ALL = ("dp", "zh", "x", "y", "core")


def dot(a, b, ca, cb):
    return lax.dot_general(a, b, (((ca,), (cb,)), ((), ())), preferred_element_type=F32)


def lanes(j):
    return slice(j * HD, (j + 1) * HD)


def split_state(state, axis):
    high = state.astype(BF16)
    low = (state - high.astype(F32)).astype(BF16)
    return jnp.concatenate([high, low], axis)


def rows_by_state(rows, state):
    return dot(jnp.concatenate([rows, rows], 1), split_state(state, 0), 1, 0)


def rows_by_state_t(rows, state):
    return dot(jnp.concatenate([rows, rows], 1), split_state(state, 1), 1, 1)


def decay_table(col, row):
    row_ids = lax.broadcasted_iota(jnp.int32, (T, T), 0)
    col_ids = lax.broadcasted_iota(jnp.int32, (T, T), 1)
    return jnp.exp(jnp.where(row_ids >= col_ids, col - row, -jnp.inf))


def states_of(k_ref, v_ref, cum, s_ref):
    last = cum[T - 1 : T, :]
    shrink = jnp.exp(last - cum)
    for j in range(GH):
        late = (k_ref[:, lanes(j)].astype(F32) * shrink[:, j : j + 1]).astype(BF16)
        s_ref[j, :HD, :] = dot(late, v_ref[:, lanes(j)], 0, 0)
        s_ref[j, HD:, :] = jnp.broadcast_to(last[:, j : j + 1], (8, HD))


def state_first_kernel(c_ref, k_ref, v_ref, ld_ref, s_ref, col_ref, row_ref):
    i = pl.program_id(0)

    @pl.when(i == 0)
    def _():
        upper = (
            lax.broadcasted_iota(jnp.int32, (T, T), 0) <= lax.broadcasted_iota(jnp.int32, (T, T), 1)
        ).astype(F32)
        logs = ld_ref[...]
        row_ref[...] = lax.dot_general(
            logs, upper, (((1,), (0,)), ((), ())), precision=HIGHEST, preferred_element_type=F32
        )
        col = lax.dot_general(
            upper, logs, (((0,), (1,)), ((), ())), precision=HIGHEST, preferred_element_type=F32
        )
        for g in range(NG):
            col_ref[g] = col[:, g * GH : (g + 1) * GH]

    states_of(k_ref, v_ref, col_ref[(1 - c_ref[0]) * HALF + i], s_ref)


def state_second_kernel(c_ref, k_ref, v_ref, col_ref, s_ref):
    states_of(k_ref, v_ref, col_ref[c_ref[0] * HALF + pl.program_id(0)], s_ref)


def combine_kernel(upward, c_ref, own_ref, got_ref, lo_ref, lg_ref, p_ref):
    first = c_ref[0] == 0 if upward else c_ref[0] == 1
    for j in range(GH):
        log_own, log_got = lo_ref[j, 0:1, :], lg_ref[j, 0:1, :]
        scale_own = jnp.where(first, jnp.exp(log_got), 1.0)
        scale_got = jnp.where(first, 1.0, jnp.exp(log_own))
        p_ref[j, :HD, :] = scale_own * own_ref[j] + scale_got * got_ref[j]
        if upward:
            p_ref[j, HD:, :] = jnp.broadcast_to(log_own + log_got, (8, HD))


def total_kernel(upward, m_ref, l_ref, t_ref):
    run = jnp.zeros((HD, HD), F32)
    for i in range(NC) if upward else reversed(range(NC)):
        run = jnp.exp(l_ref[i, 0:1, :]) * run + m_ref[i]
    t_ref[...] = run


def scan_kernel(upward, m_ref, l_ref, t_ref, o_ref):
    run = t_ref[...]
    for i in range(NC) if upward else reversed(range(NC)):
        o_ref[i] = run
        run = jnp.exp(l_ref[i, 0:1, :]) * run + m_ref[i]


def send_kernel(upward, c_ref, d_ref, own_ref, lo_ref, o_ref):
    step_on = c_ref[0] == 0 if upward else c_ref[0] == 1
    for j in range(GH):
        scale = jnp.where(step_on, jnp.exp(lo_ref[j, 0:1, :]), 1.0)
        keep = jnp.where(step_on, 1.0, 0.0)
        o_ref[j] = scale * d_ref[j] + keep * own_ref[j]


def own_state(upward, c_ref, d_ref, got_ref, lg_ref, j):
    at_edge = c_ref[0] == 0 if upward else c_ref[0] == 1
    scale = jnp.where(at_edge, 1.0, jnp.exp(lg_ref[j, 0:1, :]))
    keep = jnp.where(at_edge, 0.0, 1.0)
    return scale * d_ref[j] + keep * got_ref[j]


def forward_kernel(own, c_ref, q_ref, k_ref, v_ref, col_ref, row_ref, fw_ref, in_ref):
    half = c_ref[0] if own else 1 - c_ref[0]
    cum = col_ref[half * HALF + pl.program_id(0)]
    for j in range(GH):
        decay = decay_table(cum[:, j : j + 1], row_ref[j : j + 1, :])
        scores = dot(q_ref[:, lanes(j)], k_ref[:, lanes(j)], 1, 1)
        weights = (scores * decay).astype(BF16)
        fw_ref[j] = weights
        in_ref[:, lanes(j)] = dot(weights, v_ref[:, lanes(j)], 1, 0)


def attend_group(q_ref, g_ref, gain_ref, cum, in_ref, state_at, att_ref, sq_ref, pr_ref):
    growth = jnp.exp(cum)
    squares = jnp.zeros((T, HD), F32)
    products = jnp.zeros((T, HD), F32)
    for j in range(GH):
        att = in_ref[:, lanes(j)] + growth[:, j : j + 1] * rows_by_state(q_ref[:, lanes(j)], state_at(j))
        att_ref[:, lanes(j)] = att
        squares += att * att
        products += att * (gain_ref[:, lanes(j)] * g_ref[:, lanes(j)].astype(F32))
    sq_ref[...] += squares
    pr_ref[...] += products


def attend_own_kernel(
    c_ref, q_ref, g_ref, gain_ref, col_ref, in_ref, d_ref, got_ref, lg_ref,
    att_ref, i_ref, sq_ref, pr_ref,
):
    @pl.when(pl.program_id(0) == 0)
    def _():
        sq_ref[...] = jnp.zeros_like(sq_ref)
        pr_ref[...] = jnp.zeros_like(pr_ref)

    def state_at(j):
        state = own_state(True, c_ref, d_ref, got_ref, lg_ref, j)
        i_ref[j] = state
        return state

    cum = col_ref[c_ref[0] * HALF + pl.program_id(0)]
    attend_group(q_ref, g_ref, gain_ref, cum, in_ref, state_at, att_ref, sq_ref, pr_ref)


def delta_group(q_ref, g_ref, gain_ref, cum, att_ref, inverse, mean, od_ref, m_ref, gt_ref):
    growth = jnp.exp(cum)
    for j in range(GH):
        grad = g_ref[:, lanes(j)].astype(F32)
        normed = att_ref[:, lanes(j)] * inverse
        delta = (inverse * (gain_ref[:, lanes(j)] * grad - normed * mean)).astype(BF16)
        od_ref[:, lanes(j)] = delta
        gt_ref[:, lanes(j)] = jnp.sum(grad * normed, axis=0, keepdims=True)
        early = (q_ref[:, lanes(j)].astype(F32) * growth[:, j : j + 1]).astype(BF16)
        m_ref[j] = dot(early, delta, 0, 0)


def attend_other_kernel(
    c_ref, q_ref, g_ref, gain_ref, col_ref, in_ref, i_ref, sq_in, pr_in,
    od_ref, m_ref, gt_ref, inv_ref, mean_ref, att_ref, sq_ref, pr_ref,
):
    step = pl.program_id(0)
    group = jnp.where(step < HALF, step, 2 * HALF - 1 - step)
    cum = col_ref[(1 - c_ref[0]) * HALF + group]

    @pl.when(step == 0)
    def _():
        sq_ref[...] = sq_in[...]
        pr_ref[...] = pr_in[...]

    @pl.when(step < HALF)
    def _():
        attend_group(
            q_ref, g_ref, gain_ref, cum, in_ref, lambda j: i_ref[j], att_ref.at[group], sq_ref, pr_ref
        )

    @pl.when(step == HALF)
    def _():
        features = NG * GW
        inverse = lax.rsqrt(jnp.sum(sq_ref[...], axis=1, keepdims=True) * (1.0 / features) + EPSILON)
        mean = inverse * (jnp.sum(pr_ref[...], axis=1, keepdims=True) * (1.0 / features))
        inv_ref[...] = jnp.broadcast_to(inverse, (T, HD))
        mean_ref[...] = jnp.broadcast_to(mean, (T, HD))

    @pl.when(step >= HALF)
    def _():
        delta_group(
            q_ref, g_ref, gain_ref, cum, att_ref.at[group], inv_ref[...], mean_ref[...],
            od_ref, m_ref, gt_ref,
        )


def delta_own_kernel(
    c_ref, q_ref, g_ref, gain_ref, col_ref, att_ref, inv_ref, mean_ref, od_ref, m_ref, gt_ref
):
    cum = col_ref[c_ref[0] * HALF + pl.program_id(0)]
    delta_group(
        q_ref, g_ref, gain_ref, cum, att_ref, inv_ref[...], mean_ref[...], od_ref, m_ref, gt_ref
    )


def backward_kernel(
    own, c_ref, od_ref, q_ref, k_ref, v_ref, fw_ref, col_ref, row_ref, i_ref, *rest
):
    qg_ref, ki_ref, vi_ref = rest[-3:]
    half = c_ref[0] if own else 1 - c_ref[0]
    cum = col_ref[half * HALF + pl.program_id(0)]
    growth = jnp.exp(cum)
    for j in range(GH):
        at = lanes(j)
        decay = decay_table(cum[:, j : j + 1], row_ref[j : j + 1, :])
        delta = od_ref[:, at]
        weights = (dot(delta, v_ref[:, at], 1, 1) * decay).astype(BF16)
        inter = growth[:, j : j + 1] * rows_by_state_t(delta, i_ref[j])
        qg_ref[:, at] = (dot(weights, k_ref[:, at], 1, 0) + inter).astype(BF16)
        ki_ref[:, at] = dot(weights, q_ref[:, at], 0, 0)
        vi_ref[:, at] = dot(fw_ref[j], delta, 0, 0)


def finish_group(k_ref, v_ref, cum, ki_ref, vi_ref, state_at, kg_ref, vg_ref):
    shrink = jnp.exp(cum[T - 1 : T, :] - cum)
    for j in range(GH):
        at = lanes(j)
        state = state_at(j)
        scale = shrink[:, j : j + 1]
        kg_ref[:, at] = (ki_ref[:, at] + scale * rows_by_state_t(v_ref[:, at], state)).astype(BF16)
        vg_ref[:, at] = (vi_ref[:, at] + scale * rows_by_state(k_ref[:, at], state)).astype(BF16)


def finish_own_kernel(
    c_ref, k_ref, v_ref, col_ref, ki_ref, vi_ref, d_ref, got_ref, lg_ref, kg_ref, vg_ref
):
    cum = col_ref[c_ref[0] * HALF + pl.program_id(0)]
    finish_group(
        k_ref, v_ref, cum, ki_ref, vi_ref,
        lambda j: own_state(False, c_ref, d_ref, got_ref, lg_ref, j), kg_ref, vg_ref,
    )


def finish_other_kernel(
    c_ref, k_ref, v_ref, col_ref, ki_ref, vi_ref, x_ref, kg_in, vg_in, kg_ref, vg_ref
):
    cum = col_ref[(1 - c_ref[0]) * HALF + pl.program_id(0)]
    finish_group(k_ref, v_ref, cum, ki_ref, vi_ref, lambda j: x_ref[j], kg_ref, vg_ref)


class Free:
    def __init__(self, array):
        self.array = array


def in_hbm(a):
    return pltpu.with_memory_space_constraint(a, pltpu.HBM)


def call(kernel, name, grid, in_specs, out_specs, out_shape, args, flops, scratch=(), aliases=None):
    nbytes = sum(math.prod(s.shape) * s.dtype.itemsize for s in out_shape)
    nbytes += sum(math.prod(a.shape) * a.dtype.itemsize for a in args[1:] if not isinstance(a, Free))
    args = [args[0]] + [a.array if isinstance(a, Free) else in_hbm(a) for a in args[1:]]
    out_shape = [pltpu.HBM(s.shape, s.dtype) for s in out_shape]
    return pl.pallas_call(
        kernel,
        name=name,
        grid_spec=pltpu.PrefetchScalarGridSpec(
            num_scalar_prefetch=1,
            grid=grid,
            in_specs=in_specs,
            out_specs=out_specs,
            scratch_shapes=scratch,
        ),
        out_shape=out_shape,
        input_output_aliases=aliases or {},
        compiler_params=pltpu.CompilerParams(vmem_limit_bytes=16 << 20),
        cost_estimate=pl.CostEstimate(flops=flops, bytes_accessed=nbytes, transcendentals=0),
    )(*args)


def shape(dims, dtype=F32):
    return jax.ShapeDtypeStruct(dims, dtype)


def half_of(own, c_ref):
    return c_ref[0] if own else 1 - c_ref[0]


def wide(own, group=lambda i: i):
    return pl.BlockSpec((None, T, GW), lambda i, c: (0, 0, half_of(own, c) * HALF + group(i)))


def narrow(group=lambda i: i):
    return pl.BlockSpec((T, GW), lambda i, c: (0, group(i)))


def gain_block(own, group=lambda i: i):
    return pl.BlockSpec((1, GW), lambda i, c: (0, half_of(own, c) * HALF + group(i)))


def row_block(own):
    return pl.BlockSpec((GH, T), lambda i, c: (half_of(own, c) * HALF + i, 0))


def state_block(rows=HD, group=lambda i: i):
    return pl.BlockSpec((GH, rows, HD), lambda i, c: (group(i), 0, 0))


LOG_BLOCK = pl.BlockSpec((GH, 8, HD), lambda i, c: (i, HD // 8, 0))
COL_WHOLE = pl.BlockSpec((NG, T, GH), lambda i, c: (0, 0, 0))
STAT_WHOLE = pl.BlockSpec((T, HD), lambda i, c: (0, 0))
ANY = pl.BlockSpec(memory_space=pl.ANY)
STATES = shape((NC, HD, HD))
LOGGED = shape((NC, HD + 8, HD))
HALF_F32 = shape((T, HALF * GW))
HALF_BF16 = shape((T, HALF * GW), BF16)
WHOLE_BF16 = shape((1, T, NG * GW), BF16)
STAT = shape((T, HD))
GAIN_ROW = shape((1, HALF * GW))
MM = 2 * T * HD * HD * NC
SM = 2 * T * T * HD * NC


def swap_cores(values):
    return lax.ppermute(values, "core", [(0, 1), (1, 0)])


def chips_all_to_all(values):
    return lax.all_to_all(values, ("x", "y"), split_axis=0, concat_axis=0, tiled=True)


def scan_over_chips(upward, got, logs):
    whole_m = pl.BlockSpec((NC, HD, HD), lambda i: (0, 0, 0))
    whole_l = pl.BlockSpec((NC, 8, HD), lambda i: (0, HD // 8, 0))
    whole_t = pl.BlockSpec((HD, HD), lambda i: (0, 0))
    params = pltpu.CompilerParams(vmem_limit_bytes=16 << 20)
    total = pl.pallas_call(
        functools.partial(total_kernel, upward),
        name="half_total",
        grid=(1,),
        in_specs=[whole_m, whole_l],
        out_specs=whole_t,
        out_shape=shape((HD, HD)),
        compiler_params=params,
    )(got, logs)
    before = lax.ppermute(total, "zh", [(0, 1)] if upward else [(1, 0)])
    return pl.pallas_call(
        functools.partial(scan_kernel, upward),
        name="chip_scan",
        grid=(1,),
        in_specs=[whole_m, whole_l, whole_t],
        out_specs=whole_m,
        out_shape=pltpu.HBM(STATES.shape, F32),
        compiler_params=params,
    )(got, logs, before)


def per_device(queries, key_rows, value_rows, out_grad, log_decay, norm_gain):
    core = lax.axis_index("core").astype(jnp.int32).reshape(1)
    q, k, v, g = queries, key_rows, value_rows, out_grad
    gain = norm_gain.reshape(1, NG * GW)
    logs = jnp.transpose(log_decay[0])

    sent, col, row = call(
        state_first_kernel, "states_other", (HALF,),
        [wide(False), wide(False), pl.BlockSpec((NG * GH, T), lambda i, c: (0, 0))],
        [state_block(HD + 8), COL_WHOLE, pl.BlockSpec((NG * GH, T), lambda i, c: (0, 0))],
        [LOGGED, shape((NG, T, GH)), shape((NG * GH, T))],
        (core, k, v, logs), MM,
    )
    got = swap_cores(sent)
    (own,) = call(
        state_second_kernel, "states_own", (HALF,),
        [wide(True), wide(True), COL_WHOLE], [state_block(HD + 8)], [LOGGED],
        (core, k, v, col), MM,
    )
    (chip_total,) = call(
        functools.partial(combine_kernel, True), "chip_total", (HALF,),
        [state_block(), state_block(), LOG_BLOCK, LOG_BLOCK], [state_block(HD + 8)], [LOGGED],
        (core, own, Free(got), own, Free(got)), 0,
    )
    gathered = chips_all_to_all(chip_total)

    weights, inside = {}, {}
    for mine in (True, False):
        weights[mine], inside[mine] = call(
            functools.partial(forward_kernel, mine), "forward_inside", (HALF,),
            [wide(mine), wide(mine), wide(mine), COL_WHOLE, row_block(mine)],
            [pl.BlockSpec((GH, T, T), lambda i, c: (i, 0, 0)), narrow()],
            [shape((NC, T, T), BF16), HALF_F32],
            (core, q, k, v, col, row), 2 * SM,
        )

    gathered, inside[True], inside[False] = lax.optimization_barrier(
        (gathered, inside[True], inside[False])
    )
    scanned = chips_all_to_all(scan_over_chips(True, gathered, gathered))
    (onward,) = call(
        functools.partial(send_kernel, True), "onward", (HALF,),
        [state_block(), state_block(), LOG_BLOCK], [state_block()], [STATES],
        (core, Free(scanned), own, own), 0,
    )
    state_other = swap_cores(onward)
    att_own, state_own, squares, products = call(
        attend_own_kernel, "attend_own", (HALF,),
        [wide(True), wide(True), gain_block(True), COL_WHOLE, narrow(), state_block(), state_block(),
         LOG_BLOCK],
        [narrow(), state_block(), STAT_WHOLE, STAT_WHOLE],
        [HALF_F32, STATES, STAT, STAT],
        (core, q, g, gain, col, inside[True], Free(scanned), Free(got), Free(got)), 2 * MM,
    )

    def turn(i):
        return jnp.where(i < HALF, i, 2 * HALF - 1 - i)

    def first(i):
        return jnp.minimum(i, HALF - 1)

    def second(i):
        return jnp.minimum(2 * HALF - 1 - i, HALF - 1)

    delta_other, moment_sent, gain_other, inverse, mean = call(
        attend_other_kernel, "attend_other", (2 * HALF,),
        [wide(False, turn), wide(False, turn), gain_block(False, turn), COL_WHOLE, narrow(first),
         state_block(HD, first), STAT_WHOLE, STAT_WHOLE],
        [narrow(second), state_block(HD, second), pl.BlockSpec((1, GW), lambda i, c: (0, second(i))),
         STAT_WHOLE, STAT_WHOLE],
        [HALF_BF16, STATES, GAIN_ROW, STAT, STAT],
        (core, q, g, gain, col, inside[False], Free(state_other), squares, products), 3 * MM,
        scratch=[pltpu.VMEM((HALF, T, GW), F32), pltpu.VMEM((T, HD), F32), pltpu.VMEM((T, HD), F32)],
    )
    moment_got = swap_cores(moment_sent)
    delta_own, moment_own, gain_own = call(
        delta_own_kernel, "delta_own", (HALF,),
        [wide(True), wide(True), gain_block(True), COL_WHOLE, narrow(), STAT_WHOLE, STAT_WHOLE],
        [narrow(), state_block(), pl.BlockSpec((1, GW), lambda i, c: (0, i))],
        [HALF_BF16, STATES, GAIN_ROW],
        (core, q, g, gain, col, att_own, inverse, mean), MM,
    )
    (chip_moment,) = call(
        functools.partial(combine_kernel, False), "chip_moment", (HALF,),
        [state_block(), state_block(), LOG_BLOCK, LOG_BLOCK], [state_block()], [STATES],
        (core, moment_own, Free(moment_got), own, Free(got)), 0,
    )
    gathered_back = chips_all_to_all(chip_moment)

    gain_halves = jnp.where(
        core[0] == 0,
        jnp.concatenate([gain_own, gain_other], 1),
        jnp.concatenate([gain_other, gain_own], 1),
    )
    members = lax.axis_size(ALL)
    gain_parts = lax.all_to_all(
        gain_halves.reshape(members, -1), ALL, split_axis=0, concat_axis=0, tiled=True
    )
    gain_grad = jnp.sum(gain_parts, axis=0) * (1.0 / math.sqrt(T * members))

    delta = {True: delta_own, False: delta_other}
    state = {True: state_own, False: Free(state_other)}
    query_grad, key_inside, value_inside = (), {}, {}
    for mine in (True, False):
        *query_grad, key_inside[mine], value_inside[mine] = call(
            functools.partial(backward_kernel, mine), "backward_inside", (HALF,),
            [narrow(), wide(mine), wide(mine), wide(mine),
             pl.BlockSpec((GH, T, T), lambda i, c: (i, 0, 0)), COL_WHOLE, row_block(mine), state_block()]
            + [ANY] * len(query_grad),
            [wide(mine), narrow(), narrow()],
            [WHOLE_BF16, HALF_F32, HALF_F32],
            (core, delta[mine], q, k, v, weights[mine], col, row, state[mine], *query_grad),
            4 * SM + 2 * MM,
            aliases={9: 0} if query_grad else None,
        )

    gathered_back, key_inside[True] = lax.optimization_barrier((gathered_back, key_inside[True]))
    scanned_back = chips_all_to_all(scan_over_chips(False, gathered_back, gathered))
    scanned_back, key_inside[False], gain_grad = lax.optimization_barrier(
        (scanned_back, key_inside[False], gain_grad)
    )
    (onward_back,) = call(
        functools.partial(send_kernel, False), "onward_back", (HALF,),
        [state_block(), state_block(), LOG_BLOCK], [state_block()], [STATES],
        (core, Free(scanned_back), moment_own, own), 0,
    )
    later_other = swap_cores(onward_back)
    key_grad, value_grad = call(
        finish_own_kernel, "finish_own", (HALF,),
        [wide(True), wide(True), COL_WHOLE, narrow(), narrow(), state_block(), state_block(), LOG_BLOCK],
        [wide(True), wide(True)], [WHOLE_BF16, WHOLE_BF16],
        (core, k, v, col, key_inside[True], value_inside[True], Free(scanned_back), Free(moment_got), Free(got)), 4 * MM,
    )
    key_grad, value_grad = call(
        finish_other_kernel, "finish_other", (HALF,),
        [wide(False), wide(False), COL_WHOLE, narrow(), narrow(), state_block(), ANY, ANY],
        [wide(False), wide(False)], [WHOLE_BF16, WHOLE_BF16],
        (core, k, v, col, key_inside[False], value_inside[False], Free(later_other), key_grad, value_grad),
        4 * MM, aliases={7: 0, 8: 1},
    )
    return query_grad[0], key_grad, value_grad, gain_grad


def solution(mesh):
    fine = Mesh(mesh.devices.reshape(4, 2, 4, 4, 2), ALL)
    rows = P("dp", ("zh", "x", "y", "core"), None)
    return jax.shard_map(
        per_device,
        mesh=fine,
        in_specs=(rows,) * 5 + (P(),),
        out_specs=(rows, rows, rows, P(ALL)),
        check_vma=False,
    )
```

```python
import functools
import math

import jax
import jax.numpy as jnp
from jax import lax
from jax.experimental import pallas as pl
from jax.experimental.pallas import tpu as pltpu
from jax.sharding import Mesh, PartitionSpec as P

EPSILON = 1e-06
HIGHEST = lax.Precision.HIGHEST
F32 = jnp.float32
BF16 = jnp.bfloat16
T = 192
HD = 128
GH = 8
GW = GH * HD
NG = 4
HALF = NG // 2
NC = 16
ALL = ("dp", "zh", "x", "y", "core")


def dot(a, b, ca, cb):
    return lax.dot_general(a, b, (((ca,), (cb,)), ((), ())), preferred_element_type=F32)


def lanes(j):
    return slice(j * HD, (j + 1) * HD)


def split_state(state, axis):
    high = state.astype(BF16)
    low = (state - high.astype(F32)).astype(BF16)
    return jnp.concatenate([high, low], axis)


def rows_by_state(rows, state):
    return dot(jnp.concatenate([rows, rows], 1), split_state(state, 0), 1, 0)


def rows_by_state_t(rows, state):
    return dot(jnp.concatenate([rows, rows], 1), split_state(state, 1), 1, 1)


def decay_table(col, row):
    row_ids = lax.broadcasted_iota(jnp.int32, (T, T), 0)
    col_ids = lax.broadcasted_iota(jnp.int32, (T, T), 1)
    return jnp.exp(jnp.where(row_ids >= col_ids, col - row, -jnp.inf))


def states_of(k_ref, v_ref, cum, s_ref):
    last = cum[T - 1 : T, :]
    shrink = jnp.exp(last - cum)
    for j in range(GH):
        late = (k_ref[:, lanes(j)].astype(F32) * shrink[:, j : j + 1]).astype(BF16)
        s_ref[j, :HD, :] = dot(late, v_ref[:, lanes(j)], 0, 0)
        s_ref[j, HD:, :] = jnp.broadcast_to(last[:, j : j + 1], (8, HD))


def state_first_kernel(c_ref, k_ref, v_ref, ld_ref, s_ref, col_ref, row_ref):
    i = pl.program_id(0)

    @pl.when(i == 0)
    def _():
        upper = (
            lax.broadcasted_iota(jnp.int32, (T, T), 0) <= lax.broadcasted_iota(jnp.int32, (T, T), 1)
        ).astype(F32)
        logs = ld_ref[...]
        row_ref[...] = lax.dot_general(
            logs, upper, (((1,), (0,)), ((), ())), precision=HIGHEST, preferred_element_type=F32
        )
        col = lax.dot_general(
            upper, logs, (((0,), (1,)), ((), ())), precision=HIGHEST, preferred_element_type=F32
        )
        for g in range(NG):
            col_ref[g] = col[:, g * GH : (g + 1) * GH]

    states_of(k_ref, v_ref, col_ref[(1 - c_ref[0]) * HALF + i], s_ref)


def state_second_kernel(c_ref, k_ref, v_ref, col_ref, s_ref):
    states_of(k_ref, v_ref, col_ref[c_ref[0] * HALF + pl.program_id(0)], s_ref)


def combine_kernel(upward, c_ref, own_ref, got_ref, lo_ref, lg_ref, p_ref, kept_ref=None):
    first = c_ref[0] == 0 if upward else c_ref[0] == 1
    for j in range(GH):
        log_own, log_got = lo_ref[j, 0:1, :], lg_ref[j, 0:1, :]
        scale_own = jnp.where(first, jnp.exp(log_got), 1.0)
        scale_got = jnp.where(first, 1.0, jnp.exp(log_own))
        p_ref[j, :HD, :] = scale_own * own_ref[j] + scale_got * got_ref[j]
        if upward:
            p_ref[j, HD:, :] = jnp.broadcast_to(log_own + log_got, (8, HD))
        else:
            kept_ref[j] = got_ref[j]


def total_kernel(upward, c_ref, m_ref, l_ref, *rest):
    run = jnp.zeros((HD, HD), F32)
    for i in range(NC) if upward else reversed(range(NC)):
        run = jnp.exp(l_ref[i, 0:1, :]) * run + m_ref[i]
    t_ref = rest[-1]
    t_ref[:HD, :] = run
    if not upward:
        t_ref[HD:, :] = rest[0][...]


def scan_kernel(upward, c_ref, m_ref, l_ref, t_ref, *rest):
    o_ref = rest[-1]
    run = t_ref[:HD, :]
    if not upward:
        run = jnp.where(c_ref[2] == 0, run, 0.0)
        both = rest[0][...] + t_ref[HD:, :]
    for i in range(NC) if upward else reversed(range(NC)):
        o_ref[i, :HD, :] = run
        run = jnp.exp(l_ref[i, 0:1, :]) * run + m_ref[i]
        if not upward:
            x = i // 4
            row = jnp.where(c_ref[2] == 0, both[x : x + 1, :], both[4 + x : 5 + x, :])
            o_ref[i, HD:, :] = jnp.broadcast_to(row, (8, HD))


def send_kernel(upward, c_ref, d_ref, own_ref, lo_ref, *rest):
    if upward:
        (o_ref,) = rest
    else:
        gains_ref, o_ref, sum_ref = rest
        part = gains_ref[0]
        for j in range(1, GH):
            part += gains_ref[j]

        @pl.when(pl.program_id(0) == 0)
        def _():
            sum_ref[...] = part

        @pl.when(pl.program_id(0) > 0)
        def _():
            sum_ref[...] += part

    step_on = c_ref[0] == 0 if upward else c_ref[0] == 1
    for j in range(GH):
        scale = jnp.where(step_on, jnp.exp(lo_ref[j, 0:1, :]), 1.0)
        keep = jnp.where(step_on, 1.0, 0.0)
        o_ref[j] = scale * d_ref[j] + keep * own_ref[j]


def own_state(upward, c_ref, d_ref, got_ref, lg_ref, j):
    at_edge = c_ref[0] == 0 if upward else c_ref[0] == 1
    scale = jnp.where(at_edge, 1.0, jnp.exp(lg_ref[j, 0:1, :]))
    keep = jnp.where(at_edge, 0.0, 1.0)
    return scale * d_ref[j] + keep * got_ref[j]


def forward_kernel(own, c_ref, q_ref, k_ref, v_ref, col_ref, row_ref, fw_ref, in_ref):
    half = c_ref[0] if own else 1 - c_ref[0]
    cum = col_ref[half * HALF + pl.program_id(0)]
    for j in range(GH):
        decay = decay_table(cum[:, j : j + 1], row_ref[j : j + 1, :])
        scores = dot(q_ref[:, lanes(j)], k_ref[:, lanes(j)], 1, 1)
        weights = (scores * decay).astype(BF16)
        fw_ref[j] = weights
        in_ref[:, lanes(j)] = dot(weights, v_ref[:, lanes(j)], 1, 0)


def attend_group(q_ref, g_ref, gain_ref, cum, in_ref, state_at, att_ref, sq_ref, pr_ref):
    growth = jnp.exp(cum)
    squares = jnp.zeros((T, HD), F32)
    products = jnp.zeros((T, HD), F32)
    for j in range(GH):
        att = in_ref[:, lanes(j)] + growth[:, j : j + 1] * rows_by_state(q_ref[:, lanes(j)], state_at(j))
        att_ref[:, lanes(j)] = att
        squares += att * att
        products += att * (gain_ref[:, lanes(j)] * g_ref[:, lanes(j)].astype(F32))
    sq_ref[...] += squares
    pr_ref[...] += products


def attend_own_kernel(
    c_ref, q_ref, g_ref, gain_ref, col_ref, in_ref, d_ref, got_ref, lg_ref,
    att_ref, i_ref, sq_ref, pr_ref,
):
    @pl.when(pl.program_id(0) == 0)
    def _():
        sq_ref[...] = jnp.zeros_like(sq_ref)
        pr_ref[...] = jnp.zeros_like(pr_ref)

    def state_at(j):
        state = own_state(True, c_ref, d_ref, got_ref, lg_ref, j)
        i_ref[j] = state
        return state

    cum = col_ref[c_ref[0] * HALF + pl.program_id(0)]
    attend_group(q_ref, g_ref, gain_ref, cum, in_ref, state_at, att_ref, sq_ref, pr_ref)


def delta_group(q_ref, g_ref, gain_ref, cum, att_ref, inverse, mean, od_ref, m_ref, gt_ref):
    growth = jnp.exp(cum)
    for j in range(GH):
        grad = g_ref[:, lanes(j)].astype(F32)
        normed = att_ref[:, lanes(j)] * inverse
        delta = (inverse * (gain_ref[:, lanes(j)] * grad - normed * mean)).astype(BF16)
        od_ref[:, lanes(j)] = delta
        gt_ref[j : j + 1, :] = jnp.sum(grad * normed, axis=0, keepdims=True)
        early = (q_ref[:, lanes(j)].astype(F32) * growth[:, j : j + 1]).astype(BF16)
        m_ref[j] = dot(early, delta, 0, 0)


def attend_other_kernel(
    c_ref, q_ref, g_ref, gain_ref, col_ref, in_ref, i_ref, sq_in, pr_in,
    od_ref, m_ref, gt_ref, inv_ref, mean_ref, att_ref, sq_ref, pr_ref,
):
    step = pl.program_id(0)
    group = jnp.where(step < HALF, step, 2 * HALF - 1 - step)
    cum = col_ref[(1 - c_ref[0]) * HALF + group]

    @pl.when(step == 0)
    def _():
        sq_ref[...] = sq_in[...]
        pr_ref[...] = pr_in[...]

    @pl.when(step < HALF)
    def _():
        attend_group(
            q_ref, g_ref, gain_ref, cum, in_ref, lambda j: i_ref[j], att_ref.at[group], sq_ref, pr_ref
        )

    @pl.when(step == HALF)
    def _():
        features = NG * GW
        inverse = lax.rsqrt(jnp.sum(sq_ref[...], axis=1, keepdims=True) * (1.0 / features) + EPSILON)
        mean = inverse * (jnp.sum(pr_ref[...], axis=1, keepdims=True) * (1.0 / features))
        inv_ref[...] = jnp.broadcast_to(inverse, (T, HD))
        mean_ref[...] = jnp.broadcast_to(mean, (T, HD))

    @pl.when(step >= HALF)
    def _():
        delta_group(
            q_ref, g_ref, gain_ref, cum, att_ref.at[group], inv_ref[...], mean_ref[...],
            od_ref, m_ref, gt_ref,
        )


def delta_own_kernel(
    c_ref, q_ref, g_ref, gain_ref, col_ref, att_ref, inv_ref, mean_ref, gt_in, od_ref, m_ref, gt_ref, kept_ref
):
    cum = col_ref[c_ref[0] * HALF + pl.program_id(0)]
    delta_group(
        q_ref, g_ref, gain_ref, cum, att_ref, inv_ref[...], mean_ref[...], od_ref, m_ref, gt_ref
    )
    kept_ref[...] = m_ref[...]


def backward_kernel(
    own, c_ref, od_ref, q_ref, k_ref, v_ref, fw_ref, col_ref, row_ref, i_ref, *rest
):
    qg_ref, ki_ref, vi_ref = rest[-3:]
    half = c_ref[0] if own else 1 - c_ref[0]
    cum = col_ref[half * HALF + pl.program_id(0)]
    growth = jnp.exp(cum)
    for j in range(GH):
        at = lanes(j)
        decay = decay_table(cum[:, j : j + 1], row_ref[j : j + 1, :])
        delta = od_ref[:, at]
        weights = (dot(delta, v_ref[:, at], 1, 1) * decay).astype(BF16)
        inter = growth[:, j : j + 1] * rows_by_state_t(delta, i_ref[j])
        qg_ref[:, at] = (dot(weights, k_ref[:, at], 1, 0) + inter).astype(BF16)
        ki_ref[:, at] = dot(weights, q_ref[:, at], 0, 0)
        vi_ref[:, at] = dot(fw_ref[j], delta, 0, 0)


def finish_group(k_ref, v_ref, cum, ki_ref, vi_ref, state_at, kg_ref, vg_ref):
    shrink = jnp.exp(cum[T - 1 : T, :] - cum)
    for j in range(GH):
        at = lanes(j)
        state = state_at(j)
        scale = shrink[:, j : j + 1]
        kg_ref[:, at] = (ki_ref[:, at] + scale * rows_by_state_t(v_ref[:, at], state)).astype(BF16)
        vg_ref[:, at] = (vi_ref[:, at] + scale * rows_by_state(k_ref[:, at], state)).astype(BF16)


def finish_own_kernel(
    c_ref, k_ref, v_ref, col_ref, ki_ref, vi_ref, d_ref, got_ref, lg_ref, kg_ref, vg_ref
):
    cum = col_ref[c_ref[0] * HALF + pl.program_id(0)]
    finish_group(
        k_ref, v_ref, cum, ki_ref, vi_ref,
        lambda j: own_state(False, c_ref, d_ref, got_ref, lg_ref, j), kg_ref, vg_ref,
    )


def finish_other_kernel(
    c_ref, k_ref, v_ref, col_ref, ki_ref, vi_ref, x_ref, kg_in, vg_in, kg_ref, vg_ref
):
    cum = col_ref[(1 - c_ref[0]) * HALF + pl.program_id(0)]
    finish_group(k_ref, v_ref, cum, ki_ref, vi_ref, lambda j: x_ref[j], kg_ref, vg_ref)


class Free:
    def __init__(self, array):
        self.array = array


def in_hbm(a):
    return pltpu.with_memory_space_constraint(a, pltpu.HBM)


def call(kernel, name, grid, in_specs, out_specs, out_shape, args, flops, scratch=(), aliases=None):
    bare = [a.array if isinstance(a, Free) else a for a in [*args[1:], *out_shape]]
    nbytes = sum(math.prod(a.shape) * a.dtype.itemsize for a in bare)
    return pl.pallas_call(
        kernel,
        name=name,
        grid_spec=pltpu.PrefetchScalarGridSpec(
            num_scalar_prefetch=1,
            grid=grid,
            in_specs=in_specs,
            out_specs=out_specs,
            scratch_shapes=scratch,
        ),
        out_shape=[s.array if isinstance(s, Free) else pltpu.HBM(s.shape, s.dtype) for s in out_shape],
        input_output_aliases=aliases or {},
        compiler_params=pltpu.CompilerParams(vmem_limit_bytes=16 << 20),
        cost_estimate=pl.CostEstimate(flops=flops, bytes_accessed=nbytes, transcendentals=0),
    )(args[0], *[a.array if isinstance(a, Free) else in_hbm(a) for a in args[1:]])


def shape(dims, dtype=F32):
    return jax.ShapeDtypeStruct(dims, dtype)


def half_of(own, c_ref):
    return c_ref[0] if own else 1 - c_ref[0]


def wide(own, group=lambda i: i):
    return pl.BlockSpec((None, T, GW), lambda i, c: (0, 0, half_of(own, c) * HALF + group(i)))


def narrow(group=lambda i: i):
    return pl.BlockSpec((T, GW), lambda i, c: (0, group(i)))


def gain_block(own, group=lambda i: i):
    return pl.BlockSpec((1, GW), lambda i, c: (0, half_of(own, c) * HALF + group(i)))


def row_block(own):
    return pl.BlockSpec((GH, T), lambda i, c: (half_of(own, c) * HALF + i, 0))


def gains_block(own, group=lambda i: i):
    return pl.BlockSpec(
        (None, GH, HD),
        lambda i, c: (jnp.bitwise_xor(half_of(own, c) * HALF + group(i), c[1]), 0, 0),
    )


def state_block(rows=HD, group=lambda i: i):
    return pl.BlockSpec((GH, rows, HD), lambda i, c: (group(i), 0, 0))


LOG_BLOCK = pl.BlockSpec((GH, 8, HD), lambda i, c: (i, HD // 8, 0))
COL_WHOLE = pl.BlockSpec((NG, T, GH), lambda i, c: (0, 0, 0))
STAT_WHOLE = pl.BlockSpec((T, HD), lambda i, c: (0, 0))
ANY = pl.BlockSpec(memory_space=pl.ANY)
STATES = shape((NC, HD, HD))
LOGGED = shape((NC, HD + 8, HD))
HALF_F32 = shape((T, HALF * GW))
HALF_BF16 = shape((T, HALF * GW), BF16)
WHOLE_BF16 = shape((1, T, NG * GW), BF16)
STAT = shape((T, HD))
GAINS = shape((NG, GH, HD))
MM = 2 * T * HD * HD * NC
SM = 2 * T * T * HD * NC


def swap_cores(values):
    return lax.ppermute(values, "core", [(0, 1), (1, 0)])


def chips_all_to_all(values):
    return lax.all_to_all(values, ("x", "y"), split_axis=0, concat_axis=0, tiled=True)


def scan_over_chips(upward, place, got, logs, gains=None):
    whole_m = pl.BlockSpec((NC, HD, HD), lambda i, c: (0, 0, 0))
    whole_l = pl.BlockSpec((NC, 8, HD), lambda i, c: (0, HD // 8, 0))
    rows = HD if upward else HD + 8
    whole_t = pl.BlockSpec((rows, HD), lambda i, c: (0, 0))
    more = [] if upward else [Free(gains)]
    more_specs = [pl.BlockSpec((8, HD), lambda i, c: (0, 0))] * len(more)
    (total,) = call(
        functools.partial(total_kernel, upward), "half_total", (1,),
        [whole_m, whole_l] + more_specs, [whole_t], [Free(shape((rows, HD)))],
        (place, Free(got), Free(logs), *more), 0,
    )
    before = lax.ppermute(total, "zh", [(0, 1)] if upward else [(0, 1), (1, 0)])
    return call(
        functools.partial(scan_kernel, upward), "chip_scan", (1,),
        [whole_m, whole_l, whole_t] + more_specs,
        [pl.BlockSpec((NC, rows, HD), lambda i, c: (0, 0, 0))], [shape((NC, rows, HD))],
        (place, Free(got), Free(logs), Free(before), *more), 0,
    )[0]


def per_device(queries, key_rows, value_rows, out_grad, log_decay, norm_gain):
    core = jnp.stack([lax.axis_index(a).astype(jnp.int32) for a in ("core", "dp", "zh")])
    q, k, v, g = queries, key_rows, value_rows, out_grad
    gain = norm_gain.reshape(1, NG * GW)
    logs = jnp.transpose(log_decay[0])

    sent, col, row = call(
        state_first_kernel, "states_other", (HALF,),
        [wide(False), wide(False), pl.BlockSpec((NG * GH, T), lambda i, c: (0, 0))],
        [state_block(HD + 8), COL_WHOLE, pl.BlockSpec((NG * GH, T), lambda i, c: (0, 0))],
        [Free(LOGGED), shape((NG, T, GH)), shape((NG * GH, T))],
        (core, k, v, logs), MM,
    )
    got = swap_cores(sent)
    (own,) = call(
        state_second_kernel, "states_own", (HALF,),
        [wide(True), wide(True), COL_WHOLE], [state_block(HD + 8)], [Free(LOGGED)],
        (core, k, v, col), MM,
    )
    (chip_total,) = call(
        functools.partial(combine_kernel, True), "chip_total", (HALF,),
        [state_block(), state_block(), LOG_BLOCK, LOG_BLOCK], [state_block(HD + 8)], [LOGGED],
        (core, Free(own), Free(got), Free(own), Free(got)), 0,
    )
    gathered = chips_all_to_all(chip_total)

    weights, inside = {}, {}
    for mine in (True, False):
        weights[mine], inside[mine] = call(
            functools.partial(forward_kernel, mine), "forward_inside", (HALF,),
            [wide(mine), wide(mine), wide(mine), COL_WHOLE, row_block(mine)],
            [pl.BlockSpec((GH, T, T), lambda i, c: (i, 0, 0)), narrow()],
            [shape((NC, T, T), BF16), HALF_F32],
            (core, q, k, v, col, row), 2 * SM,
        )

    gathered, inside[True], inside[False] = lax.optimization_barrier(
        (gathered, inside[True], inside[False])
    )
    scanned = chips_all_to_all(scan_over_chips(True, core, gathered, gathered))
    (onward,) = call(
        functools.partial(send_kernel, True), "onward", (HALF,),
        [state_block(), state_block(), LOG_BLOCK], [state_block()], [Free(STATES)],
        (core, Free(scanned), Free(own), Free(own)), 0,
    )
    state_other = swap_cores(onward)
    att_own, state_own, squares, products = call(
        attend_own_kernel, "attend_own", (HALF,),
        [wide(True), wide(True), gain_block(True), COL_WHOLE, narrow(), state_block(), state_block(),
         LOG_BLOCK],
        [narrow(), state_block(), STAT_WHOLE, STAT_WHOLE],
        [Free(HALF_F32), STATES, Free(STAT), Free(STAT)],
        (core, q, g, gain, col, inside[True], Free(scanned), Free(got), Free(got)), 2 * MM,
    )

    def turn(i):
        return jnp.where(i < HALF, i, 2 * HALF - 1 - i)

    def first(i):
        return jnp.minimum(i, HALF - 1)

    def second(i):
        return jnp.minimum(2 * HALF - 1 - i, HALF - 1)

    delta_other, moment_sent, gains, inverse, mean = call(
        attend_other_kernel, "attend_other", (2 * HALF,),
        [wide(False, turn), wide(False, turn), gain_block(False, turn), COL_WHOLE, narrow(first),
         state_block(HD, first), STAT_WHOLE, STAT_WHOLE],
        [narrow(second), state_block(HD, second), gains_block(False, second), STAT_WHOLE, STAT_WHOLE],
        [HALF_BF16, Free(STATES), GAINS, Free(STAT), Free(STAT)],
        (core, q, g, gain, col, inside[False], Free(state_other), Free(squares), Free(products)), 3 * MM,
        scratch=[pltpu.VMEM((HALF, T, GW), F32), pltpu.VMEM((T, HD), F32), pltpu.VMEM((T, HD), F32)],
    )
    moment_got = swap_cores(moment_sent)
    delta_own, moment_own, gains, moment_own_kept = call(
        delta_own_kernel, "delta_own", (HALF,),
        [wide(True), wide(True), gain_block(True), COL_WHOLE, narrow(), STAT_WHOLE, STAT_WHOLE, ANY],
        [narrow(), state_block(), gains_block(True), state_block()],
        [HALF_BF16, Free(STATES), GAINS, STATES],
        (core, q, g, gain, col, Free(att_own), Free(inverse), Free(mean), gains), MM,
        aliases={8: 2},
    )
    chip_moment, moment_got_kept = call(
        functools.partial(combine_kernel, False), "chip_moment", (HALF,),
        [state_block(), state_block(), LOG_BLOCK, LOG_BLOCK], [state_block()] * 2, [STATES] * 2,
        (core, Free(moment_own), Free(moment_got), Free(own), Free(got)), 0,
    )
    gathered_back = chips_all_to_all(chip_moment)

    collected = gains[0]
    for distance in range(1, NG):
        collected += lax.ppermute(gains[distance], "dp", [(i, i ^ distance) for i in range(NG)])

    delta = {True: delta_own, False: delta_other}
    state = {True: state_own, False: Free(state_other)}
    query_grad, key_inside, value_inside = (), {}, {}
    for mine in (True, False):
        *query_grad, key_inside[mine], value_inside[mine] = call(
            functools.partial(backward_kernel, mine), "backward_inside", (HALF,),
            [narrow(), wide(mine), wide(mine), wide(mine),
             pl.BlockSpec((GH, T, T), lambda i, c: (i, 0, 0)), COL_WHOLE, row_block(mine), state_block()]
            + [ANY] * len(query_grad),
            [wide(mine), narrow(), narrow()],
            [WHOLE_BF16, HALF_F32, HALF_F32],
            (core, delta[mine], q, k, v, weights[mine], col, row, state[mine], *query_grad),
            4 * SM + 2 * MM,
            aliases={9: 0} if query_grad else None,
        )

    gathered_back, key_inside[True] = lax.optimization_barrier((gathered_back, key_inside[True]))
    scanned_back = chips_all_to_all(scan_over_chips(False, core, gathered_back, gathered, collected))
    scanned_back, key_inside[False] = lax.optimization_barrier((scanned_back, key_inside[False]))
    onward_back, collected = call(
        functools.partial(send_kernel, False), "onward_back", (HALF,),
        [state_block(), state_block(), LOG_BLOCK, LOG_BLOCK],
        [state_block(), pl.BlockSpec((8, HD), lambda i, c: (0, 0))],
        [Free(STATES), Free(shape((8, HD)))],
        (core, Free(scanned_back), moment_own_kept, Free(own), Free(scanned_back)), 0,
    )
    later_other = swap_cores(onward_back)
    key_grad, value_grad = call(
        finish_own_kernel, "finish_own", (HALF,),
        [wide(True), wide(True), COL_WHOLE, narrow(), narrow(), state_block(), state_block(), LOG_BLOCK],
        [wide(True), wide(True)], [WHOLE_BF16, WHOLE_BF16],
        (core, k, v, col, key_inside[True], value_inside[True], Free(scanned_back), moment_got_kept, Free(got)), 4 * MM,
    )
    key_grad, value_grad = call(
        finish_other_kernel, "finish_other", (HALF,),
        [wide(False), wide(False), COL_WHOLE, narrow(), narrow(), state_block(), ANY, ANY],
        [wide(False), wide(False)], [WHOLE_BF16, WHOLE_BF16],
        (core, k, v, col, key_inside[False], value_inside[False], Free(later_other), key_grad, value_grad),
        4 * MM, aliases={7: 0, 8: 1},
    )
    collected = (collected + swap_cores(collected))[0]
    at = lax.axis_index("y") * 32 + lax.axis_index("core") * 16
    positions = T * lax.axis_size(ALL)
    gain_grad = lax.dynamic_slice_in_dim(collected, at, 16) * (1.0 / math.sqrt(positions))
    return query_grad[0], key_grad, value_grad, gain_grad


def solution(mesh):
    fine = Mesh(mesh.devices.reshape(4, 2, 4, 4, 2), ALL)
    rows = P("dp", ("zh", "x", "y", "core"), None)
    return jax.shard_map(
        per_device,
        mesh=fine,
        in_specs=(rows,) * 5 + (P(),),
        out_specs=(rows, rows, rows, P(ALL)),
        check_vma=False,
    )
```

```python
import functools
import math

import jax
import jax.numpy as jnp
from jax import lax
from jax.experimental import pallas as pl
from jax.experimental.pallas import tpu as pltpu
from jax.sharding import Mesh, PartitionSpec as P

EPSILON = 1e-06
HIGHEST = lax.Precision.HIGHEST
F32 = jnp.float32
BF16 = jnp.bfloat16
T = 192
HD = 128
GH = 8
GW = GH * HD
NG = 4
HALF = NG // 2
NC = 16
ALL = ("dp", "zh", "x", "y", "core")


def dot(a, b, ca, cb):
    return lax.dot_general(a, b, (((ca,), (cb,)), ((), ())), preferred_element_type=F32)


def lanes(j):
    return slice(j * HD, (j + 1) * HD)


def split_state(state, axis):
    high = state.astype(BF16)
    low = (state - high.astype(F32)).astype(BF16)
    return jnp.concatenate([high, low], axis)


def rows_by_state(rows, state):
    return dot(jnp.concatenate([rows, rows], 1), split_state(state, 0), 1, 0)


def rows_by_state_t(rows, state):
    return dot(jnp.concatenate([rows, rows], 1), split_state(state, 1), 1, 1)


def decay_table(col, row):
    row_ids = lax.broadcasted_iota(jnp.int32, (T, T), 0)
    col_ids = lax.broadcasted_iota(jnp.int32, (T, T), 1)
    return jnp.exp(jnp.where(row_ids >= col_ids, col - row, -jnp.inf))


def states_of(k_ref, v_ref, cum, store):
    last = cum[T - 1 : T, :]
    shrink = jnp.exp(last - cum)
    for j in range(GH):
        late = (k_ref[:, lanes(j)].astype(F32) * shrink[:, j : j + 1]).astype(BF16)
        store(j, dot(late, v_ref[:, lanes(j)], 0, 0), jnp.broadcast_to(last[:, j : j + 1], (8, HD)))


def state_first_kernel(c_ref, k_ref, v_ref, ld_ref, s_ref, col_ref, row_ref):
    i = pl.program_id(0)

    @pl.when(i == 0)
    def _():
        upper = (
            lax.broadcasted_iota(jnp.int32, (T, T), 0) <= lax.broadcasted_iota(jnp.int32, (T, T), 1)
        ).astype(F32)
        logs = ld_ref[...]
        row_ref[...] = lax.dot_general(
            logs, upper, (((1,), (0,)), ((), ())), precision=HIGHEST, preferred_element_type=F32
        )
        col = lax.dot_general(
            upper, logs, (((0,), (1,)), ((), ())), precision=HIGHEST, preferred_element_type=F32
        )
        for g in range(NG):
            col_ref[g] = col[:, g * GH : (g + 1) * GH]

    def store(j, state, log):
        s_ref[j, :HD, :] = state
        s_ref[j, HD:, :] = log

    states_of(k_ref, v_ref, col_ref[(1 - c_ref[0]) * HALF + i], store)


def state_second_kernel(c_ref, k_ref, v_ref, col_ref, s_ref, kept_ref, l_ref):
    def store(j, state, log):
        s_ref[j] = state
        kept_ref[j] = state
        l_ref[j] = log

    states_of(k_ref, v_ref, col_ref[c_ref[0] * HALF + pl.program_id(0)], store)


def combine_kernel(upward, c_ref, own_ref, got_ref, lo_ref, lg_ref, p_ref, kept_ref, log_ref=None):
    first = c_ref[0] == 0 if upward else c_ref[0] == 1
    for j in range(GH):
        log_own, log_got = lo_ref[j, 0:1, :], lg_ref[j, 0:1, :]
        scale_own = jnp.where(first, jnp.exp(log_got), 1.0)
        scale_got = jnp.where(first, 1.0, jnp.exp(log_own))
        p_ref[j, :HD, :] = scale_own * own_ref[j] + scale_got * got_ref[j]
        kept_ref[j] = got_ref[j]
        if upward:
            p_ref[j, HD:, :] = lo_ref[j] + lg_ref[j]
            log_ref[j] = lg_ref[j]


def total_kernel(upward, c_ref, m_ref, l_ref, *rest):
    run = jnp.zeros((HD, HD), F32)
    for i in range(NC) if upward else reversed(range(NC)):
        run = jnp.exp(l_ref[i, 0:1, :]) * run + m_ref[i]
    t_ref = rest[-1]
    t_ref[:HD, :] = run
    if not upward:
        t_ref[HD:, :] = rest[0][...]


def scan_kernel(upward, c_ref, m_ref, l_ref, t_ref, *rest):
    if upward:
        o_ref, log_ref = rest
        log_ref[...] = l_ref[...]
    else:
        gain_ref, o_ref = rest
        both = gain_ref[...] + t_ref[HD:, :]
    run = t_ref[:HD, :]
    run = jnp.where(c_ref[2] == (1 if upward else 0), run, 0.0)
    for i in range(NC) if upward else reversed(range(NC)):
        o_ref[i, :HD, :] = run
        run = jnp.exp(l_ref[i, 0:1, :]) * run + m_ref[i]
        if not upward:
            x = i // 4
            row = jnp.where(c_ref[2] == 0, both[x : x + 1, :], both[4 + x : 5 + x, :])
            o_ref[i, HD:, :] = jnp.broadcast_to(row, (8, HD))


def hand_on_kernel(
    upward, c_ref, d_ref, own_ref, got_ref, lo_ref, lg_ref, *rest
):
    if upward:
        send_ref, state_ref = rest
    else:
        gains_ref, send_ref, state_ref, sum_ref = rest
        part = gains_ref[0]
        for j in range(1, GH):
            part += gains_ref[j]

        @pl.when(pl.program_id(0) == 0)
        def _():
            sum_ref[...] = part

        @pl.when(pl.program_id(0) > 0)
        def _():
            sum_ref[...] += part

    at_edge = c_ref[0] == (0 if upward else 1)
    for j in range(GH):
        edge = d_ref[j]
        send_ref[j] = (
            jnp.where(at_edge, jnp.exp(lo_ref[j, 0:1, :]), 1.0) * edge
            + jnp.where(at_edge, 1.0, 0.0) * own_ref[j]
        )
        state_ref[j] = (
            jnp.where(at_edge, 1.0, jnp.exp(lg_ref[j, 0:1, :])) * edge
            + jnp.where(at_edge, 0.0, 1.0) * got_ref[j]
        )


def forward_kernel(own, c_ref, q_ref, k_ref, v_ref, col_ref, row_ref, fw_ref, in_ref):
    half = c_ref[0] if own else 1 - c_ref[0]
    cum = col_ref[half * HALF + pl.program_id(0)]
    for j in range(GH):
        decay = decay_table(cum[:, j : j + 1], row_ref[j : j + 1, :])
        scores = dot(q_ref[:, lanes(j)], k_ref[:, lanes(j)], 1, 1)
        weights = (scores * decay).astype(BF16)
        fw_ref[j] = weights
        in_ref[:, lanes(j)] = dot(weights, v_ref[:, lanes(j)], 1, 0)


def attend_group(q_ref, g_ref, gain_ref, cum, in_ref, state_at, att_ref, sq_ref, pr_ref):
    growth = jnp.exp(cum)
    squares = jnp.zeros((T, HD), F32)
    products = jnp.zeros((T, HD), F32)
    for j in range(GH):
        att = in_ref[:, lanes(j)] + growth[:, j : j + 1] * rows_by_state(q_ref[:, lanes(j)], state_at(j))
        att_ref[:, lanes(j)] = att
        squares += att * att
        products += att * (gain_ref[:, lanes(j)] * g_ref[:, lanes(j)].astype(F32))
    sq_ref[...] += squares
    pr_ref[...] += products


def attend_own_kernel(
    c_ref, q_ref, g_ref, gain_ref, col_ref, in_ref, x_ref, att_ref, i_ref, sq_ref, pr_ref
):
    @pl.when(pl.program_id(0) == 0)
    def _():
        sq_ref[...] = jnp.zeros_like(sq_ref)
        pr_ref[...] = jnp.zeros_like(pr_ref)

    def state_at(j):
        i_ref[j] = x_ref[j]
        return x_ref[j]

    cum = col_ref[c_ref[0] * HALF + pl.program_id(0)]
    attend_group(q_ref, g_ref, gain_ref, cum, in_ref, state_at, att_ref, sq_ref, pr_ref)


def delta_group(q_ref, g_ref, gain_ref, cum, att_ref, inverse, mean, od_ref, m_ref, gt_ref):
    growth = jnp.exp(cum)
    for j in range(GH):
        grad = g_ref[:, lanes(j)].astype(F32)
        normed = att_ref[:, lanes(j)] * inverse
        delta = (inverse * (gain_ref[:, lanes(j)] * grad - normed * mean)).astype(BF16)
        od_ref[:, lanes(j)] = delta
        gt_ref[j : j + 1, :] = jnp.sum(grad * normed, axis=0, keepdims=True)
        early = (q_ref[:, lanes(j)].astype(F32) * growth[:, j : j + 1]).astype(BF16)
        m_ref[j] = dot(early, delta, 0, 0)


def attend_other_kernel(
    c_ref, q_ref, g_ref, gain_ref, col_ref, in_ref, i_ref, sq_in, pr_in,
    od_ref, m_ref, gt_ref, inv_ref, mean_ref, att_ref, sq_ref, pr_ref,
):
    step = pl.program_id(0)
    group = jnp.where(step < HALF, step, 2 * HALF - 1 - step)
    cum = col_ref[(1 - c_ref[0]) * HALF + group]

    @pl.when(step == 0)
    def _():
        sq_ref[...] = sq_in[...]
        pr_ref[...] = pr_in[...]

    @pl.when(step < HALF)
    def _():
        attend_group(
            q_ref, g_ref, gain_ref, cum, in_ref, lambda j: i_ref[j], att_ref.at[group], sq_ref, pr_ref
        )

    @pl.when(step == HALF)
    def _():
        features = NG * GW
        inverse = lax.rsqrt(jnp.sum(sq_ref[...], axis=1, keepdims=True) * (1.0 / features) + EPSILON)
        mean = inverse * (jnp.sum(pr_ref[...], axis=1, keepdims=True) * (1.0 / features))
        inv_ref[...] = jnp.broadcast_to(inverse, (T, HD))
        mean_ref[...] = jnp.broadcast_to(mean, (T, HD))

    @pl.when(step >= HALF)
    def _():
        delta_group(
            q_ref, g_ref, gain_ref, cum, att_ref.at[group], inv_ref[...], mean_ref[...],
            od_ref, m_ref, gt_ref,
        )


def delta_own_kernel(
    c_ref, q_ref, g_ref, gain_ref, col_ref, att_ref, inv_ref, mean_ref, gt_in, od_ref, m_ref, gt_ref, kept_ref
):
    cum = col_ref[c_ref[0] * HALF + pl.program_id(0)]
    delta_group(
        q_ref, g_ref, gain_ref, cum, att_ref, inv_ref[...], mean_ref[...], od_ref, m_ref, gt_ref
    )
    kept_ref[...] = m_ref[...]


def backward_kernel(
    own, c_ref, od_ref, q_ref, k_ref, v_ref, fw_ref, col_ref, row_ref, i_ref, *rest
):
    qg_ref, ki_ref, vi_ref = rest[-3:]
    half = c_ref[0] if own else 1 - c_ref[0]
    cum = col_ref[half * HALF + pl.program_id(0)]
    growth = jnp.exp(cum)
    for j in range(GH):
        at = lanes(j)
        decay = decay_table(cum[:, j : j + 1], row_ref[j : j + 1, :])
        delta = od_ref[:, at]
        weights = (dot(delta, v_ref[:, at], 1, 1) * decay).astype(BF16)
        inter = growth[:, j : j + 1] * rows_by_state_t(delta, i_ref[j])
        qg_ref[:, at] = (dot(weights, k_ref[:, at], 1, 0) + inter).astype(BF16)
        ki_ref[:, at] = dot(weights, q_ref[:, at], 0, 0)
        vi_ref[:, at] = dot(fw_ref[j], delta, 0, 0)


def finish_kernel(own, c_ref, k_ref, v_ref, col_ref, ki_ref, vi_ref, x_ref, *rest):
    cum = col_ref[half_of(own, c_ref) * HALF + pl.program_id(0)]
    shrink = jnp.exp(cum[T - 1 : T, :] - cum)
    kg_ref, vg_ref = rest[-2:]
    for j in range(GH):
        at = lanes(j)
        scale = shrink[:, j : j + 1]
        kg_ref[:, at] = (ki_ref[:, at] + scale * rows_by_state_t(v_ref[:, at], x_ref[j])).astype(BF16)
        vg_ref[:, at] = (vi_ref[:, at] + scale * rows_by_state(k_ref[:, at], x_ref[j])).astype(BF16)


class Free:
    def __init__(self, array):
        self.array = array


def in_hbm(a):
    return pltpu.with_memory_space_constraint(a, pltpu.HBM)


def call(kernel, name, grid, in_specs, out_specs, out_shape, args, flops, scratch=(), aliases=None):
    bare = [a.array if isinstance(a, Free) else a for a in [*args[1:], *out_shape]]
    nbytes = sum(math.prod(a.shape) * a.dtype.itemsize for a in bare)
    return pl.pallas_call(
        kernel,
        name=name,
        grid_spec=pltpu.PrefetchScalarGridSpec(
            num_scalar_prefetch=1,
            grid=grid,
            in_specs=in_specs,
            out_specs=out_specs,
            scratch_shapes=scratch,
        ),
        out_shape=[s.array if isinstance(s, Free) else pltpu.HBM(s.shape, s.dtype) for s in out_shape],
        input_output_aliases=aliases or {},
        compiler_params=pltpu.CompilerParams(vmem_limit_bytes=16 << 20),
        cost_estimate=pl.CostEstimate(flops=flops, bytes_accessed=nbytes, transcendentals=0),
    )(args[0], *[a.array if isinstance(a, Free) else in_hbm(a) for a in args[1:]])


def shape(dims, dtype=F32):
    return jax.ShapeDtypeStruct(dims, dtype)


def half_of(own, c_ref):
    return c_ref[0] if own else 1 - c_ref[0]


def wide(own, group=lambda i: i):
    return pl.BlockSpec((None, T, GW), lambda i, c: (0, 0, half_of(own, c) * HALF + group(i)))


def narrow(group=lambda i: i):
    return pl.BlockSpec((T, GW), lambda i, c: (0, group(i)))


def gain_block(own, group=lambda i: i):
    return pl.BlockSpec((1, GW), lambda i, c: (0, half_of(own, c) * HALF + group(i)))


def row_block(own):
    return pl.BlockSpec((GH, T), lambda i, c: (half_of(own, c) * HALF + i, 0))


def gains_block(own, group=lambda i: i):
    return pl.BlockSpec(
        (None, GH, HD),
        lambda i, c: (jnp.bitwise_xor(half_of(own, c) * HALF + group(i), c[1]), 0, 0),
    )


def state_block(rows=HD, group=lambda i: i):
    return pl.BlockSpec((GH, rows, HD), lambda i, c: (group(i), 0, 0))


LOG_BLOCK = pl.BlockSpec((GH, 8, HD), lambda i, c: (i, 0, 0))
LOG_TAIL = pl.BlockSpec((GH, 8, HD), lambda i, c: (i, HD // 8, 0))
COL_WHOLE = pl.BlockSpec((NG, T, GH), lambda i, c: (0, 0, 0))
STAT_WHOLE = pl.BlockSpec((T, HD), lambda i, c: (0, 0))
ANY = pl.BlockSpec(memory_space=pl.ANY)
STATES = shape((NC, HD, HD))
LOGGED = shape((NC, HD + 8, HD))
LOGS = shape((NC, 8, HD))
HALF_F32 = shape((T, HALF * GW))
HALF_BF16 = shape((T, HALF * GW), BF16)
WHOLE_BF16 = shape((1, T, NG * GW), BF16)
STAT = shape((T, HD))
GAINS = shape((NG, GH, HD))
MM = 2 * T * HD * HD * NC
SM = 2 * T * T * HD * NC


def swap_cores(values):
    return lax.ppermute(values, "core", [(0, 1), (1, 0)])


def chips_all_to_all(values):
    return lax.all_to_all(values, ("x", "y"), split_axis=0, concat_axis=0, tiled=True)


def scan_over_chips(upward, place, got, logs, gains=None):
    whole_m = pl.BlockSpec((NC, HD, HD), lambda i, c: (0, 0, 0))
    whole_l = pl.BlockSpec((NC, 8, HD), lambda i, c: (0, HD // 8 if upward else 0, 0))
    logs_out = pl.BlockSpec((NC, 8, HD), lambda i, c: (0, 0, 0))
    rows = HD if upward else HD + 8
    whole_t = pl.BlockSpec((rows, HD), lambda i, c: (0, 0))
    more = [] if upward else [Free(gains)]
    more_specs = [pl.BlockSpec((8, HD), lambda i, c: (0, 0))] * len(more)
    (total,) = call(
        functools.partial(total_kernel, upward), "half_total", (1,),
        [whole_m, whole_l] + more_specs, [whole_t], [Free(shape((rows, HD)))],
        (place, Free(got), Free(logs), *more), 0,
    )
    before = lax.ppermute(total, "zh", [(0, 1), (1, 0)])
    outs = [pl.BlockSpec((NC, rows, HD), lambda i, c: (0, 0, 0))] + [logs_out] * upward
    return call(
        functools.partial(scan_kernel, upward), "chip_scan", (1,),
        [whole_m, whole_l, whole_t] + more_specs, outs, [shape((NC, rows, HD)), LOGS][: len(outs)],
        (place, Free(got), Free(logs), Free(before), *more), 0,
    )


def per_device(queries, key_rows, value_rows, out_grad, log_decay, norm_gain):
    core = jnp.stack([lax.axis_index(a).astype(jnp.int32) for a in ("core", "dp", "zh")])
    q, k, v, g = queries, key_rows, value_rows, out_grad
    gain = norm_gain.reshape(1, NG * GW)
    logs = jnp.transpose(log_decay[0])

    sent, col, row = call(
        state_first_kernel, "states_other", (HALF,),
        [wide(False), wide(False), pl.BlockSpec((NG * GH, T), lambda i, c: (0, 0))],
        [state_block(HD + 8), COL_WHOLE, pl.BlockSpec((NG * GH, T), lambda i, c: (0, 0))],
        [Free(LOGGED), shape((NG, T, GH)), shape((NG * GH, T))],
        (core, k, v, logs), MM,
    )
    got = swap_cores(sent)
    own, own_kept, log_own = call(
        state_second_kernel, "states_own", (HALF,),
        [wide(True), wide(True), COL_WHOLE],
        [state_block(), state_block(), LOG_BLOCK], [Free(STATES), STATES, LOGS],
        (core, k, v, col), MM,
    )
    chip_total, got_kept, log_got = call(
        functools.partial(combine_kernel, True), "chip_total", (HALF,),
        [state_block(), state_block(), LOG_BLOCK, LOG_TAIL],
        [state_block(HD + 8), state_block(), LOG_BLOCK], [LOGGED, STATES, LOGS],
        (core, Free(own), Free(got), Free(log_own), Free(got)), 0,
    )
    gathered = chips_all_to_all(chip_total)

    weights, inside = {}, {}
    for mine in (True, False):
        weights[mine], inside[mine] = call(
            functools.partial(forward_kernel, mine), "forward_inside", (HALF,),
            [wide(mine), wide(mine), wide(mine), COL_WHOLE, row_block(mine)],
            [pl.BlockSpec((GH, T, T), lambda i, c: (i, 0, 0)), narrow()],
            [shape((NC, T, T), BF16), HALF_F32],
            (core, q, k, v, col, row), 2 * SM,
        )

    gathered, inside[True], inside[False] = lax.optimization_barrier(
        (gathered, inside[True], inside[False])
    )
    before_chips, log_chips = scan_over_chips(True, core, gathered, gathered)
    scanned = chips_all_to_all(before_chips)
    onward, state_here = call(
        functools.partial(hand_on_kernel, True), "onward", (HALF,),
        [state_block()] * 3 + [LOG_BLOCK] * 2, [state_block()] * 2, [Free(STATES)] * 2,
        (core, Free(scanned), Free(own_kept), Free(got_kept), Free(log_own), Free(log_got)), 0,
    )
    state_other = swap_cores(onward)
    att_own, state_own, squares, products = call(
        attend_own_kernel, "attend_own", (HALF,),
        [wide(True), wide(True), gain_block(True), COL_WHOLE, narrow(), state_block()],
        [narrow(), state_block(), STAT_WHOLE, STAT_WHOLE],
        [Free(HALF_F32), STATES, Free(STAT), Free(STAT)],
        (core, Free(q), Free(g), gain, col, Free(inside[True]), Free(state_here)), 2 * MM,
    )

    def turn(i):
        return jnp.where(i < HALF, i, 2 * HALF - 1 - i)

    def first(i):
        return jnp.minimum(i, HALF - 1)

    def second(i):
        return jnp.minimum(2 * HALF - 1 - i, HALF - 1)

    delta_other, moment_sent, gains, inverse, mean = call(
        attend_other_kernel, "attend_other", (2 * HALF,),
        [wide(False, turn), wide(False, turn), gain_block(False, turn), COL_WHOLE, narrow(first),
         state_block(HD, first), STAT_WHOLE, STAT_WHOLE],
        [narrow(second), state_block(HD, second), gains_block(False, second), STAT_WHOLE, STAT_WHOLE],
        [HALF_BF16, Free(STATES), GAINS, Free(STAT), Free(STAT)],
        (core, Free(q), Free(g), gain, col, Free(inside[False]), Free(state_other), Free(squares), Free(products)), 3 * MM,
        scratch=[pltpu.VMEM((HALF, T, GW), F32), pltpu.VMEM((T, HD), F32), pltpu.VMEM((T, HD), F32)],
    )
    moment_got = swap_cores(moment_sent)
    delta_own, moment_own, gains, moment_own_kept = call(
        delta_own_kernel, "delta_own", (HALF,),
        [wide(True), wide(True), gain_block(True), COL_WHOLE, narrow(), STAT_WHOLE, STAT_WHOLE, ANY],
        [narrow(), state_block(), gains_block(True), state_block()],
        [HALF_BF16, Free(STATES), GAINS, STATES],
        (core, Free(q), Free(g), gain, col, Free(att_own), Free(inverse), Free(mean), gains), MM,
        aliases={8: 2},
    )
    chip_moment, moment_got_kept = call(
        functools.partial(combine_kernel, False), "chip_moment", (HALF,),
        [state_block(), state_block(), LOG_BLOCK, LOG_BLOCK], [state_block()] * 2, [STATES] * 2,
        (core, Free(moment_own), Free(moment_got), Free(log_own), Free(log_got)), 0,
    )
    gathered_back = chips_all_to_all(chip_moment)

    collected = gains[0]
    for distance in range(1, NG):
        collected += lax.ppermute(gains[distance], "dp", [(i, i ^ distance) for i in range(NG)])

    delta = {True: delta_own, False: delta_other}
    state = {True: state_own, False: Free(state_other)}
    query_grad, key_inside, value_inside = (), {}, {}
    for mine in (True, False):
        *query_grad, key_inside[mine], value_inside[mine] = call(
            functools.partial(backward_kernel, mine), "backward_inside", (HALF,),
            [narrow(), wide(mine), wide(mine), wide(mine),
             pl.BlockSpec((GH, T, T), lambda i, c: (i, 0, 0)), COL_WHOLE, row_block(mine), state_block()]
            + [ANY] * len(query_grad),
            [wide(mine), narrow(), narrow()],
            [WHOLE_BF16, HALF_F32, HALF_F32],
            (core, delta[mine], q, k, v, weights[mine], col, row, state[mine], *query_grad),
            4 * SM + 2 * MM,
            aliases={9: 0} if query_grad else None,
        )

    gathered_back, key_inside[True] = lax.optimization_barrier((gathered_back, key_inside[True]))
    (after_chips,) = scan_over_chips(False, core, gathered_back, log_chips, collected)
    scanned_back = chips_all_to_all(after_chips)
    scanned_back, key_inside[False] = lax.optimization_barrier((scanned_back, key_inside[False]))
    onward_back, later_here, collected = call(
        functools.partial(hand_on_kernel, False), "onward_back", (HALF,),
        [state_block()] * 3 + [LOG_BLOCK] * 2 + [LOG_TAIL],
        [state_block(), state_block(), pl.BlockSpec((8, HD), lambda i, c: (0, 0))],
        [Free(STATES), Free(STATES), Free(shape((8, HD)))],
        (core, Free(scanned_back), moment_own_kept, moment_got_kept, Free(log_own),
         Free(log_got), Free(scanned_back)), 0,
    )
    later_other = swap_cores(onward_back)
    later = {True: later_here, False: later_other}
    grads = ()
    for mine in (True, False):
        grads = call(
            functools.partial(finish_kernel, mine), "finish", (HALF,),
            [wide(mine), wide(mine), COL_WHOLE, narrow(), narrow(), state_block()] + [ANY] * len(grads),
            [wide(mine)] * 2, [WHOLE_BF16] * 2,
            (core, k, v, col, key_inside[mine], value_inside[mine],
             Free(later[mine]), *grads), 4 * MM, aliases={7: 0, 8: 1} if grads else None,
        )
    key_grad, value_grad = grads
    collected = (collected + swap_cores(collected))[0]
    at = lax.axis_index("y") * 32 + lax.axis_index("core") * 16
    positions = T * lax.axis_size(ALL)
    gain_grad = lax.dynamic_slice_in_dim(collected, at, 16) * (1.0 / math.sqrt(positions))
    return query_grad[0], key_grad, value_grad, gain_grad


def solution(mesh):
    fine = Mesh(mesh.devices.reshape(4, 2, 4, 4, 2), ALL)
    rows = P("dp", ("zh", "x", "y", "core"), None)
    return jax.shard_map(
        per_device,
        mesh=fine,
        in_specs=(rows,) * 5 + (P(),),
        out_specs=(rows, rows, rows, P(ALL)),
        check_vma=False,
    )
```

```python
import functools
import math

import jax
import jax.numpy as jnp
from jax import lax
from jax.experimental import pallas as pl
from jax.experimental.pallas import tpu as pltpu
from jax.sharding import Mesh, PartitionSpec as P

EPSILON = 1e-06
HIGHEST = lax.Precision.HIGHEST
F32 = jnp.float32
BF16 = jnp.bfloat16
T = 192
HD = 128
GH = 8
FH = 4
GW = GH * HD
NG = 4
HALF = NG // 2
NC = 16
ALL = ("dp", "zh", "x", "y", "core")


def dot(a, b, ca, cb):
    return lax.dot_general(a, b, (((ca,), (cb,)), ((), ())), preferred_element_type=F32)


def lanes(j):
    return slice(j * HD, (j + 1) * HD)


def split_state(state, axis):
    high = state.astype(BF16)
    low = (state - high.astype(F32)).astype(BF16)
    return jnp.concatenate([high, low], axis)


def rows_by_state(rows, state):
    return dot(jnp.concatenate([rows, rows], 1), split_state(state, 0), 1, 0)


def rows_by_state_t(rows, state):
    return dot(jnp.concatenate([rows, rows], 1), split_state(state, 1), 1, 1)


def columns(row_ref, heads=GH):
    cum = jnp.transpose(row_ref[...])
    if heads == GH:
        return cum
    return jnp.where(pl.program_id(0) % 2 == 0, cum[:, :heads], cum[:, heads:])


def decay_table(col, row):
    row_ids = lax.broadcasted_iota(jnp.int32, (T, T), 0)
    col_ids = lax.broadcasted_iota(jnp.int32, (T, T), 1)
    return jnp.exp(jnp.where(row_ids >= col_ids, col - row, -jnp.inf))


def states_of(k_ref, v_ref, row_ref, store):
    cum = columns(row_ref, FH)
    last = cum[T - 1 : T, :]
    shrink = jnp.exp(last - cum)
    for j in range(FH):
        late = (k_ref[:, lanes(j)].astype(F32) * shrink[:, j : j + 1]).astype(BF16)
        store(j, dot(late, v_ref[:, lanes(j)], 0, 0), jnp.broadcast_to(last[:, j : j + 1], (8, HD)))


def state_first_kernel(c_ref, k_ref, v_ref, ld_ref, s_ref, row_ref):
    i = pl.program_id(0)

    @pl.when(i == 0)
    def _():
        upper = (
            lax.broadcasted_iota(jnp.int32, (T, T), 0) <= lax.broadcasted_iota(jnp.int32, (T, T), 1)
        ).astype(F32)
        logs = ld_ref[...]
        row_ref[...] = lax.dot_general(
            logs, upper, (((1,), (0,)), ((), ())), precision=HIGHEST, preferred_element_type=F32
        )

    def store(j, state, log):
        s_ref[j, :HD, :] = state
        s_ref[j, HD:, :] = log

    group = (1 - c_ref[0]) * HALF + i // 2
    states_of(k_ref, v_ref, row_ref.at[pl.ds(pl.multiple_of(group * GH, GH), GH)], store)


def state_second_kernel(c_ref, k_ref, v_ref, row_ref, s_ref, l_ref):
    def store(j, state, log):
        s_ref[j] = state
        l_ref[j] = log

    states_of(k_ref, v_ref, row_ref, store)


def combine_kernel(upward, c_ref, own_ref, got_ref, lo_ref, lg_ref, p_ref, log_ref=None):
    first = c_ref[0] == 0 if upward else c_ref[0] == 1
    for j in range(GH):
        log_own, log_got = lo_ref[j, 0:1, :], lg_ref[j, 0:1, :]
        scale_own = jnp.where(first, jnp.exp(log_got), 1.0)
        scale_got = jnp.where(first, 1.0, jnp.exp(log_own))
        p_ref[j, :HD, :] = scale_own * own_ref[j] + scale_got * got_ref[j]
        if upward:
            p_ref[j, HD:, :] = lo_ref[j] + lg_ref[j]
            log_ref[j] = lg_ref[j]


def total_kernel(upward, c_ref, m_ref, l_ref, *rest):
    run = jnp.zeros((HD, HD), F32)
    for i in range(NC) if upward else reversed(range(NC)):
        run = jnp.exp(l_ref[i, 0:1, :]) * run + m_ref[i]
    t_ref = rest[-1]
    t_ref[:HD, :] = run
    if not upward:
        t_ref[HD:, :] = rest[0][...]


def scan_kernel(upward, c_ref, m_ref, l_ref, t_ref, *rest):
    if upward:
        o_ref, log_ref = rest
        log_ref[...] = l_ref[...]
    else:
        gain_ref, o_ref = rest
        both = gain_ref[...] + t_ref[HD:, :]
    run = t_ref[:HD, :]
    run = jnp.where(c_ref[2] == (1 if upward else 0), run, 0.0)
    for i in range(NC) if upward else reversed(range(NC)):
        o_ref[i, :HD, :] = run
        run = jnp.exp(l_ref[i, 0:1, :]) * run + m_ref[i]
        if not upward:
            x = i // 4
            row = jnp.where(c_ref[2] == 0, both[x : x + 1, :], both[4 + x : 5 + x, :])
            o_ref[i, HD:, :] = jnp.broadcast_to(row, (8, HD))


def hand_on_kernel(
    upward, c_ref, d_ref, own_ref, got_ref, lo_ref, lg_ref, *rest
):
    if upward:
        send_ref, state_ref = rest
    else:
        gains_ref, send_ref, state_ref, sum_ref = rest
        part = gains_ref[0]
        for j in range(1, GH):
            part += gains_ref[j]

        @pl.when(pl.program_id(0) == 0)
        def _():
            sum_ref[...] = part

        @pl.when(pl.program_id(0) > 0)
        def _():
            sum_ref[...] += part

    at_edge = c_ref[0] == (0 if upward else 1)
    for j in range(GH):
        edge = d_ref[j]
        send_ref[j] = (
            jnp.where(at_edge, jnp.exp(lo_ref[j, 0:1, :]), 1.0) * edge
            + jnp.where(at_edge, 1.0, 0.0) * own_ref[j]
        )
        state_ref[j] = (
            jnp.where(at_edge, 1.0, jnp.exp(lg_ref[j, 0:1, :])) * edge
            + jnp.where(at_edge, 0.0, 1.0) * got_ref[j]
        )


def forward_kernel(c_ref, q_ref, k_ref, v_ref, row_ref, fw_ref, in_ref):
    cum = columns(row_ref)
    for j in range(GH):
        decay = decay_table(cum[:, j : j + 1], row_ref[j : j + 1, :])
        scores = dot(q_ref[:, lanes(j)], k_ref[:, lanes(j)], 1, 1)
        weights = (scores * decay).astype(BF16)
        fw_ref[j] = weights
        in_ref[:, lanes(j)] = dot(weights, v_ref[:, lanes(j)], 1, 0)


def attend_group(q_ref, g_ref, gain_ref, cum, in_ref, x_ref, att_ref, sq_ref, pr_ref):
    growth = jnp.exp(cum)
    squares = jnp.zeros((T, HD), F32)
    products = jnp.zeros((T, HD), F32)
    for j in range(GH):
        att = in_ref[:, lanes(j)] + growth[:, j : j + 1] * rows_by_state(q_ref[:, lanes(j)], x_ref[j])
        att_ref[:, lanes(j)] = att
        squares += att * att
        products += att * (gain_ref[:, lanes(j)] * g_ref[:, lanes(j)].astype(F32))
    sq_ref[...] += squares
    pr_ref[...] += products


def attend_own_kernel(
    c_ref, q_ref, g_ref, gain_ref, row_ref, in_ref, x_ref, att_ref, sq_ref, pr_ref
):
    @pl.when(pl.program_id(0) == 0)
    def _():
        sq_ref[...] = jnp.zeros_like(sq_ref)
        pr_ref[...] = jnp.zeros_like(pr_ref)

    attend_group(
        q_ref, g_ref, gain_ref, columns(row_ref), in_ref, x_ref, att_ref, sq_ref, pr_ref
    )


def delta_group(q_ref, g_ref, gain_ref, cum, att_ref, inverse, mean, od_ref, m_ref, gt_ref):
    growth = jnp.exp(cum)
    for j in range(GH):
        grad = g_ref[:, lanes(j)].astype(F32)
        normed = att_ref[:, lanes(j)] * inverse
        delta = (inverse * (gain_ref[:, lanes(j)] * grad - normed * mean)).astype(BF16)
        od_ref[:, lanes(j)] = delta
        gt_ref[j : j + 1, :] = jnp.sum(grad * normed, axis=0, keepdims=True)
        early = (q_ref[:, lanes(j)].astype(F32) * growth[:, j : j + 1]).astype(BF16)
        m_ref[j] = dot(early, delta, 0, 0)


def attend_other_kernel(
    c_ref, q_ref, g_ref, gain_ref, row_ref, in_ref, i_ref, sq_in, pr_in,
    od_ref, m_ref, gt_ref, inv_ref, mean_ref, att_ref, sq_ref, pr_ref,
):
    step = pl.program_id(0)
    group = jnp.where(step < HALF, step, 2 * HALF - 1 - step)
    cum = columns(row_ref)

    @pl.when(step == 0)
    def _():
        sq_ref[...] = sq_in[...]
        pr_ref[...] = pr_in[...]

    @pl.when(step < HALF)
    def _():
        attend_group(
            q_ref, g_ref, gain_ref, cum, in_ref, i_ref, att_ref.at[group], sq_ref, pr_ref
        )

    @pl.when(step == HALF)
    def _():
        features = NG * GW
        inverse = lax.rsqrt(jnp.sum(sq_ref[...], axis=1, keepdims=True) * (1.0 / features) + EPSILON)
        mean = inverse * (jnp.sum(pr_ref[...], axis=1, keepdims=True) * (1.0 / features))
        inv_ref[...] = jnp.broadcast_to(inverse, (T, HD))
        mean_ref[...] = jnp.broadcast_to(mean, (T, HD))

    @pl.when(step >= HALF)
    def _():
        delta_group(
            q_ref, g_ref, gain_ref, cum, att_ref.at[group], inv_ref[...], mean_ref[...],
            od_ref, m_ref, gt_ref,
        )


def delta_own_kernel(
    c_ref, q_ref, g_ref, gain_ref, row_ref, att_ref, inv_ref, mean_ref, gt_in, od_ref, m_ref, gt_ref
):
    delta_group(
        q_ref, g_ref, gain_ref, columns(row_ref), att_ref, inv_ref[...], mean_ref[...], od_ref, m_ref, gt_ref
    )


def backward_kernel(
    c_ref, od_ref, q_ref, k_ref, v_ref, fw_ref, row_ref, i_ref, *rest
):
    qg_ref, ki_ref, vi_ref = rest[-3:]
    cum = columns(row_ref)
    growth = jnp.exp(cum)
    for j in range(GH):
        at = lanes(j)
        decay = decay_table(cum[:, j : j + 1], row_ref[j : j + 1, :])
        delta = od_ref[:, at]
        weights = (dot(delta, v_ref[:, at], 1, 1) * decay).astype(BF16)
        inter = growth[:, j : j + 1] * rows_by_state_t(delta, i_ref[j])
        qg_ref[:, at] = (dot(weights, k_ref[:, at], 1, 0) + inter).astype(BF16)
        ki_ref[:, at] = dot(weights, q_ref[:, at], 0, 0)
        vi_ref[:, at] = dot(fw_ref[j], delta, 0, 0)


def finish_kernel(c_ref, k_ref, v_ref, row_ref, ki_ref, vi_ref, x_ref, *rest):
    cum = columns(row_ref, FH)
    shrink = jnp.exp(cum[T - 1 : T, :] - cum)
    kg_ref, vg_ref = rest[-2:]
    for j in range(FH):
        at = lanes(j)
        scale = shrink[:, j : j + 1]
        kg_ref[:, at] = (ki_ref[:, at] + scale * rows_by_state_t(v_ref[:, at], x_ref[j])).astype(BF16)
        vg_ref[:, at] = (vi_ref[:, at] + scale * rows_by_state(k_ref[:, at], x_ref[j])).astype(BF16)


class Kept:
    def __init__(self, array):
        self.array = array
        self.shape, self.dtype = array.shape, array.dtype


def in_hbm(a):
    return pltpu.with_memory_space_constraint(a.array, pltpu.HBM) if isinstance(a, Kept) else a


def call(
    kernel, name, grid, in_specs, out_specs, out_shape, args, flops, scratch=(), aliases=None, kept=False
):
    place, *args = args
    nbytes = sum(math.prod(a.shape) * a.dtype.itemsize for a in [*args, *out_shape])
    if kept:
        args, out_shape = [Kept(a) for a in args], [Kept(s) for s in out_shape]
    return pl.pallas_call(
        kernel,
        name=name,
        grid_spec=pltpu.PrefetchScalarGridSpec(
            num_scalar_prefetch=1,
            grid=grid,
            in_specs=in_specs,
            out_specs=out_specs,
            scratch_shapes=scratch,
        ),
        out_shape=[pltpu.HBM(s.shape, s.dtype) if isinstance(s, Kept) else s for s in out_shape],
        input_output_aliases=aliases or {},
        compiler_params=pltpu.CompilerParams(vmem_limit_bytes=16 << 20),
        cost_estimate=pl.CostEstimate(flops=flops, bytes_accessed=nbytes, transcendentals=0),
    )(place, *[in_hbm(a) for a in args])


def shape(dims, dtype=F32):
    return jax.ShapeDtypeStruct(dims, dtype)


def half_of(own, c_ref):
    return c_ref[0] if own else 1 - c_ref[0]


def wide(own, group=lambda i: i):
    return pl.BlockSpec((None, T, GW), lambda i, c: (0, 0, half_of(own, c) * HALF + group(i)))


def narrow(group=lambda i: i):
    return pl.BlockSpec((T, GW), lambda i, c: (0, group(i)))


def fine(own):
    return pl.BlockSpec((None, T, FH * HD), lambda i, c: (0, 0, half_of(own, c) * (NC // FH) + i))


FINE_NARROW = pl.BlockSpec((T, FH * HD), lambda i, c: (0, i))


def fine_block(rows=HD):
    return pl.BlockSpec((FH, rows, HD), lambda i, c: (i, 0, 0))


def gain_block(own, group=lambda i: i):
    return pl.BlockSpec((1, GW), lambda i, c: (0, half_of(own, c) * HALF + group(i)))


def row_block(own, group=lambda i: i):
    return pl.BlockSpec((GH, T), lambda i, c: (half_of(own, c) * HALF + group(i), 0))


def gains_block(own, group=lambda i: i):
    return pl.BlockSpec(
        (None, GH, HD),
        lambda i, c: (jnp.bitwise_xor(half_of(own, c) * HALF + group(i), c[1]), 0, 0),
    )


def state_block(rows=HD, group=lambda i: i):
    return pl.BlockSpec((GH, rows, HD), lambda i, c: (group(i), 0, 0))


LOG_BLOCK = pl.BlockSpec((GH, 8, HD), lambda i, c: (i, 0, 0))
LOG_TAIL = pl.BlockSpec((GH, 8, HD), lambda i, c: (i, HD // 8, 0))
STAT_WHOLE = pl.BlockSpec((T, HD), lambda i, c: (0, 0))
ANY = pl.BlockSpec(memory_space=pl.ANY)
STATES = shape((NC, HD, HD))
LOGGED = shape((NC, HD + 8, HD))
LOGS = shape((NC, 8, HD))
HALF_F32 = shape((T, HALF * GW))
HALF_BF16 = shape((T, HALF * GW), BF16)
WHOLE_BF16 = shape((1, T, NG * GW), BF16)
STAT = shape((T, HD))
GAINS = shape((NG, GH, HD))
MM = 2 * T * HD * HD * NC
SM = 2 * T * T * HD * NC


def swap_cores(values):
    return lax.ppermute(values, "core", [(0, 1), (1, 0)])


def chips_all_to_all(values):
    return lax.all_to_all(values, ("x", "y"), split_axis=0, concat_axis=0, tiled=True)


def scan_over_chips(upward, place, got, logs, gains=None):
    whole_m = pl.BlockSpec((NC, HD, HD), lambda i, c: (0, 0, 0))
    whole_l = pl.BlockSpec((NC, 8, HD), lambda i, c: (0, HD // 8 if upward else 0, 0))
    logs_out = pl.BlockSpec((NC, 8, HD), lambda i, c: (0, 0, 0))
    rows = HD if upward else HD + 8
    whole_t = pl.BlockSpec((rows, HD), lambda i, c: (0, 0))
    more = [] if upward else [gains]
    more_specs = [pl.BlockSpec((8, HD), lambda i, c: (0, 0))] * len(more)
    (total,) = call(
        functools.partial(total_kernel, upward), "half_total", (1,),
        [whole_m, whole_l] + more_specs, [whole_t], [shape((rows, HD))],
        (place, got, logs, *more), 0,
    )
    before = lax.ppermute(total, "zh", [(0, 1), (1, 0)])
    outs = [pl.BlockSpec((NC, rows, HD), lambda i, c: (0, 0, 0))] + [logs_out] * upward
    return call(
        functools.partial(scan_kernel, upward), "chip_scan", (1,),
        [whole_m, whole_l, whole_t] + more_specs, outs, [Kept(shape((NC, rows, HD))), LOGS][: len(outs)],
        (place, got, logs, before, *more), 0,
    )


def per_device(queries, key_rows, value_rows, out_grad, log_decay, norm_gain):
    core = jnp.stack([lax.axis_index(a).astype(jnp.int32) for a in ("core", "dp", "zh")])
    q, k, v, g = queries, key_rows, value_rows, out_grad
    gain = norm_gain.reshape(1, NG * GW)
    logs = jnp.transpose(log_decay[0])

    whole_rows = pl.BlockSpec((NG * GH, T), lambda i, c: (0, 0))
    sent, row = call(
        state_first_kernel, "states_other", (NC // FH,),
        [fine(False), fine(False), whole_rows], [fine_block(HD + 8), whole_rows],
        [LOGGED, shape((NG * GH, T))], (core, Kept(k), Kept(v), logs), MM,
    )
    got = swap_cores(sent)
    own, log_own = call(
        state_second_kernel, "states_own", (NC // FH,),
        [fine(True), fine(True), row_block(True, lambda i: i // 2)], [fine_block(), fine_block(8)],
        [STATES, LOGS],
        (core, Kept(k), Kept(v), row), MM,
    )
    chip_total, log_got = call(
        functools.partial(combine_kernel, True), "chip_total", (HALF,),
        [state_block(), state_block(), LOG_BLOCK, LOG_TAIL],
        [state_block(HD + 8), LOG_BLOCK], [Kept(LOGGED), LOGS],
        (core, own, got, log_own, got), 0,
    )
    gathered = chips_all_to_all(chip_total)

    weights, inside = {}, {}
    for mine in (True, False):
        weights[mine], inside[mine] = call(
            forward_kernel, "forward_inside", (HALF,),
            [wide(mine), wide(mine), wide(mine), row_block(mine)],
            [pl.BlockSpec((GH, T, T), lambda i, c: (i, 0, 0)), narrow()],
            [shape((NC, T, T), BF16), HALF_F32],
            (core, q, k, v, row), 2 * SM, kept=True,
        )

    gathered, inside[True], inside[False] = lax.optimization_barrier(
        (gathered, inside[True], inside[False])
    )
    before_chips, log_chips = scan_over_chips(True, core, gathered, gathered)
    scanned = chips_all_to_all(before_chips)
    onward, state_here = call(
        functools.partial(hand_on_kernel, True), "onward", (HALF,),
        [state_block()] * 3 + [LOG_BLOCK] * 2, [state_block()] * 2, [STATES] * 2,
        (core, scanned, own, got, log_own, log_got), 0,
    )
    state_other = swap_cores(onward)
    att_own, squares, products = call(
        attend_own_kernel, "attend_own", (HALF,),
        [wide(True), wide(True), gain_block(True), row_block(True), narrow(), state_block()],
        [narrow(), STAT_WHOLE, STAT_WHOLE], [HALF_F32, STAT, STAT],
        (core, q, g, gain, row, inside[True], state_here), 2 * MM,
    )

    def turn(i):
        return jnp.where(i < HALF, i, 2 * HALF - 1 - i)

    def first(i):
        return jnp.minimum(i, HALF - 1)

    def second(i):
        return jnp.minimum(2 * HALF - 1 - i, HALF - 1)

    delta_other, moment_sent, gains, inverse, mean = call(
        attend_other_kernel, "attend_other", (2 * HALF,),
        [wide(False, turn), wide(False, turn), gain_block(False, turn), row_block(False, turn), narrow(first),
         state_block(HD, first), STAT_WHOLE, STAT_WHOLE],
        [narrow(second), state_block(HD, second), gains_block(False, second), STAT_WHOLE, STAT_WHOLE],
        [HALF_BF16, STATES, Kept(GAINS), STAT, STAT],
        (core, q, g, gain, row, inside[False], state_other, squares, products), 3 * MM,
        scratch=[pltpu.VMEM((HALF, T, GW), F32), pltpu.VMEM((T, HD), F32), pltpu.VMEM((T, HD), F32)],
    )
    moment_got = swap_cores(moment_sent)
    delta_own, moment_own, gains = call(
        delta_own_kernel, "delta_own", (HALF,),
        [wide(True), wide(True), gain_block(True), row_block(True), narrow(), STAT_WHOLE, STAT_WHOLE, ANY],
        [narrow(), state_block(), gains_block(True)],
        [HALF_BF16, STATES, Kept(GAINS)],
        (core, q, g, gain, row, att_own, inverse, mean, Kept(gains)), MM,
        aliases={8: 2},
    )
    (chip_moment,) = call(
        functools.partial(combine_kernel, False), "chip_moment", (HALF,),
        [state_block(), state_block(), LOG_BLOCK, LOG_BLOCK], [state_block()], [Kept(STATES)],
        (core, moment_own, moment_got, log_own, log_got), 0,
    )
    gathered_back = chips_all_to_all(chip_moment)

    collected = gains[0]
    for distance in range(1, NG):
        collected += lax.ppermute(gains[distance], "dp", [(i, i ^ distance) for i in range(NG)])

    delta = {True: delta_own, False: delta_other}
    state = {True: state_here, False: state_other}
    query_grad, key_inside, value_inside = (), {}, {}
    for mine in (True, False):
        *query_grad, key_inside[mine], value_inside[mine] = call(
            backward_kernel, "backward_inside", (HALF,),
            [narrow(), wide(mine), wide(mine), wide(mine),
             pl.BlockSpec((GH, T, T), lambda i, c: (i, 0, 0)), row_block(mine), state_block()]
            + [ANY] * len(query_grad),
            [wide(mine), narrow(), narrow()],
            [WHOLE_BF16, HALF_F32, HALF_F32],
            (core, delta[mine], q, k, v, weights[mine], row, state[mine], *query_grad),
            4 * SM + 2 * MM, aliases={8: 0} if query_grad else None, kept=True,
        )

    gathered_back, key_inside[True] = lax.optimization_barrier((gathered_back, key_inside[True]))
    (after_chips,) = scan_over_chips(False, core, gathered_back, log_chips, collected)
    scanned_back = chips_all_to_all(after_chips)
    scanned_back, key_inside[False] = lax.optimization_barrier((scanned_back, key_inside[False]))
    onward_back, later_here, collected = call(
        functools.partial(hand_on_kernel, False), "onward_back", (HALF,),
        [state_block()] * 3 + [LOG_BLOCK] * 2 + [LOG_TAIL],
        [state_block(), state_block(), pl.BlockSpec((8, HD), lambda i, c: (0, 0))],
        [STATES, STATES, shape((8, HD))],
        (core, scanned_back, Kept(moment_own), Kept(moment_got), log_own,
         log_got, scanned_back), 0,
    )
    later_other = swap_cores(onward_back)
    later = {True: later_here, False: later_other}
    grads = ()
    for mine in (True, False):
        grads = call(
            finish_kernel, "finish", (NC // FH,),
            [fine(mine), fine(mine), row_block(mine, lambda i: i // 2), FINE_NARROW, FINE_NARROW,
             fine_block()] + [ANY] * len(grads),
            [fine(mine)] * 2, [Kept(WHOLE_BF16)] * 2,
            (core, Kept(k), Kept(v), row, Kept(key_inside[mine]), Kept(value_inside[mine]),
             later[mine], *[Kept(a) for a in grads]), 4 * MM, aliases={7: 0, 8: 1} if grads else None,
        )
    key_grad, value_grad = grads
    collected = (collected + swap_cores(collected))[0]
    at = lax.axis_index("y") * 32 + lax.axis_index("core") * 16
    positions = T * lax.axis_size(ALL)
    gain_grad = lax.dynamic_slice_in_dim(collected, at, 16) * (1.0 / math.sqrt(positions))
    return query_grad[0], key_grad, value_grad, gain_grad


def solution(mesh):
    fine = Mesh(mesh.devices.reshape(4, 2, 4, 4, 2), ALL)
    rows = P("dp", ("zh", "x", "y", "core"), None)
    return jax.shard_map(
        per_device,
        mesh=fine,
        in_specs=(rows,) * 5 + (P(),),
        out_specs=(rows, rows, rows, P(ALL)),
        check_vma=False,
    )
```

```python
import functools
import math

import jax
import jax.numpy as jnp
from jax import lax
from jax.experimental import pallas as pl
from jax.experimental.pallas import tpu as pltpu
from jax.sharding import Mesh, PartitionSpec as P

EPSILON = 1e-06
HIGHEST = lax.Precision.HIGHEST
F32 = jnp.float32
BF16 = jnp.bfloat16
T = 192
HD = 128
GH = 8
FH = 8
GW = GH * HD
NG = 4
HALF = NG // 2
NC = 16
ALL = ("dp", "zh", "x", "y", "core")


def dot(a, b, ca, cb):
    return lax.dot_general(a, b, (((ca,), (cb,)), ((), ())), preferred_element_type=F32)


def lanes(j):
    return slice(j * HD, (j + 1) * HD)


def split_state(state, axis):
    high = state.astype(BF16)
    low = (state - high.astype(F32)).astype(BF16)
    return jnp.concatenate([high, low], axis)


def rows_by_state(rows, state):
    return dot(jnp.concatenate([rows, rows], 1), split_state(state, 0), 1, 0)


def rows_by_state_t(rows, state):
    return dot(jnp.concatenate([rows, rows], 1), split_state(state, 1), 1, 1)


def columns(row_ref, heads=GH):
    cum = jnp.transpose(row_ref[...])
    if heads == GH:
        return cum
    return jnp.where(pl.program_id(0) % 2 == 0, cum[:, :heads], cum[:, heads:])


def decay_table(col, row):
    row_ids = lax.broadcasted_iota(jnp.int32, (T, T), 0)
    col_ids = lax.broadcasted_iota(jnp.int32, (T, T), 1)
    return jnp.exp(jnp.where(row_ids >= col_ids, col - row, -jnp.inf))


def states_of(k_ref, v_ref, row_ref, store):
    cum = columns(row_ref, FH)
    last = cum[T - 1 : T, :]
    shrink = jnp.exp(last - cum)
    for j in range(FH):
        late = (k_ref[:, lanes(j)].astype(F32) * shrink[:, j : j + 1]).astype(BF16)
        store(j, dot(late, v_ref[:, lanes(j)], 0, 0), jnp.broadcast_to(last[:, j : j + 1], (8, HD)))


def state_first_kernel(c_ref, k_ref, v_ref, ld_ref, s_ref, row_ref):
    i = pl.program_id(0)

    @pl.when(i == 0)
    def _():
        upper = (
            lax.broadcasted_iota(jnp.int32, (T, T), 0) <= lax.broadcasted_iota(jnp.int32, (T, T), 1)
        ).astype(F32)
        logs = ld_ref[...]
        row_ref[...] = lax.dot_general(
            logs, upper, (((1,), (0,)), ((), ())), precision=HIGHEST, preferred_element_type=F32
        )

    def store(j, state, log):
        s_ref[j, :HD, :] = state
        s_ref[j, HD:, :] = log

    group = (1 - c_ref[0]) * HALF + i
    states_of(k_ref, v_ref, row_ref.at[pl.ds(pl.multiple_of(group * GH, GH), GH)], store)


def state_second_kernel(c_ref, k_ref, v_ref, row_ref, s_ref, l_ref):
    def store(j, state, log):
        s_ref[j] = state
        l_ref[j] = log

    states_of(k_ref, v_ref, row_ref, store)


def combine_kernel(upward, c_ref, own_ref, got_ref, lo_ref, lg_ref, p_ref, log_ref=None):
    first = c_ref[0] == 0 if upward else c_ref[0] == 1
    for j in range(GH):
        log_own, log_got = lo_ref[j, 0:1, :], lg_ref[j, 0:1, :]
        scale_own = jnp.where(first, jnp.exp(log_got), 1.0)
        scale_got = jnp.where(first, 1.0, jnp.exp(log_own))
        p_ref[j, :HD, :] = scale_own * own_ref[j] + scale_got * got_ref[j]
        if upward:
            p_ref[j, HD:, :] = lo_ref[j] + lg_ref[j]
            log_ref[j] = lg_ref[j]


def total_kernel(upward, c_ref, m_ref, l_ref, *rest):
    run = jnp.zeros((HD, HD), F32)
    for i in range(NC) if upward else reversed(range(NC)):
        run = jnp.exp(l_ref[i, 0:1, :]) * run + m_ref[i]
    t_ref = rest[-1]
    t_ref[:HD, :] = run
    if not upward:
        t_ref[HD:, :] = rest[0][...]


def scan_kernel(upward, c_ref, m_ref, l_ref, t_ref, *rest):
    if upward:
        o_ref, log_ref = rest
        log_ref[...] = l_ref[...]
    else:
        gain_ref, o_ref = rest
        both = gain_ref[...] + t_ref[HD:, :]
    run = t_ref[:HD, :]
    run = jnp.where(c_ref[2] == (1 if upward else 0), run, 0.0)
    for i in range(NC) if upward else reversed(range(NC)):
        o_ref[i, :HD, :] = run
        run = jnp.exp(l_ref[i, 0:1, :]) * run + m_ref[i]
        if not upward:
            x = i // 4
            row = jnp.where(c_ref[2] == 0, both[x : x + 1, :], both[4 + x : 5 + x, :])
            o_ref[i, HD:, :] = jnp.broadcast_to(row, (8, HD))


def hand_on_kernel(
    upward, c_ref, d_ref, own_ref, got_ref, lo_ref, lg_ref, *rest
):
    if upward:
        send_ref, state_ref = rest
    else:
        gains_ref, send_ref, state_ref, sum_ref = rest
        part = gains_ref[0]
        for j in range(1, GH):
            part += gains_ref[j]

        @pl.when(pl.program_id(0) == 0)
        def _():
            sum_ref[...] = part

        @pl.when(pl.program_id(0) > 0)
        def _():
            sum_ref[...] += part

    at_edge = c_ref[0] == (0 if upward else 1)
    for j in range(GH):
        edge = d_ref[j]
        send_ref[j] = (
            jnp.where(at_edge, jnp.exp(lo_ref[j, 0:1, :]), 1.0) * edge
            + jnp.where(at_edge, 1.0, 0.0) * own_ref[j]
        )
        state_ref[j] = (
            jnp.where(at_edge, 1.0, jnp.exp(lg_ref[j, 0:1, :])) * edge
            + jnp.where(at_edge, 0.0, 1.0) * got_ref[j]
        )


def forward_kernel(c_ref, q_ref, k_ref, v_ref, row_ref, fw_ref, in_ref):
    cum = columns(row_ref)
    for j in range(GH):
        decay = decay_table(cum[:, j : j + 1], row_ref[j : j + 1, :])
        scores = dot(q_ref[:, lanes(j)], k_ref[:, lanes(j)], 1, 1)
        weights = (scores * decay).astype(BF16)
        fw_ref[j] = weights
        in_ref[:, lanes(j)] = dot(weights, v_ref[:, lanes(j)], 1, 0)


def attend_group(q_ref, g_ref, gain_ref, cum, in_ref, x_ref, att_ref, sq_ref, pr_ref):
    growth = jnp.exp(cum)
    squares = jnp.zeros((T, HD), F32)
    products = jnp.zeros((T, HD), F32)
    for j in range(GH):
        att = in_ref[:, lanes(j)] + growth[:, j : j + 1] * rows_by_state(q_ref[:, lanes(j)], x_ref[j])
        att_ref[:, lanes(j)] = att
        squares += att * att
        products += att * (gain_ref[:, lanes(j)] * g_ref[:, lanes(j)].astype(F32))
    sq_ref[...] += squares
    pr_ref[...] += products


def attend_own_kernel(
    c_ref, q_ref, g_ref, gain_ref, row_ref, in_ref, x_ref, att_ref, sq_ref, pr_ref
):
    @pl.when(pl.program_id(0) == 0)
    def _():
        sq_ref[...] = jnp.zeros_like(sq_ref)
        pr_ref[...] = jnp.zeros_like(pr_ref)

    attend_group(
        q_ref, g_ref, gain_ref, columns(row_ref), in_ref, x_ref, att_ref, sq_ref, pr_ref
    )


def delta_group(q_ref, g_ref, gain_ref, cum, att_ref, inverse, mean, od_ref, m_ref, gt_ref):
    growth = jnp.exp(cum)
    for j in range(GH):
        grad = g_ref[:, lanes(j)].astype(F32)
        normed = att_ref[:, lanes(j)] * inverse
        delta = (inverse * (gain_ref[:, lanes(j)] * grad - normed * mean)).astype(BF16)
        od_ref[:, lanes(j)] = delta
        gt_ref[j : j + 1, :] = jnp.sum(grad * normed, axis=0, keepdims=True)
        early = (q_ref[:, lanes(j)].astype(F32) * growth[:, j : j + 1]).astype(BF16)
        m_ref[j] = dot(early, delta, 0, 0)


def attend_other_kernel(
    c_ref, q_ref, g_ref, gain_ref, row_ref, in_ref, i_ref, sq_in, pr_in,
    od_ref, m_ref, gt_ref, inv_ref, mean_ref, att_ref, sq_ref, pr_ref,
):
    step = pl.program_id(0)
    group = jnp.where(step < HALF, step, 2 * HALF - 1 - step)
    cum = columns(row_ref)

    @pl.when(step == 0)
    def _():
        sq_ref[...] = sq_in[...]
        pr_ref[...] = pr_in[...]

    @pl.when(step < HALF)
    def _():
        attend_group(
            q_ref, g_ref, gain_ref, cum, in_ref, i_ref, att_ref.at[group], sq_ref, pr_ref
        )

    @pl.when(step == HALF)
    def _():
        features = NG * GW
        inverse = lax.rsqrt(jnp.sum(sq_ref[...], axis=1, keepdims=True) * (1.0 / features) + EPSILON)
        mean = inverse * (jnp.sum(pr_ref[...], axis=1, keepdims=True) * (1.0 / features))
        inv_ref[...] = jnp.broadcast_to(inverse, (T, HD))
        mean_ref[...] = jnp.broadcast_to(mean, (T, HD))

    @pl.when(step >= HALF)
    def _():
        delta_group(
            q_ref, g_ref, gain_ref, cum, att_ref.at[group], inv_ref[...], mean_ref[...],
            od_ref, m_ref, gt_ref,
        )


def delta_own_kernel(
    c_ref, q_ref, g_ref, gain_ref, row_ref, att_ref, inv_ref, mean_ref, od_ref, m_ref, gt_ref, kept_ref
):
    delta_group(
        q_ref, g_ref, gain_ref, columns(row_ref), att_ref, inv_ref[...], mean_ref[...], od_ref, m_ref, gt_ref
    )
    kept_ref[...] = m_ref[...]


def backward_kernel(
    c_ref, od_ref, q_ref, k_ref, v_ref, fw_ref, row_ref, i_ref, *rest
):
    qg_ref, ki_ref, vi_ref = rest[-3:]
    cum = columns(row_ref)
    growth = jnp.exp(cum)
    for j in range(GH):
        at = lanes(j)
        decay = decay_table(cum[:, j : j + 1], row_ref[j : j + 1, :])
        delta = od_ref[:, at]
        weights = (dot(delta, v_ref[:, at], 1, 1) * decay).astype(BF16)
        inter = growth[:, j : j + 1] * rows_by_state_t(delta, i_ref[j])
        qg_ref[:, at] = (dot(weights, k_ref[:, at], 1, 0) + inter).astype(BF16)
        ki_ref[:, at] = dot(weights, q_ref[:, at], 0, 0)
        vi_ref[:, at] = dot(fw_ref[j], delta, 0, 0)


def finish_kernel(c_ref, k_ref, v_ref, row_ref, ki_ref, vi_ref, x_ref, *rest):
    cum = columns(row_ref, FH)
    shrink = jnp.exp(cum[T - 1 : T, :] - cum)
    kg_ref, vg_ref = rest[-2:]
    for j in range(FH):
        at = lanes(j)
        scale = shrink[:, j : j + 1]
        kg_ref[:, at] = (ki_ref[:, at] + scale * rows_by_state_t(v_ref[:, at], x_ref[j])).astype(BF16)
        vg_ref[:, at] = (vi_ref[:, at] + scale * rows_by_state(k_ref[:, at], x_ref[j])).astype(BF16)


class Kept:
    def __init__(self, array):
        self.array = array
        self.shape, self.dtype = array.shape, array.dtype


def in_hbm(a):
    return pltpu.with_memory_space_constraint(a.array, pltpu.HBM) if isinstance(a, Kept) else a


def call(
    kernel, name, grid, in_specs, out_specs, out_shape, args, flops, scratch=(), aliases=None
):
    place, *args = args
    nbytes = sum(math.prod(a.shape) * a.dtype.itemsize for a in [*args, *out_shape])
    return pl.pallas_call(
        kernel,
        name=name,
        grid_spec=pltpu.PrefetchScalarGridSpec(
            num_scalar_prefetch=1,
            grid=grid,
            in_specs=in_specs,
            out_specs=out_specs,
            scratch_shapes=scratch,
        ),
        out_shape=[pltpu.HBM(s.shape, s.dtype) if isinstance(s, Kept) else s for s in out_shape],
        input_output_aliases=aliases or {},
        compiler_params=pltpu.CompilerParams(vmem_limit_bytes=16 << 20),
        cost_estimate=pl.CostEstimate(flops=flops, bytes_accessed=nbytes, transcendentals=0),
    )(place, *[in_hbm(a) for a in args])


def shape(dims, dtype=F32):
    return jax.ShapeDtypeStruct(dims, dtype)


def half_of(own, c_ref):
    return c_ref[0] if own else 1 - c_ref[0]


def wide(own, group=lambda i: i):
    return pl.BlockSpec((None, T, GW), lambda i, c: (0, 0, half_of(own, c) * HALF + group(i)))


def narrow(group=lambda i: i):
    return pl.BlockSpec((T, GW), lambda i, c: (0, group(i)))


def fine(own):
    return pl.BlockSpec((None, T, FH * HD), lambda i, c: (0, 0, half_of(own, c) * (NC // FH) + i))


FINE_NARROW = pl.BlockSpec((T, FH * HD), lambda i, c: (0, i))


def fine_block(rows=HD):
    return pl.BlockSpec((FH, rows, HD), lambda i, c: (i, 0, 0))


def gain_block(own, group=lambda i: i):
    return pl.BlockSpec((1, GW), lambda i, c: (0, half_of(own, c) * HALF + group(i)))


def row_block(own, group=lambda i: i):
    return pl.BlockSpec((GH, T), lambda i, c: (half_of(own, c) * HALF + group(i), 0))


def gains_block(group=lambda i: i):
    return pl.BlockSpec((None, GH, HD), lambda i, c: (jnp.bitwise_xor(group(i), c[1] % 2), 0, 0))


def state_block(rows=HD, group=lambda i: i):
    return pl.BlockSpec((GH, rows, HD), lambda i, c: (group(i), 0, 0))


LOG_BLOCK = pl.BlockSpec((GH, 8, HD), lambda i, c: (i, 0, 0))
LOG_TAIL = pl.BlockSpec((GH, 8, HD), lambda i, c: (i, HD // 8, 0))
STAT_WHOLE = pl.BlockSpec((T, HD), lambda i, c: (0, 0))
ANY = pl.BlockSpec(memory_space=pl.ANY)
STATES = shape((NC, HD, HD))
LOGGED = shape((NC, HD + 8, HD))
LOGS = shape((NC, 8, HD))
HALF_F32 = shape((T, HALF * GW))
HALF_BF16 = shape((T, HALF * GW), BF16)
WHOLE_BF16 = shape((1, T, NG * GW), BF16)
STAT = shape((T, HD))
GAINS = shape((HALF, GH, HD))
MM = 2 * T * HD * HD * NC
SM = 2 * T * T * HD * NC


def swap_cores(values):
    return lax.ppermute(values, "core", [(0, 1), (1, 0)])


def chips_all_to_all(values):
    return lax.all_to_all(values, ("x", "y"), split_axis=0, concat_axis=0, tiled=True)


def scan_over_chips(upward, place, got, logs, gains=None):
    whole_m = pl.BlockSpec((NC, HD, HD), lambda i, c: (0, 0, 0))
    whole_l = pl.BlockSpec((NC, 8, HD), lambda i, c: (0, HD // 8 if upward else 0, 0))
    logs_out = pl.BlockSpec((NC, 8, HD), lambda i, c: (0, 0, 0))
    rows = HD if upward else HD + 8
    whole_t = pl.BlockSpec((rows, HD), lambda i, c: (0, 0))
    more = [] if upward else [gains]
    more_specs = [pl.BlockSpec((8, HD), lambda i, c: (0, 0))] * len(more)
    (total,) = call(
        functools.partial(total_kernel, upward), "half_total", (1,),
        [whole_m, whole_l] + more_specs, [whole_t], [shape((rows, HD))],
        (place, got, logs, *more), 0,
    )
    before = lax.ppermute(total, "zh", [(0, 1), (1, 0)])
    outs = [pl.BlockSpec((NC, rows, HD), lambda i, c: (0, 0, 0))] + [logs_out] * upward
    return call(
        functools.partial(scan_kernel, upward), "chip_scan", (1,),
        [whole_m, whole_l, whole_t] + more_specs, outs, [Kept(shape((NC, rows, HD))), LOGS][: len(outs)],
        (place, got, logs, before, *more), 0,
    )


def per_device(queries, key_rows, value_rows, out_grad, log_decay, norm_gain):
    core = jnp.stack([lax.axis_index(a).astype(jnp.int32) for a in ("core", "dp", "zh")])
    q, k, v, g = queries, key_rows, value_rows, out_grad
    gain = norm_gain.reshape(1, NG * GW)
    logs = jnp.transpose(log_decay[0])

    whole_rows = pl.BlockSpec((NG * GH, T), lambda i, c: (0, 0))
    sent, row = call(
        state_first_kernel, "states_other", (NC // FH,),
        [fine(False), fine(False), whole_rows], [fine_block(HD + 8), whole_rows],
        [LOGGED, shape((NG * GH, T))], (core, Kept(k), Kept(v), logs), MM,
    )
    got = swap_cores(sent)
    own, log_own = call(
        state_second_kernel, "states_own", (NC // FH,),
        [fine(True), fine(True), row_block(True)], [fine_block(), fine_block(8)],
        [STATES, LOGS],
        (core, Kept(k), Kept(v), row), MM,
    )
    chip_total, log_got = call(
        functools.partial(combine_kernel, True), "chip_total", (HALF,),
        [state_block(), state_block(), LOG_BLOCK, LOG_TAIL],
        [state_block(HD + 8), LOG_BLOCK], [Kept(LOGGED), LOGS],
        (core, own, got, log_own, got), 0,
    )
    gathered = chips_all_to_all(chip_total)

    weights, inside = {}, {}
    for mine in (True, False):
        weights[mine], inside[mine] = call(
            forward_kernel, "forward_inside", (HALF,),
            [wide(mine), wide(mine), wide(mine), row_block(mine)],
            [pl.BlockSpec((GH, T, T), lambda i, c: (i, 0, 0)), narrow()],
            [Kept(shape((NC, T, T), BF16)), Kept(HALF_F32)],
            (core, Kept(q), Kept(k), Kept(v), row), 2 * SM,
        )

    gathered, inside[True], inside[False] = lax.optimization_barrier(
        (gathered, inside[True], inside[False])
    )
    before_chips, log_chips = scan_over_chips(True, core, gathered, gathered)
    scanned = chips_all_to_all(before_chips)
    onward, state_here = call(
        functools.partial(hand_on_kernel, True), "onward", (HALF,),
        [state_block()] * 3 + [LOG_BLOCK] * 2, [state_block()] * 2, [STATES] * 2,
        (core, scanned, own, got, log_own, log_got), 0,
    )
    state_other = swap_cores(onward)
    att_own, squares, products = call(
        attend_own_kernel, "attend_own", (HALF,),
        [wide(True), wide(True), gain_block(True), row_block(True), narrow(), state_block()],
        [narrow(), STAT_WHOLE, STAT_WHOLE], [HALF_F32, STAT, STAT],
        (core, q, g, gain, row, inside[True], state_here), 2 * MM,
    )

    def turn(i):
        return jnp.where(i < HALF, i, 2 * HALF - 1 - i)

    def first(i):
        return jnp.minimum(i, HALF - 1)

    def second(i):
        return jnp.minimum(2 * HALF - 1 - i, HALF - 1)

    delta_other, moment_sent, gains_other, inverse, mean = call(
        attend_other_kernel, "attend_other", (2 * HALF,),
        [wide(False, turn), wide(False, turn), gain_block(False, turn), row_block(False, turn), narrow(first),
         state_block(HD, first), STAT_WHOLE, STAT_WHOLE],
        [narrow(second), state_block(HD, second), gains_block(second), STAT_WHOLE, STAT_WHOLE],
        [Kept(HALF_BF16), STATES, GAINS, STAT, STAT],
        (core, q, g, gain, row, inside[False], state_other, squares, products), 3 * MM,
        scratch=[pltpu.VMEM((HALF, T, GW), F32), pltpu.VMEM((T, HD), F32), pltpu.VMEM((T, HD), F32)],
    )
    moment_got = swap_cores(moment_sent)
    delta_own, moment_own, gains_own, moment_kept = call(
        delta_own_kernel, "delta_own", (HALF,),
        [wide(True), wide(True), gain_block(True), row_block(True), narrow(), STAT_WHOLE, STAT_WHOLE],
        [narrow(), state_block(), gains_block(), state_block()],
        [Kept(HALF_BF16), STATES, GAINS, Kept(STATES)],
        (core, q, g, gain, row, att_own, inverse, mean), MM,
    )
    (chip_moment,) = call(
        functools.partial(combine_kernel, False), "chip_moment", (HALF,),
        [state_block(), state_block(), LOG_BLOCK, LOG_BLOCK], [state_block()], [Kept(STATES)],
        (core, moment_own, moment_got, log_own, log_got), 0,
    )
    gathered_back = chips_all_to_all(chip_moment)

    near = core[0] == core[1] // 2
    gains = [*jnp.where(near, gains_own, gains_other), *jnp.where(near, gains_other, gains_own)]
    collected = gains[0]
    for distance in range(1, NG):
        collected += lax.ppermute(gains[distance], "dp", [(i, i ^ distance) for i in range(NG)])

    delta = {True: delta_own, False: delta_other}
    state = {True: state_here, False: state_other}
    query_grad, key_inside, value_inside = (), {}, {}
    for mine in (True, False):
        *query_grad, key_inside[mine], value_inside[mine] = call(
            backward_kernel, "backward_inside", (HALF,),
            [narrow(), wide(mine), wide(mine), wide(mine),
             pl.BlockSpec((GH, T, T), lambda i, c: (i, 0, 0)), row_block(mine), state_block()]
            + [ANY] * len(query_grad),
            [wide(mine), narrow(), narrow()],
            [Kept(WHOLE_BF16), Kept(HALF_F32), Kept(HALF_F32)],
            (core, Kept(delta[mine]), Kept(q), Kept(k), Kept(v), Kept(weights[mine]), row, state[mine],
             *[Kept(a) for a in query_grad]),
            4 * SM + 2 * MM, aliases={8: 0} if query_grad else None,
        )

    gathered_back, key_inside[True] = lax.optimization_barrier((gathered_back, key_inside[True]))
    (after_chips,) = scan_over_chips(False, core, gathered_back, log_chips, collected)
    scanned_back = chips_all_to_all(after_chips)
    scanned_back, key_inside[False] = lax.optimization_barrier((scanned_back, key_inside[False]))
    onward_back, later_here, collected = call(
        functools.partial(hand_on_kernel, False), "onward_back", (HALF,),
        [state_block()] * 3 + [LOG_BLOCK] * 2 + [LOG_TAIL],
        [state_block(), state_block(), pl.BlockSpec((8, HD), lambda i, c: (0, 0))],
        [STATES, STATES, shape((8, HD))],
        (core, scanned_back, Kept(moment_kept), Kept(moment_got), log_own,
         log_got, scanned_back), 0,
    )
    later_other = swap_cores(onward_back)
    later = {True: later_here, False: later_other}
    grads = ()
    for mine in (True, False):
        grads = call(
            finish_kernel, "finish", (NC // FH,),
            [fine(mine), fine(mine), row_block(mine), FINE_NARROW, FINE_NARROW,
             fine_block()] + [ANY] * len(grads),
            [fine(mine)] * 2, [Kept(WHOLE_BF16)] * 2,
            (core, Kept(k), Kept(v), row, Kept(key_inside[mine]), Kept(value_inside[mine]),
             later[mine], *[Kept(a) for a in grads]), 4 * MM, aliases={7: 0, 8: 1} if grads else None,
        )
    key_grad, value_grad = grads
    collected = (collected + swap_cores(collected))[0]
    at = lax.axis_index("y") * 32 + lax.axis_index("core") * 16
    positions = T * lax.axis_size(ALL)
    gain_grad = lax.dynamic_slice_in_dim(collected, at, 16) * (1.0 / math.sqrt(positions))
    return query_grad[0], key_grad, value_grad, gain_grad


def solution(mesh):
    fine = Mesh(mesh.devices.reshape(4, 2, 4, 4, 2), ALL)
    rows = P("dp", ("zh", "x", "y", "core"), None)
    return jax.shard_map(
        per_device,
        mesh=fine,
        in_specs=(rows,) * 5 + (P(),),
        out_specs=(rows, rows, rows, P(ALL)),
        check_vma=False,
    )
```

```python
import functools
import math

import jax
import jax.numpy as jnp
from jax import lax
from jax.experimental import pallas as pl
from jax.experimental.pallas import tpu as pltpu
from jax.sharding import Mesh, PartitionSpec as P

EPSILON = 1e-06
HIGHEST = lax.Precision.HIGHEST
F32 = jnp.float32
BF16 = jnp.bfloat16
T = 192
HD = 128
GH = 8
GW = GH * HD
NG = 4
HALF = NG // 2
NC = 16
ALL = ("dp", "zh", "x", "y", "core")


def dot(a, b, ca, cb):
    return lax.dot_general(a, b, (((ca,), (cb,)), ((), ())), preferred_element_type=F32)


def lanes(j):
    return slice(j * HD, (j + 1) * HD)


def split_state(state, axis):
    high = state.astype(BF16)
    low = (state - high.astype(F32)).astype(BF16)
    return jnp.concatenate([high, low], axis)


def rows_by_state(rows, state):
    return dot(jnp.concatenate([rows, rows], 1), split_state(state, 0), 1, 0)


def rows_by_state_t(rows, state):
    return dot(jnp.concatenate([rows, rows], 1), split_state(state, 1), 1, 1)


def columns(row_ref):
    return jnp.transpose(row_ref[...])


def decay_table(col, row):
    row_ids = lax.broadcasted_iota(jnp.int32, (T, T), 0)
    col_ids = lax.broadcasted_iota(jnp.int32, (T, T), 1)
    return jnp.exp(jnp.where(row_ids >= col_ids, col - row, -jnp.inf))


def scaled_columns(x, factors):
    return (jnp.transpose(x).astype(F32) * factors).astype(BF16)


def states_of(k_ref, v_ref, row_ref, store):
    rows = row_ref[...]
    last = rows[:, T - 1 : T]
    shrink = jnp.exp(last - rows)
    for j in range(GH):
        late = scaled_columns(k_ref[:, lanes(j)], shrink[j : j + 1, :])
        log = jnp.broadcast_to(last[j : j + 1, :], (8, HD))
        store(j, dot(late, v_ref[:, lanes(j)], 1, 0), log)


def state_first_kernel(c_ref, k_ref, v_ref, ld_ref, s_ref, row_ref):
    i = pl.program_id(0)

    @pl.when(i == 0)
    def _():
        upper = (
            lax.broadcasted_iota(jnp.int32, (T, T), 0) <= lax.broadcasted_iota(jnp.int32, (T, T), 1)
        ).astype(F32)
        logs = ld_ref[...]
        row_ref[...] = lax.dot_general(
            logs, upper, (((1,), (0,)), ((), ())), precision=HIGHEST, preferred_element_type=F32
        )

    def store(j, state, log):
        s_ref[j, :HD, :] = state
        s_ref[j, HD:, :] = log

    group = (1 - c_ref[0]) * HALF + i
    states_of(k_ref, v_ref, row_ref.at[pl.ds(pl.multiple_of(group * GH, GH), GH)], store)


def state_second_kernel(c_ref, k_ref, v_ref, row_ref, s_ref, l_ref):
    def store(j, state, log):
        s_ref[j] = state
        l_ref[j] = log

    states_of(k_ref, v_ref, row_ref, store)


def combine_kernel(upward, c_ref, own_ref, got_ref, lo_ref, lg_ref, p_ref, kept_ref, log_ref=None):
    first = c_ref[0] == 0 if upward else c_ref[0] == 1
    for j in range(GH):
        log_own, log_got = lo_ref[j, 0:1, :], lg_ref[j, 0:1, :]
        scale_own = jnp.where(first, jnp.exp(log_got), 1.0)
        scale_got = jnp.where(first, 1.0, jnp.exp(log_own))
        p_ref[j, :HD, :] = scale_own * own_ref[j] + scale_got * got_ref[j]
        kept_ref[j] = jnp.where(first, own_ref[j], got_ref[j])
        if upward:
            p_ref[j, HD:, :] = lo_ref[j] + lg_ref[j]
            log_ref[j] = lg_ref[j]


def total_kernel(upward, c_ref, m_ref, l_ref, *rest):
    run = jnp.zeros((HD, HD), F32)
    for i in range(NC) if upward else reversed(range(NC)):
        run = jnp.exp(l_ref[i, 0:1, :]) * run + m_ref[i]
    t_ref = rest[-1]
    t_ref[:HD, :] = run
    if not upward:
        t_ref[HD:, :] = rest[0][...]


def scan_kernel(upward, c_ref, m_ref, l_ref, t_ref, *rest):
    if upward:
        o_ref, log_ref = rest
        log_ref[...] = l_ref[...]
    else:
        gain_ref, o_ref = rest
        both = gain_ref[...] + t_ref[HD:, :]
    run = t_ref[:HD, :]
    run = jnp.where(c_ref[2] == (1 if upward else 0), run, 0.0)
    for i in range(NC) if upward else reversed(range(NC)):
        o_ref[i, :HD, :] = run
        run = jnp.exp(l_ref[i, 0:1, :]) * run + m_ref[i]
        if not upward:
            x = i // 4
            row = jnp.where(c_ref[2] == 0, both[x : x + 1, :], both[4 + x : 5 + x, :])
            o_ref[i, HD:, :] = jnp.broadcast_to(row, (8, HD))


def hand_on_kernel(upward, c_ref, d_ref, kept_ref, lo_ref, lg_ref, *rest):
    if upward:
        send_ref, state_ref = rest
    else:
        gains_ref, send_ref, state_ref, sum_ref = rest
        part = gains_ref[0]
        for j in range(1, GH):
            part += gains_ref[j]

        @pl.when(pl.program_id(0) == 0)
        def _():
            sum_ref[...] = part

        @pl.when(pl.program_id(0) > 0)
        def _():
            sum_ref[...] += part

    at_edge = c_ref[0] == (0 if upward else 1)
    for j in range(GH):
        edge = d_ref[j]
        passed = jnp.exp(jnp.where(at_edge, lo_ref[j, 0:1, :], lg_ref[j, 0:1, :])) * edge + kept_ref[j]
        send_ref[j] = jnp.where(at_edge, passed, edge)
        state_ref[j] = jnp.where(at_edge, edge, passed)


def forward_kernel(c_ref, q_ref, k_ref, v_ref, row_ref, fw_ref, in_ref):
    cum = columns(row_ref)
    for j in range(GH):
        decay = decay_table(cum[:, j : j + 1], row_ref[j : j + 1, :])
        scores = dot(q_ref[:, lanes(j)], k_ref[:, lanes(j)], 1, 1)
        weights = (scores * decay).astype(BF16)
        fw_ref[j] = weights
        in_ref[:, lanes(j)] = dot(weights, v_ref[:, lanes(j)], 1, 0)


def attend_group(q_ref, g_ref, gain_ref, cum, in_ref, x_ref, att_ref, sq_ref, pr_ref):
    growth = jnp.exp(cum)
    squares = jnp.zeros((T, HD), F32)
    products = jnp.zeros((T, HD), F32)
    for j in range(GH):
        att = in_ref[:, lanes(j)] + growth[:, j : j + 1] * rows_by_state(q_ref[:, lanes(j)], x_ref[j])
        att_ref[:, lanes(j)] = att
        squares += att * att
        products += att * (gain_ref[:, lanes(j)] * g_ref[:, lanes(j)].astype(F32))
    sq_ref[...] += squares
    pr_ref[...] += products


def attend_own_kernel(
    c_ref, q_ref, g_ref, gain_ref, row_ref, in_ref, x_ref, att_ref, sq_ref, pr_ref
):
    @pl.when(pl.program_id(0) == 0)
    def _():
        sq_ref[...] = jnp.zeros_like(sq_ref)
        pr_ref[...] = jnp.zeros_like(pr_ref)

    attend_group(
        q_ref, g_ref, gain_ref, columns(row_ref), in_ref, x_ref, att_ref, sq_ref, pr_ref
    )


def delta_group(q_ref, g_ref, gain_ref, row_ref, att_ref, inverse, mean, od_ref, m_ref, gt_ref):
    growth = jnp.exp(row_ref[...])
    for j in range(GH):
        grad = g_ref[:, lanes(j)].astype(F32)
        normed = att_ref[:, lanes(j)] * inverse
        delta = (inverse * (gain_ref[:, lanes(j)] * grad - normed * mean)).astype(BF16)
        od_ref[:, lanes(j)] = delta
        gt_ref[j : j + 1, :] = jnp.sum(grad * normed, axis=0, keepdims=True)
        early = scaled_columns(q_ref[:, lanes(j)], growth[j : j + 1, :])
        m_ref[j] = dot(early, delta, 1, 0)


def attend_other_kernel(
    c_ref, q_ref, g_ref, gain_ref, row_ref, in_ref, i_ref, sq_in, pr_in,
    od_ref, m_ref, gt_ref, inv_ref, mean_ref, att_ref, sq_ref, pr_ref,
):
    step = pl.program_id(0)
    group = jnp.where(step < HALF, step, 2 * HALF - 1 - step)

    @pl.when(step == 0)
    def _():
        sq_ref[...] = sq_in[...]
        pr_ref[...] = pr_in[...]

    @pl.when(step < HALF)
    def _():
        attend_group(
            q_ref, g_ref, gain_ref, columns(row_ref), in_ref, i_ref, att_ref.at[group], sq_ref, pr_ref
        )

    @pl.when(step == HALF)
    def _():
        features = NG * GW
        inverse = lax.rsqrt(jnp.sum(sq_ref[...], axis=1, keepdims=True) * (1.0 / features) + EPSILON)
        mean = inverse * (jnp.sum(pr_ref[...], axis=1, keepdims=True) * (1.0 / features))
        inv_ref[...] = jnp.broadcast_to(inverse, (T, HD))
        mean_ref[...] = jnp.broadcast_to(mean, (T, HD))

    @pl.when(step >= HALF)
    def _():
        delta_group(
            q_ref, g_ref, gain_ref, row_ref, att_ref.at[group], inv_ref[...], mean_ref[...],
            od_ref, m_ref, gt_ref,
        )


def delta_own_kernel(
    c_ref, q_ref, g_ref, gain_ref, row_ref, att_ref, inv_ref, mean_ref, od_ref, m_ref, gt_ref
):
    delta_group(
        q_ref, g_ref, gain_ref, row_ref, att_ref, inv_ref[...], mean_ref[...], od_ref, m_ref, gt_ref
    )


def backward_kernel(
    c_ref, od_ref, q_ref, k_ref, v_ref, fw_ref, row_ref, i_ref, *rest
):
    qg_ref, ki_ref, vi_ref = rest[-3:]
    cum = columns(row_ref)
    growth = jnp.exp(cum)
    for j in range(GH):
        at = lanes(j)
        decay = decay_table(cum[:, j : j + 1], row_ref[j : j + 1, :])
        delta = od_ref[:, at]
        weights = (dot(delta, v_ref[:, at], 1, 1) * decay).astype(BF16)
        inter = growth[:, j : j + 1] * rows_by_state_t(delta, i_ref[j])
        qg_ref[:, at] = (dot(weights, k_ref[:, at], 1, 0) + inter).astype(BF16)
        ki_ref[:, at] = dot(weights, q_ref[:, at], 0, 0)
        vi_ref[:, at] = dot(fw_ref[j], delta, 0, 0)


def finish_kernel(c_ref, k_ref, v_ref, row_ref, ki_ref, vi_ref, x_ref, *rest):
    cum = columns(row_ref)
    shrink = jnp.exp(cum[T - 1 : T, :] - cum)
    kg_ref, vg_ref = rest[-2:]
    for j in range(GH):
        at = lanes(j)
        scale = shrink[:, j : j + 1]
        kg_ref[:, at] = (ki_ref[:, at] + scale * rows_by_state_t(v_ref[:, at], x_ref[j])).astype(BF16)
        vg_ref[:, at] = (vi_ref[:, at] + scale * rows_by_state(k_ref[:, at], x_ref[j])).astype(BF16)


class Kept:
    def __init__(self, array):
        self.array = array
        self.shape, self.dtype = array.shape, array.dtype


def in_hbm(a):
    return pltpu.with_memory_space_constraint(a.array, pltpu.HBM) if isinstance(a, Kept) else a


def call(
    kernel, name, grid, in_specs, out_specs, out_shape, args, flops, scratch=(), aliases=None
):
    place, *args = args
    nbytes = sum(math.prod(a.shape) * a.dtype.itemsize for a in [*args, *out_shape])
    return pl.pallas_call(
        kernel,
        name=name,
        grid_spec=pltpu.PrefetchScalarGridSpec(
            num_scalar_prefetch=1,
            grid=grid,
            in_specs=in_specs,
            out_specs=out_specs,
            scratch_shapes=scratch,
        ),
        out_shape=[pltpu.HBM(s.shape, s.dtype) if isinstance(s, Kept) else s for s in out_shape],
        input_output_aliases=aliases or {},
        compiler_params=pltpu.CompilerParams(vmem_limit_bytes=16 << 20),
        cost_estimate=pl.CostEstimate(flops=flops, bytes_accessed=nbytes, transcendentals=0),
    )(place, *[in_hbm(a) for a in args])


def shape(dims, dtype=F32):
    return jax.ShapeDtypeStruct(dims, dtype)


def half_of(own, c_ref):
    return c_ref[0] if own else 1 - c_ref[0]


def wide(own, group=lambda i: i):
    return pl.BlockSpec((None, T, GW), lambda i, c: (0, 0, half_of(own, c) * HALF + group(i)))


def narrow(group=lambda i: i):
    return pl.BlockSpec((T, GW), lambda i, c: (0, group(i)))


def gain_block(own, group=lambda i: i):
    return pl.BlockSpec((1, GW), lambda i, c: (0, half_of(own, c) * HALF + group(i)))


def row_block(own, group=lambda i: i):
    return pl.BlockSpec((GH, T), lambda i, c: (half_of(own, c) * HALF + group(i), 0))


def gains_block(group=lambda i: i):
    return pl.BlockSpec((None, GH, HD), lambda i, c: (jnp.bitwise_xor(group(i), c[1] % 2), 0, 0))


def state_block(rows=HD, group=lambda i: i):
    return pl.BlockSpec((GH, rows, HD), lambda i, c: (group(i), 0, 0))


LOG_BLOCK = pl.BlockSpec((GH, 8, HD), lambda i, c: (i, 0, 0))
LOG_TAIL = pl.BlockSpec((GH, 8, HD), lambda i, c: (i, HD // 8, 0))
STAT_WHOLE = pl.BlockSpec((T, HD), lambda i, c: (0, 0))
ANY = pl.BlockSpec(memory_space=pl.ANY)
STATES = shape((NC, HD, HD))
LOGGED = shape((NC, HD + 8, HD))
LOGS = shape((NC, 8, HD))
HALF_F32 = shape((T, HALF * GW))
HALF_BF16 = shape((T, HALF * GW), BF16)
WHOLE_BF16 = shape((1, T, NG * GW), BF16)
STAT = shape((T, HD))
GAINS = shape((HALF, GH, HD))
MM = 2 * T * HD * HD * NC
SM = 2 * T * T * HD * NC


def swap_cores(values):
    return lax.ppermute(values, "core", [(0, 1), (1, 0)])


def chips_all_to_all(values):
    return lax.all_to_all(values, ("x", "y"), split_axis=0, concat_axis=0, tiled=True)


def scan_over_chips(upward, place, got, logs, gains=None):
    whole_m = pl.BlockSpec((NC, HD, HD), lambda i, c: (0, 0, 0))
    whole_l = pl.BlockSpec((NC, 8, HD), lambda i, c: (0, HD // 8 if upward else 0, 0))
    logs_out = pl.BlockSpec((NC, 8, HD), lambda i, c: (0, 0, 0))
    rows = HD if upward else HD + 8
    whole_t = pl.BlockSpec((rows, HD), lambda i, c: (0, 0))
    more = [] if upward else [gains]
    more_specs = [pl.BlockSpec((8, HD), lambda i, c: (0, 0))] * len(more)
    (total,) = call(
        functools.partial(total_kernel, upward), "half_total", (1,),
        [whole_m, whole_l] + more_specs, [whole_t], [shape((rows, HD))],
        (place, got, logs, *more), 0,
    )
    before = lax.ppermute(total, "zh", [(0, 1), (1, 0)])
    outs = [pl.BlockSpec((NC, rows, HD), lambda i, c: (0, 0, 0))] + [logs_out] * upward
    return call(
        functools.partial(scan_kernel, upward), "chip_scan", (1,),
        [whole_m, whole_l, whole_t] + more_specs, outs, [Kept(shape((NC, rows, HD))), LOGS][: len(outs)],
        (place, got, logs, before, *more), 0,
    )


def per_device(queries, key_rows, value_rows, out_grad, log_decay, norm_gain):
    core = jnp.stack([lax.axis_index(a).astype(jnp.int32) for a in ("core", "dp", "zh")])
    q, k, v, g = queries, key_rows, value_rows, out_grad
    gain = norm_gain.reshape(1, NG * GW)
    logs = jnp.transpose(log_decay[0])

    whole_rows = pl.BlockSpec((NG * GH, T), lambda i, c: (0, 0))
    sent, row = call(
        state_first_kernel, "states_other", (HALF,),
        [wide(False), wide(False), whole_rows], [state_block(HD + 8), whole_rows],
        [LOGGED, shape((NG * GH, T))], (core, Kept(k), Kept(v), Kept(logs)), MM,
    )
    got = swap_cores(sent)
    own, log_own = call(
        state_second_kernel, "states_own", (HALF,),
        [wide(True), wide(True), row_block(True)], [state_block(), LOG_BLOCK], [STATES, LOGS],
        (core, Kept(k), Kept(v), row), MM,
    )
    chip_total, kept_state, log_got = call(
        functools.partial(combine_kernel, True), "chip_total", (HALF,),
        [state_block(), state_block(), LOG_BLOCK, LOG_TAIL],
        [state_block(HD + 8), state_block(), LOG_BLOCK], [Kept(LOGGED), Kept(STATES), LOGS],
        (core, own, got, log_own, got), 0,
    )
    gathered = chips_all_to_all(chip_total)

    weights, inside = {}, {}
    for mine in (True, False):
        weights[mine], inside[mine] = call(
            forward_kernel, "forward_inside", (HALF,),
            [wide(mine), wide(mine), wide(mine), row_block(mine)],
            [pl.BlockSpec((GH, T, T), lambda i, c: (i, 0, 0)), narrow()],
            [Kept(shape((NC, T, T), BF16)), Kept(HALF_F32)],
            (core, Kept(q), Kept(k), Kept(v), row), 2 * SM,
        )

    gathered, inside[True], inside[False] = lax.optimization_barrier(
        (gathered, inside[True], inside[False])
    )
    before_chips, log_chips = scan_over_chips(True, core, gathered, gathered)
    scanned = chips_all_to_all(before_chips)
    onward, state_here = call(
        functools.partial(hand_on_kernel, True), "onward", (HALF,),
        [state_block()] * 2 + [LOG_BLOCK] * 2, [state_block()] * 2, [STATES] * 2,
        (core, scanned, kept_state, log_own, log_got), 0,
    )
    state_other = swap_cores(onward)
    att_own, squares, products = call(
        attend_own_kernel, "attend_own", (HALF,),
        [wide(True), wide(True), gain_block(True), row_block(True), narrow(), state_block()],
        [narrow(), STAT_WHOLE, STAT_WHOLE], [HALF_F32, STAT, STAT],
        (core, q, g, gain, row, inside[True], state_here), 2 * MM,
    )

    def turn(i):
        return jnp.where(i < HALF, i, 2 * HALF - 1 - i)

    def first(i):
        return jnp.minimum(i, HALF - 1)

    def second(i):
        return jnp.minimum(2 * HALF - 1 - i, HALF - 1)

    delta_other, moment_sent, gains_other, inverse, mean = call(
        attend_other_kernel, "attend_other", (2 * HALF,),
        [wide(False, turn), wide(False, turn), gain_block(False, turn), row_block(False, turn), narrow(first),
         state_block(HD, first), STAT_WHOLE, STAT_WHOLE],
        [narrow(second), state_block(HD, second), gains_block(second), STAT_WHOLE, STAT_WHOLE],
        [Kept(HALF_BF16), STATES, GAINS, STAT, STAT],
        (core, q, g, gain, row, inside[False], state_other, squares, products), 3 * MM,
        scratch=[pltpu.VMEM((HALF, T, GW), F32), pltpu.VMEM((T, HD), F32), pltpu.VMEM((T, HD), F32)],
    )
    moment_got = swap_cores(moment_sent)
    delta_own, moment_own, gains_own = call(
        delta_own_kernel, "delta_own", (HALF,),
        [wide(True), wide(True), gain_block(True), row_block(True), narrow(), STAT_WHOLE, STAT_WHOLE],
        [narrow(), state_block(), gains_block()], [Kept(HALF_BF16), STATES, GAINS],
        (core, q, g, gain, row, att_own, inverse, mean), MM,
    )
    chip_moment, kept_moment = call(
        functools.partial(combine_kernel, False), "chip_moment", (HALF,),
        [state_block(), state_block(), LOG_BLOCK, LOG_BLOCK], [state_block()] * 2, [Kept(STATES)] * 2,
        (core, moment_own, moment_got, log_own, log_got), 0,
    )
    gathered_back = chips_all_to_all(chip_moment)

    near = core[0] == core[1] // 2
    gains = [*jnp.where(near, gains_own, gains_other), *jnp.where(near, gains_other, gains_own)]
    collected = gains[0]
    for distance in range(1, NG):
        collected += lax.ppermute(gains[distance], "dp", [(i, i ^ distance) for i in range(NG)])

    delta = {True: delta_own, False: delta_other}
    state = {True: state_here, False: state_other}
    query_grad, key_inside, value_inside = (), {}, {}
    for mine in (True, False):
        *query_grad, key_inside[mine], value_inside[mine] = call(
            backward_kernel, "backward_inside", (HALF,),
            [narrow(), wide(mine), wide(mine), wide(mine),
             pl.BlockSpec((GH, T, T), lambda i, c: (i, 0, 0)), row_block(mine), state_block()]
            + [ANY] * len(query_grad),
            [wide(mine), narrow(), narrow()],
            [Kept(WHOLE_BF16), Kept(HALF_F32), Kept(HALF_F32)],
            (core, Kept(delta[mine]), Kept(q), Kept(k), Kept(v), Kept(weights[mine]), row, state[mine],
             *[Kept(a) for a in query_grad]),
            4 * SM + 2 * MM, aliases={8: 0} if query_grad else None,
        )

    gathered_back, key_inside[True] = lax.optimization_barrier((gathered_back, key_inside[True]))
    (after_chips,) = scan_over_chips(False, core, gathered_back, log_chips, collected)
    scanned_back = chips_all_to_all(after_chips)
    scanned_back, key_inside[False] = lax.optimization_barrier((scanned_back, key_inside[False]))
    onward_back, later_here, collected = call(
        functools.partial(hand_on_kernel, False), "onward_back", (HALF,),
        [state_block()] * 2 + [LOG_BLOCK] * 2 + [LOG_TAIL],
        [state_block(), state_block(), pl.BlockSpec((8, HD), lambda i, c: (0, 0))],
        [STATES, STATES, shape((8, HD))],
        (core, scanned_back, Kept(kept_moment), log_own, log_got, scanned_back), 0,
    )
    later_other = swap_cores(onward_back)
    later = {True: later_here, False: later_other}
    grads = ()
    for mine in (True, False):
        grads = call(
            finish_kernel, "finish", (HALF,),
            [wide(mine), wide(mine), row_block(mine), narrow(), narrow(), state_block()]
            + [ANY] * len(grads),
            [wide(mine)] * 2, [Kept(WHOLE_BF16)] * 2,
            (core, Kept(k), Kept(v), row, Kept(key_inside[mine]), Kept(value_inside[mine]),
             later[mine], *[Kept(a) for a in grads]), 4 * MM, aliases={7: 0, 8: 1} if grads else None,
        )
    key_grad, value_grad = grads
    collected = (collected + swap_cores(collected))[0]
    at = lax.axis_index("y") * 32 + lax.axis_index("core") * 16
    positions = T * lax.axis_size(ALL)
    gain_grad = lax.dynamic_slice_in_dim(collected, at, 16) * (1.0 / math.sqrt(positions))
    return query_grad[0], key_grad, value_grad, gain_grad


def solution(mesh):
    fine = Mesh(mesh.devices.reshape(4, 2, 4, 4, 2), ALL)
    rows = P("dp", ("zh", "x", "y", "core"), None)
    return jax.shard_map(
        per_device,
        mesh=fine,
        in_specs=(rows,) * 5 + (P(),),
        out_specs=(rows, rows, rows, P(ALL)),
        check_vma=False,
    )
```

```python
import functools
import math

import jax
import jax.numpy as jnp
from jax import lax
from jax.experimental import pallas as pl
from jax.experimental.pallas import tpu as pltpu
from jax.sharding import Mesh, PartitionSpec as P

EPSILON = 1e-06
HIGHEST = lax.Precision.HIGHEST
F32 = jnp.float32
BF16 = jnp.bfloat16
T = 192
HD = 128
GH = 8
GW = GH * HD
NG = 4
HALF = NG // 2
CH = 4
NC = 16
ALL = ("dp", "zh", "x", "y", "core")


def dot(a, b, ca, cb):
    return lax.dot_general(a, b, (((ca,), (cb,)), ((), ())), preferred_element_type=F32)


def lanes(j):
    return slice(j * HD, (j + 1) * HD)


def split_state(state, axis):
    high = state.astype(BF16)
    low = (state - high.astype(F32)).astype(BF16)
    return jnp.concatenate([high, low], axis)


def rows_by_state(rows, state):
    return dot(jnp.concatenate([rows, rows], 1), split_state(state, 0), 1, 0)


def rows_by_state_t(rows, state):
    return dot(jnp.concatenate([rows, rows], 1), split_state(state, 1), 1, 1)


def columns(row_ref):
    return jnp.transpose(row_ref[...])


def decay_table(col, row):
    row_ids = lax.broadcasted_iota(jnp.int32, (T, T), 0)
    col_ids = lax.broadcasted_iota(jnp.int32, (T, T), 1)
    return jnp.exp(jnp.where(row_ids >= col_ids, col - row, -jnp.inf))


def scaled_columns(x, factors):
    return (jnp.transpose(x).astype(F32) * factors).astype(BF16)


def states_of(k_ref, v_ref, row_ref, store):
    rows = row_ref[...]
    last = rows[:, T - 1 : T]
    shrink = jnp.exp(last - rows)
    for j in range(GH):
        late = scaled_columns(k_ref[:, lanes(j)], shrink[j : j + 1, :])
        log = jnp.broadcast_to(last[j : j + 1, :], (8, HD))
        store(j, dot(late, v_ref[:, lanes(j)], 1, 0), log)


def state_first_kernel(c_ref, k_ref, v_ref, ld_ref, s_ref, row_ref):
    i = pl.program_id(0)

    @pl.when(i == 0)
    def _():
        upper = (
            lax.broadcasted_iota(jnp.int32, (T, T), 0) <= lax.broadcasted_iota(jnp.int32, (T, T), 1)
        ).astype(F32)
        logs = ld_ref[...]
        row_ref[...] = lax.dot_general(
            logs, upper, (((1,), (0,)), ((), ())), precision=HIGHEST, preferred_element_type=F32
        )

    def store(j, state, log):
        s_ref[j, :HD, :] = state
        s_ref[j, HD:, :] = log

    group = (1 - c_ref[0]) * HALF + i
    states_of(k_ref, v_ref, row_ref.at[pl.ds(pl.multiple_of(group * GH, GH), GH)], store)


def state_second_kernel(c_ref, k_ref, v_ref, row_ref, s_ref, l_ref):
    def store(j, state, log):
        s_ref[j] = state
        l_ref[j] = log

    states_of(k_ref, v_ref, row_ref, store)


def combine_kernel(upward, c_ref, own_ref, got_ref, lo_ref, lg_ref, p_ref, kept_ref, log_ref=None):
    first = c_ref[0] == 0 if upward else c_ref[0] == 1
    for j in range(GH):
        log_own, log_got = lo_ref[j, 0:1, :], lg_ref[j, 0:1, :]
        scale_own = jnp.where(first, jnp.exp(log_got), 1.0)
        scale_got = jnp.where(first, 1.0, jnp.exp(log_own))
        p_ref[j, :HD, :] = scale_own * own_ref[j] + scale_got * got_ref[j]
        kept_ref[j] = jnp.where(first, own_ref[j], got_ref[j])
        if upward:
            p_ref[j, HD:, :] = lo_ref[j] + lg_ref[j]
            log_ref[j] = lg_ref[j]


def total_kernel(upward, c_ref, m_ref, l_ref, *rest):
    run = jnp.zeros((HD, HD), F32)
    for i in range(NC) if upward else reversed(range(NC)):
        run = jnp.exp(l_ref[i, 0:1, :]) * run + m_ref[i]
    t_ref = rest[-1]
    t_ref[:HD, :] = run
    if not upward:
        t_ref[HD:, :] = rest[0][...]


def scan_kernel(upward, c_ref, m_ref, l_ref, t_ref, *rest):
    if upward:
        o_ref, log_ref = rest
        log_ref[...] = l_ref[...]
    else:
        gain_ref, o_ref = rest
        both = gain_ref[...] + t_ref[HD:, :]
    run = t_ref[:HD, :]
    run = jnp.where(c_ref[2] == (1 if upward else 0), run, 0.0)
    for i in range(NC) if upward else reversed(range(NC)):
        o_ref[i, :HD, :] = run
        run = jnp.exp(l_ref[i, 0:1, :]) * run + m_ref[i]
        if not upward:
            x = i // 4
            row = jnp.where(c_ref[2] == 0, both[x : x + 1, :], both[4 + x : 5 + x, :])
            o_ref[i, HD:, :] = jnp.broadcast_to(row, (8, HD))


def hand_on_kernel(upward, c_ref, d_ref, kept_ref, lo_ref, lg_ref, *rest):
    if upward:
        send_ref, state_ref = rest
    else:
        gains_ref, send_ref, state_ref, sum_ref = rest
        part = gains_ref[0]
        for j in range(1, GH):
            part += gains_ref[j]

        @pl.when(pl.program_id(0) == 0)
        def _():
            sum_ref[...] = part

        @pl.when(pl.program_id(0) > 0)
        def _():
            sum_ref[...] += part

    at_edge = c_ref[0] == (0 if upward else 1)
    for j in range(GH):
        edge = d_ref[j]
        passed = jnp.exp(jnp.where(at_edge, lo_ref[j, 0:1, :], lg_ref[j, 0:1, :])) * edge + kept_ref[j]
        send_ref[j] = jnp.where(at_edge, passed, edge)
        state_ref[j] = jnp.where(at_edge, edge, passed)


def forward_kernel(c_ref, q_ref, k_ref, v_ref, row_ref, fw_ref, in_ref):
    cum = columns(row_ref)
    for j in range(GH):
        decay = decay_table(cum[:, j : j + 1], row_ref[j : j + 1, :])
        scores = dot(q_ref[:, lanes(j)], k_ref[:, lanes(j)], 1, 1)
        weights = (scores * decay).astype(BF16)
        fw_ref[j] = jnp.transpose(weights)
        in_ref[:, lanes(j)] = dot(weights, v_ref[:, lanes(j)], 1, 0)


def attend_group(q_ref, g_ref, gain_ref, cum, in_ref, x_ref, att_ref, sq_ref, pr_ref):
    growth = jnp.exp(cum)
    squares = jnp.zeros((T, HD), F32)
    products = jnp.zeros((T, HD), F32)
    for j in range(GH):
        att = in_ref[:, lanes(j)] + growth[:, j : j + 1] * rows_by_state(q_ref[:, lanes(j)], x_ref[j])
        att_ref[:, lanes(j)] = att
        squares += att * att
        products += att * (gain_ref[:, lanes(j)] * g_ref[:, lanes(j)].astype(F32))
    sq_ref[...] += squares
    pr_ref[...] += products


def attend_own_kernel(
    c_ref, q_ref, g_ref, gain_ref, row_ref, in_ref, x_ref, att_ref, sq_ref, pr_ref
):
    @pl.when(pl.program_id(0) == 0)
    def _():
        sq_ref[...] = jnp.zeros_like(sq_ref)
        pr_ref[...] = jnp.zeros_like(pr_ref)

    attend_group(
        q_ref, g_ref, gain_ref, columns(row_ref), in_ref, x_ref, att_ref, sq_ref, pr_ref
    )


def delta_group(q_ref, g_ref, gain_ref, row_ref, att_ref, inverse, mean, od_ref, m_ref, gt_ref):
    growth = jnp.exp(row_ref[...])
    for j in range(GH):
        grad = g_ref[:, lanes(j)].astype(F32)
        normed = att_ref[:, lanes(j)] * inverse
        delta = (inverse * (gain_ref[:, lanes(j)] * grad - normed * mean)).astype(BF16)
        od_ref[:, lanes(j)] = delta
        gt_ref[j : j + 1, :] = jnp.sum(grad * normed, axis=0, keepdims=True)
        early = scaled_columns(q_ref[:, lanes(j)], growth[j : j + 1, :])
        m_ref[j] = dot(early, delta, 1, 0)


def attend_other_kernel(
    c_ref, q_ref, g_ref, gain_ref, row_ref, in_ref, i_ref, sq_in, pr_in,
    od_ref, m_ref, gt_ref, inv_ref, mean_ref, att_ref, sq_ref, pr_ref,
):
    step = pl.program_id(0)
    group = jnp.where(step < HALF, step, 2 * HALF - 1 - step)

    @pl.when(step == 0)
    def _():
        sq_ref[...] = sq_in[...]
        pr_ref[...] = pr_in[...]

    @pl.when(step < HALF)
    def _():
        attend_group(
            q_ref, g_ref, gain_ref, columns(row_ref), in_ref, i_ref, att_ref.at[group], sq_ref, pr_ref
        )

    @pl.when(step == HALF)
    def _():
        features = NG * GW
        inverse = lax.rsqrt(jnp.sum(sq_ref[...], axis=1, keepdims=True) * (1.0 / features) + EPSILON)
        mean = inverse * (jnp.sum(pr_ref[...], axis=1, keepdims=True) * (1.0 / features))
        inv_ref[...] = jnp.broadcast_to(inverse, (T, HD))
        mean_ref[...] = jnp.broadcast_to(mean, (T, HD))

    @pl.when(step >= HALF)
    def _():
        delta_group(
            q_ref, g_ref, gain_ref, row_ref, att_ref.at[group], inv_ref[...], mean_ref[...],
            od_ref, m_ref, gt_ref,
        )


def delta_own_kernel(
    c_ref, q_ref, g_ref, gain_ref, row_ref, att_ref, inv_ref, mean_ref, od_ref, m_ref, gt_ref
):
    delta_group(
        q_ref, g_ref, gain_ref, row_ref, att_ref, inv_ref[...], mean_ref[...], od_ref, m_ref, gt_ref
    )


def backward_kernel(
    c_ref, od_ref, q_ref, k_ref, v_ref, fw_ref, row_ref, i_ref, *rest
):
    qg_ref, ki_ref, vi_ref = rest[-3:]
    cum = columns(row_ref)
    growth = jnp.exp(cum)
    for j in range(GH):
        at = lanes(j)
        decay = decay_table(cum[:, j : j + 1], row_ref[j : j + 1, :])
        delta = od_ref[:, at]
        weights = (dot(delta, v_ref[:, at], 1, 1) * decay).astype(BF16)
        inter = growth[:, j : j + 1] * rows_by_state_t(delta, i_ref[j])
        qg_ref[:, at] = (dot(weights, k_ref[:, at], 1, 0) + inter).astype(BF16)
        ki_ref[:, at] = dot(weights, q_ref[:, at], 0, 0)
        vi_ref[:, at] = dot(fw_ref[j], delta, 1, 0)


def finish_kernel(own, c_ref, row_ref, k_hbm, v_hbm, ki_hbm, vi_hbm, x_hbm, *rest):
    kg_hbm, vg_hbm, k_buf, v_buf, ki_buf, vi_buf, x_buf, kg_buf, vg_buf, in_sem, out_sem = rest[-11:]
    half = half_of(own, c_ref)
    pieces = NC // CH
    width = CH * HD

    def whole(n):
        return pl.ds(pl.multiple_of(half * (NC * HD) + n * width, width), width)

    def loads(n):
        part, heads = pl.ds(n * width, width), pl.ds(n * CH, CH)
        moves = [
            (x_hbm.at[heads], x_buf.at[heads]),
            (k_hbm.at[0, :, whole(n)], k_buf.at[:, part]),
            (v_hbm.at[0, :, whole(n)], v_buf.at[:, part]),
            (ki_hbm.at[:, part], ki_buf.at[:, part]),
            (vi_hbm.at[:, part], vi_buf.at[:, part]),
        ]
        return [pltpu.make_async_copy(a, b, in_sem.at[n, i]) for i, (a, b) in enumerate(moves)]

    def stores(n):
        part = pl.ds(n * width, width)
        moves = [(kg_buf.at[:, part], kg_hbm.at[0, :, whole(n)]), (vg_buf.at[:, part], vg_hbm.at[0, :, whole(n)])]
        return [pltpu.make_async_copy(a, b, out_sem.at[n, i]) for i, (a, b) in enumerate(moves)]

    for n in range(pieces):
        for copy in loads(n):
            copy.start()
    cum = jnp.transpose(row_ref[...])
    shrink = jnp.exp(cum[T - 1 : T, :] - cum)
    for n in range(pieces):
        for copy in loads(n):
            copy.wait()
        for j in range(n * CH, (n + 1) * CH):
            at = lanes(j)
            scale = shrink[:, j : j + 1]
            key_part = scale * rows_by_state_t(v_buf[:, at], x_buf[j])
            kg_buf[:, at] = (ki_buf[:, at] + key_part).astype(BF16)
            value_part = scale * rows_by_state(k_buf[:, at], x_buf[j])
            vg_buf[:, at] = (vi_buf[:, at] + value_part).astype(BF16)
        for copy in stores(n):
            copy.start()
    for n in range(pieces):
        for copy in stores(n):
            copy.wait()


class Kept:
    def __init__(self, array):
        self.array = array
        self.shape, self.dtype = array.shape, array.dtype


def in_hbm(a):
    return pltpu.with_memory_space_constraint(a.array, pltpu.HBM) if isinstance(a, Kept) else a


def call(
    kernel, name, grid, in_specs, out_specs, out_shape, args, flops, scratch=(), aliases=None
):
    place, *args = args
    nbytes = sum(math.prod(a.shape) * a.dtype.itemsize for a in [*args, *out_shape])
    return pl.pallas_call(
        kernel,
        name=name,
        grid_spec=pltpu.PrefetchScalarGridSpec(
            num_scalar_prefetch=1,
            grid=grid,
            in_specs=in_specs,
            out_specs=out_specs,
            scratch_shapes=scratch,
        ),
        out_shape=[pltpu.HBM(s.shape, s.dtype) if isinstance(s, Kept) else s for s in out_shape],
        input_output_aliases=aliases or {},
        compiler_params=pltpu.CompilerParams(vmem_limit_bytes=16 << 20),
        cost_estimate=pl.CostEstimate(flops=flops, bytes_accessed=nbytes, transcendentals=0),
    )(place, *[in_hbm(a) for a in args])


def shape(dims, dtype=F32):
    return jax.ShapeDtypeStruct(dims, dtype)


def half_of(own, c_ref):
    return c_ref[0] if own else 1 - c_ref[0]


def wide(own, group=lambda i: i):
    return pl.BlockSpec((None, T, GW), lambda i, c: (0, 0, half_of(own, c) * HALF + group(i)))


def narrow(group=lambda i: i):
    return pl.BlockSpec((T, GW), lambda i, c: (0, group(i)))


def gain_block(own, group=lambda i: i):
    return pl.BlockSpec((1, GW), lambda i, c: (0, half_of(own, c) * HALF + group(i)))


def row_block(own, group=lambda i: i):
    return pl.BlockSpec((GH, T), lambda i, c: (half_of(own, c) * HALF + group(i), 0))


def gains_block(group=lambda i: i):
    return pl.BlockSpec((None, GH, HD), lambda i, c: (jnp.bitwise_xor(group(i), c[1] % 2), 0, 0))


def state_block(rows=HD, group=lambda i: i):
    return pl.BlockSpec((GH, rows, HD), lambda i, c: (group(i), 0, 0))


LOG_BLOCK = pl.BlockSpec((GH, 8, HD), lambda i, c: (i, 0, 0))
LOG_TAIL = pl.BlockSpec((GH, 8, HD), lambda i, c: (i, HD // 8, 0))
STAT_WHOLE = pl.BlockSpec((T, HD), lambda i, c: (0, 0))
ANY = pl.BlockSpec(memory_space=pl.ANY)
STATES = shape((NC, HD, HD))
LOGGED = shape((NC, HD + 8, HD))
LOGS = shape((NC, 8, HD))
HALF_F32 = shape((T, HALF * GW))
HALF_BF16 = shape((T, HALF * GW), BF16)
WHOLE_BF16 = shape((1, T, NG * GW), BF16)
STAT = shape((T, HD))
GAINS = shape((HALF, GH, HD))
MM = 2 * T * HD * HD * NC
SM = 2 * T * T * HD * NC


def swap_cores(values):
    return lax.ppermute(values, "core", [(0, 1), (1, 0)])


def chips_all_to_all(values):
    return lax.all_to_all(values, ("x", "y"), split_axis=0, concat_axis=0, tiled=True)


def scan_over_chips(upward, place, got, logs, gains=None):
    whole_m = pl.BlockSpec((NC, HD, HD), lambda i, c: (0, 0, 0))
    whole_l = pl.BlockSpec((NC, 8, HD), lambda i, c: (0, HD // 8 if upward else 0, 0))
    logs_out = pl.BlockSpec((NC, 8, HD), lambda i, c: (0, 0, 0))
    rows = HD if upward else HD + 8
    whole_t = pl.BlockSpec((rows, HD), lambda i, c: (0, 0))
    more = [] if upward else [gains]
    more_specs = [pl.BlockSpec((8, HD), lambda i, c: (0, 0))] * len(more)
    (total,) = call(
        functools.partial(total_kernel, upward), "half_total", (1,),
        [whole_m, whole_l] + more_specs, [whole_t], [shape((rows, HD))],
        (place, got, logs, *more), 0,
    )
    before = lax.ppermute(total, "zh", [(0, 1), (1, 0)])
    outs = [pl.BlockSpec((NC, rows, HD), lambda i, c: (0, 0, 0))] + [logs_out] * upward
    return call(
        functools.partial(scan_kernel, upward), "chip_scan", (1,),
        [whole_m, whole_l, whole_t] + more_specs, outs, [Kept(shape((NC, rows, HD))), LOGS][: len(outs)],
        (place, got, logs, before, *more), 0,
    )


def per_device(queries, key_rows, value_rows, out_grad, log_decay, norm_gain):
    core = jnp.stack([lax.axis_index(a).astype(jnp.int32) for a in ("core", "dp", "zh")])
    q, k, v, g = queries, key_rows, value_rows, out_grad
    gain = norm_gain.reshape(1, NG * GW)
    logs = jnp.transpose(log_decay[0])

    whole_rows = pl.BlockSpec((NG * GH, T), lambda i, c: (0, 0))
    sent, row = call(
        state_first_kernel, "states_other", (HALF,),
        [wide(False), wide(False), whole_rows], [state_block(HD + 8), whole_rows],
        [LOGGED, shape((NG * GH, T))], (core, Kept(k), Kept(v), Kept(logs)), MM,
    )
    got = swap_cores(sent)
    own, log_own = call(
        state_second_kernel, "states_own", (HALF,),
        [wide(True), wide(True), row_block(True)], [state_block(), LOG_BLOCK], [STATES, LOGS],
        (core, Kept(k), Kept(v), row), MM,
    )
    chip_total, kept_state, log_got = call(
        functools.partial(combine_kernel, True), "chip_total", (HALF,),
        [state_block(), state_block(), LOG_BLOCK, LOG_TAIL],
        [state_block(HD + 8), state_block(), LOG_BLOCK], [Kept(LOGGED), Kept(STATES), LOGS],
        (core, own, got, log_own, got), 0,
    )
    gathered = chips_all_to_all(chip_total)

    weights, inside = {}, {}
    for mine in (True, False):
        weights[mine], inside[mine] = call(
            forward_kernel, "forward_inside", (HALF,),
            [wide(mine), wide(mine), wide(mine), row_block(mine)],
            [pl.BlockSpec((GH, T, T), lambda i, c: (i, 0, 0)), narrow()],
            [Kept(shape((NC, T, T), BF16)), Kept(HALF_F32)],
            (core, Kept(q), Kept(k), Kept(v), row), 2 * SM,
        )

    gathered, inside[True], inside[False] = lax.optimization_barrier(
        (gathered, inside[True], inside[False])
    )
    before_chips, log_chips = scan_over_chips(True, core, gathered, gathered)
    scanned = chips_all_to_all(before_chips)
    onward, state_here = call(
        functools.partial(hand_on_kernel, True), "onward", (HALF,),
        [state_block()] * 2 + [LOG_BLOCK] * 2, [state_block()] * 2, [STATES] * 2,
        (core, scanned, kept_state, log_own, log_got), 0,
    )
    state_other = swap_cores(onward)
    att_own, squares, products = call(
        attend_own_kernel, "attend_own", (HALF,),
        [wide(True), wide(True), gain_block(True), row_block(True), narrow(), state_block()],
        [narrow(), STAT_WHOLE, STAT_WHOLE], [HALF_F32, STAT, STAT],
        (core, q, g, gain, row, inside[True], state_here), 2 * MM,
    )

    def turn(i):
        return jnp.where(i < HALF, i, 2 * HALF - 1 - i)

    def first(i):
        return jnp.minimum(i, HALF - 1)

    def second(i):
        return jnp.minimum(2 * HALF - 1 - i, HALF - 1)

    delta_other, moment_sent, gains_other, inverse, mean = call(
        attend_other_kernel, "attend_other", (2 * HALF,),
        [wide(False, turn), wide(False, turn), gain_block(False, turn), row_block(False, turn), narrow(first),
         state_block(HD, first), STAT_WHOLE, STAT_WHOLE],
        [narrow(second), state_block(HD, second), gains_block(second), STAT_WHOLE, STAT_WHOLE],
        [Kept(HALF_BF16), STATES, GAINS, STAT, STAT],
        (core, q, g, gain, row, inside[False], state_other, squares, products), 3 * MM,
        scratch=[pltpu.VMEM((HALF, T, GW), F32), pltpu.VMEM((T, HD), F32), pltpu.VMEM((T, HD), F32)],
    )
    moment_got = swap_cores(moment_sent)
    delta_own, moment_own, gains_own = call(
        delta_own_kernel, "delta_own", (HALF,),
        [wide(True), wide(True), gain_block(True), row_block(True), narrow(), STAT_WHOLE, STAT_WHOLE],
        [narrow(), state_block(), gains_block()], [Kept(HALF_BF16), STATES, GAINS],
        (core, q, g, gain, row, att_own, inverse, mean), MM,
    )
    chip_moment, kept_moment = call(
        functools.partial(combine_kernel, False), "chip_moment", (HALF,),
        [state_block(), state_block(), LOG_BLOCK, LOG_BLOCK], [state_block()] * 2, [Kept(STATES)] * 2,
        (core, moment_own, moment_got, log_own, log_got), 0,
    )
    gathered_back = chips_all_to_all(chip_moment)

    near = core[0] == core[1] // 2
    gains = [*jnp.where(near, gains_own, gains_other), *jnp.where(near, gains_other, gains_own)]
    collected = gains[0]
    for distance in range(1, NG):
        collected += lax.ppermute(gains[distance], "dp", [(i, i ^ distance) for i in range(NG)])

    delta = {True: delta_own, False: delta_other}
    state = {True: state_here, False: state_other}
    query_grad, key_inside, value_inside = (), {}, {}
    for mine in (True, False):
        *query_grad, key_inside[mine], value_inside[mine] = call(
            backward_kernel, "backward_inside", (HALF,),
            [narrow(), wide(mine), wide(mine), wide(mine),
             pl.BlockSpec((GH, T, T), lambda i, c: (i, 0, 0)), row_block(mine), state_block()]
            + [ANY] * len(query_grad),
            [wide(mine), narrow(), narrow()],
            [Kept(WHOLE_BF16), Kept(HALF_F32), Kept(HALF_F32)],
            (core, Kept(delta[mine]), Kept(q), Kept(k), Kept(v), Kept(weights[mine]), row, state[mine],
             *[Kept(a) for a in query_grad]),
            4 * SM + 2 * MM, aliases={8: 0} if query_grad else None,
        )

    gathered_back, key_inside[True] = lax.optimization_barrier((gathered_back, key_inside[True]))
    (after_chips,) = scan_over_chips(False, core, gathered_back, log_chips, collected)
    scanned_back = chips_all_to_all(after_chips)
    scanned_back, key_inside[False] = lax.optimization_barrier((scanned_back, key_inside[False]))
    onward_back, later_here, collected = call(
        functools.partial(hand_on_kernel, False), "onward_back", (HALF,),
        [state_block()] * 2 + [LOG_BLOCK] * 2 + [LOG_TAIL],
        [state_block(), state_block(), pl.BlockSpec((8, HD), lambda i, c: (0, 0))],
        [STATES, Kept(STATES), shape((8, HD))],
        (core, scanned_back, kept_moment, log_own, log_got, scanned_back), 0,
    )
    later_other = swap_cores(onward_back)
    later = {True: later_here, False: later_other}
    grads = ()
    for mine in (True, False):
        grads = call(
            functools.partial(finish_kernel, mine), "finish", (1,),
            [pl.BlockSpec((NC, T), lambda i, c, mine=mine: (half_of(mine, c), 0))] + [ANY] * (5 + len(grads)),
            [ANY] * 2, [Kept(WHOLE_BF16)] * 2,
            (core, row, Kept(k), Kept(v), Kept(key_inside[mine]), Kept(value_inside[mine]),
             Kept(later[mine]) if mine else later[mine], *[Kept(a) for a in grads]), 4 * MM,
            scratch=[pltpu.VMEM((T, NC * HD), BF16)] * 2 + [pltpu.VMEM((T, NC * HD), F32)] * 2
            + [pltpu.VMEM((NC, HD, HD), F32)] + [pltpu.VMEM((T, NC * HD), BF16)] * 2
            + [pltpu.SemaphoreType.DMA((NC // CH, 5)), pltpu.SemaphoreType.DMA((NC // CH, 2))],
            aliases={7: 0, 8: 1} if grads else None,
        )
    key_grad, value_grad = grads
    collected = (collected + swap_cores(collected))[0]
    at = lax.axis_index("y") * 32 + lax.axis_index("core") * 16
    positions = T * lax.axis_size(ALL)
    gain_grad = lax.dynamic_slice_in_dim(collected, at, 16) * (1.0 / math.sqrt(positions))
    return query_grad[0], key_grad, value_grad, gain_grad


def solution(mesh):
    fine = Mesh(mesh.devices.reshape(4, 2, 4, 4, 2), ALL)
    rows = P("dp", ("zh", "x", "y", "core"), None)
    return jax.shard_map(
        per_device,
        mesh=fine,
        in_specs=(rows,) * 5 + (P(),),
        out_specs=(rows, rows, rows, P(ALL)),
        check_vma=False,
    )
```

```python
import functools
import math

import jax
import jax.numpy as jnp
from jax import lax
from jax.experimental import pallas as pl
from jax.experimental.pallas import tpu as pltpu
from jax.sharding import Mesh, PartitionSpec as P

EPSILON = 1e-06
HIGHEST = lax.Precision.HIGHEST
F32 = jnp.float32
BF16 = jnp.bfloat16
T = 192
HD = 128
GH = 8
GW = GH * HD
NG = 4
HALF = NG // 2
DEVICES = 256
NC = 16
ALL = ("dp", "zh", "x", "y", "core")


def dot(a, b, ca, cb):
    return lax.dot_general(a, b, (((ca,), (cb,)), ((), ())), preferred_element_type=F32)


def lanes(j):
    return slice(j * HD, (j + 1) * HD)


def split_state(state, axis):
    high = state.astype(BF16)
    low = (state - high.astype(F32)).astype(BF16)
    return jnp.concatenate([high, low], axis)


def rows_by_state(rows, state):
    return dot(jnp.concatenate([rows, rows], 1), split_state(state, 0), 1, 0)


def rows_by_state_t(rows, state):
    return dot(jnp.concatenate([rows, rows], 1), split_state(state, 1), 1, 1)


def columns(row_ref):
    return jnp.transpose(row_ref[...])


def decay_table(col, row):
    row_ids = lax.broadcasted_iota(jnp.int32, (T, T), 0)
    col_ids = lax.broadcasted_iota(jnp.int32, (T, T), 1)
    return jnp.exp(jnp.where(row_ids >= col_ids, col - row, -jnp.inf))


def scaled_columns(x, factors):
    return (jnp.transpose(x).astype(F32) * factors).astype(BF16)


def states_of(k_ref, v_ref, row_ref, store):
    rows = row_ref[...]
    last = rows[:, T - 1 : T]
    shrink = jnp.exp(last - rows)
    for j in range(GH):
        late = scaled_columns(k_ref[:, lanes(j)], shrink[j : j + 1, :])
        log = jnp.broadcast_to(last[j : j + 1, :], (8, HD))
        store(j, dot(late, v_ref[:, lanes(j)], 1, 0), log)


def state_first_kernel(c_ref, k_ref, v_ref, ld_ref, s_ref, row_ref):
    i = pl.program_id(0)

    @pl.when(i == 0)
    def _():
        upper = (
            lax.broadcasted_iota(jnp.int32, (T, T), 0) <= lax.broadcasted_iota(jnp.int32, (T, T), 1)
        ).astype(F32)
        logs = ld_ref[...]
        row_ref[...] = lax.dot_general(
            logs, upper, (((1,), (0,)), ((), ())), precision=HIGHEST, preferred_element_type=F32
        )

    def store(j, state, log):
        s_ref[j, :HD, :] = state
        s_ref[j, HD:, :] = log

    group = (1 - c_ref[0]) * HALF + i
    states_of(k_ref, v_ref, row_ref.at[pl.ds(pl.multiple_of(group * GH, GH), GH)], store)


def state_second_kernel(c_ref, k_ref, v_ref, row_ref, s_ref, l_ref):
    def store(j, state, log):
        s_ref[j] = state
        l_ref[j] = log

    states_of(k_ref, v_ref, row_ref, store)


def combine_kernel(upward, c_ref, own_ref, got_ref, lo_ref, lg_ref, p_ref, kept_ref, log_ref=None):
    first = c_ref[0] == 0 if upward else c_ref[0] == 1
    for j in range(GH):
        log_own, log_got = lo_ref[j, 0:1, :], lg_ref[j, 0:1, :]
        scale_own = jnp.where(first, jnp.exp(log_got), 1.0)
        scale_got = jnp.where(first, 1.0, jnp.exp(log_own))
        p_ref[j, :HD, :] = scale_own * own_ref[j] + scale_got * got_ref[j]
        kept_ref[j] = jnp.where(first, own_ref[j], got_ref[j])
        if upward:
            p_ref[j, HD:, :] = lo_ref[j] + lg_ref[j]
            log_ref[j] = lg_ref[j]


def total_kernel(upward, c_ref, m_ref, l_ref, *rest):
    run = jnp.zeros((HD, HD), F32)
    for i in range(NC) if upward else reversed(range(NC)):
        run = jnp.exp(l_ref[i, 0:1, :]) * run + m_ref[i]
    t_ref = rest[-1]
    t_ref[:HD, :] = run
    if not upward:
        t_ref[HD:, :] = rest[0][...]


def scan_kernel(upward, c_ref, m_ref, l_ref, t_ref, *rest):
    if upward:
        o_hbm, log_ref, o_buf, sem = rest
        log_ref[...] = l_ref[...]
    else:
        gain_ref, o_hbm, o_buf, sem = rest
        both = gain_ref[...] + t_ref[HD:, :]
    run = jnp.where(c_ref[2] == (1 if upward else 0), t_ref[:HD, :], 0.0)
    copies = [pltpu.make_async_copy(o_buf.at[i], o_hbm.at[i], sem.at[i]) for i in range(NC)]
    for i in range(NC) if upward else reversed(range(NC)):
        o_buf[i, :HD, :] = run
        if not upward:
            x = i // 4
            row = jnp.where(c_ref[2] == 0, both[x : x + 1, :], both[4 + x : 5 + x, :])
            o_buf[i, HD:, :] = jnp.broadcast_to(row, (8, HD))
        copies[i].start()
        run = jnp.exp(l_ref[i, 0:1, :]) * run + m_ref[i]
    for copy in copies:
        copy.wait()


def hand_on_kernel(upward, c_ref, d_ref, kept_ref, lo_ref, lg_ref, *rest):
    if upward:
        send_ref, state_ref = rest
    else:
        gains_ref, send_ref, state_ref, sum_ref = rest
        part = gains_ref[0]
        for j in range(1, GH):
            part += gains_ref[j]

        @pl.when(pl.program_id(0) == 0)
        def _():
            sum_ref[...] = part

        @pl.when(pl.program_id(0) > 0)
        def _():
            sum_ref[...] += part

    at_edge = c_ref[0] == (0 if upward else 1)
    for j in range(GH):
        edge = d_ref[j]
        passed = jnp.exp(jnp.where(at_edge, lo_ref[j, 0:1, :], lg_ref[j, 0:1, :])) * edge + kept_ref[j]
        send_ref[j] = jnp.where(at_edge, passed, edge)
        state_ref[j] = jnp.where(at_edge, edge, passed)


def forward_kernel(c_ref, q_ref, k_ref, v_ref, row_ref, fw_ref, in_ref):
    cum = columns(row_ref)
    for j in range(GH):
        decay = decay_table(cum[:, j : j + 1], row_ref[j : j + 1, :])
        scores = dot(q_ref[:, lanes(j)], k_ref[:, lanes(j)], 1, 1)
        weights = (scores * decay).astype(BF16)
        fw_ref[j] = jnp.transpose(weights)
        in_ref[:, lanes(j)] = dot(weights, v_ref[:, lanes(j)], 1, 0)


def attend_group(q_ref, g_ref, gain_ref, cum, in_ref, x_ref, att_ref, sq_ref, pr_ref):
    growth = jnp.exp(cum)
    squares = jnp.zeros((T, HD), F32)
    products = jnp.zeros((T, HD), F32)
    for j in range(GH):
        att = in_ref[:, lanes(j)] + growth[:, j : j + 1] * rows_by_state(q_ref[:, lanes(j)], x_ref[j])
        att_ref[:, lanes(j)] = att
        squares += att * att
        products += att * (gain_ref[:, lanes(j)] * g_ref[:, lanes(j)].astype(F32))
    sq_ref[...] += squares
    pr_ref[...] += products


def attend_own_kernel(
    c_ref, q_ref, g_ref, gain_ref, row_ref, in_ref, x_ref, att_ref, sq_ref, pr_ref
):
    @pl.when(pl.program_id(0) == 0)
    def _():
        sq_ref[...] = jnp.zeros_like(sq_ref)
        pr_ref[...] = jnp.zeros_like(pr_ref)

    attend_group(
        q_ref, g_ref, gain_ref, columns(row_ref), in_ref, x_ref, att_ref, sq_ref, pr_ref
    )


def delta_group(q_ref, g_ref, gain_ref, row_ref, att_ref, inverse, mean, od_ref, m_ref, gt_ref):
    growth = jnp.exp(row_ref[...])
    for j in range(GH):
        grad = g_ref[:, lanes(j)].astype(F32)
        normed = att_ref[:, lanes(j)] * inverse
        delta = (inverse * (gain_ref[:, lanes(j)] * grad - normed * mean)).astype(BF16)
        od_ref[:, lanes(j)] = delta
        gt_ref[j : j + 1, :] = jnp.sum(grad * normed, axis=0, keepdims=True)
        early = scaled_columns(q_ref[:, lanes(j)], growth[j : j + 1, :])
        m_ref[j] = dot(early, delta, 1, 0)


def attend_other_kernel(
    c_ref, q_ref, g_ref, gain_ref, row_ref, in_ref, i_ref, sq_in, pr_in,
    od_ref, m_ref, gt_ref, inv_ref, mean_ref, att_ref, sq_ref, pr_ref,
):
    step = pl.program_id(0)
    group = jnp.where(step < HALF, step, 2 * HALF - 1 - step)

    @pl.when(step == 0)
    def _():
        sq_ref[...] = sq_in[...]
        pr_ref[...] = pr_in[...]

    @pl.when(step < HALF)
    def _():
        attend_group(
            q_ref, g_ref, gain_ref, columns(row_ref), in_ref, i_ref, att_ref.at[group], sq_ref, pr_ref
        )

    @pl.when(step == HALF)
    def _():
        features = NG * GW
        inverse = lax.rsqrt(jnp.sum(sq_ref[...], axis=1, keepdims=True) * (1.0 / features) + EPSILON)
        mean = inverse * (jnp.sum(pr_ref[...], axis=1, keepdims=True) * (1.0 / features))
        inv_ref[...] = jnp.broadcast_to(inverse, (T, HD))
        mean_ref[...] = jnp.broadcast_to(mean, (T, HD))

    @pl.when(step >= HALF)
    def _():
        delta_group(
            q_ref, g_ref, gain_ref, row_ref, att_ref.at[group], inv_ref[...], mean_ref[...],
            od_ref, m_ref, gt_ref,
        )


def delta_own_kernel(
    c_ref, q_ref, g_ref, gain_ref, row_ref, att_ref, inv_ref, mean_ref, od_ref, m_ref, gt_ref
):
    delta_group(
        q_ref, g_ref, gain_ref, row_ref, att_ref, inv_ref[...], mean_ref[...], od_ref, m_ref, gt_ref
    )


def backward_kernel(
    c_ref, od_ref, q_ref, k_ref, v_ref, fw_ref, row_ref, i_ref, *rest
):
    qg_ref, ki_ref, vi_ref = rest[-3:]
    cum = columns(row_ref)
    growth = jnp.exp(cum)
    for j in range(GH):
        at = lanes(j)
        decay = decay_table(cum[:, j : j + 1], row_ref[j : j + 1, :])
        delta = od_ref[:, at]
        weights = (dot(delta, v_ref[:, at], 1, 1) * decay).astype(BF16)
        inter = growth[:, j : j + 1] * rows_by_state_t(delta, i_ref[j])
        qg_ref[:, at] = (dot(weights, k_ref[:, at], 1, 0) + inter).astype(BF16)
        ki_ref[:, at] = dot(weights, q_ref[:, at], 0, 0).astype(BF16)
        vi_ref[:, at] = dot(fw_ref[j], delta, 1, 0).astype(BF16)


def finish_kernel(own, c_ref, k_ref, v_ref, row_ref, ki_ref, vi_ref, x_ref, *rest):
    cum = columns(row_ref)
    shrink = jnp.exp(cum[T - 1 : T, :] - cum)
    if own:
        kg_ref, vg_ref = rest
    else:
        mine_ref, pair_ref, _, _, kg_ref, vg_ref, gain_ref = rest
        total = (mine_ref[...] + pair_ref[...]) * (1.0 / math.sqrt(T * DEVICES))
        at = c_ref[3] * 32 + c_ref[0] * 16
        gain_ref[...] = pltpu.roll(total, lax.rem(HD - at, HD), 1)[0:1, :16]
    for j in range(GH):
        at = lanes(j)
        scale = shrink[:, j : j + 1]
        kg_ref[:, at] = (ki_ref[:, at].astype(F32) + scale * rows_by_state_t(v_ref[:, at], x_ref[j])).astype(BF16)
        vg_ref[:, at] = (vi_ref[:, at].astype(F32) + scale * rows_by_state(k_ref[:, at], x_ref[j])).astype(BF16)


class Kept:
    def __init__(self, array):
        self.array = array
        self.shape, self.dtype = array.shape, array.dtype


def in_hbm(a):
    return pltpu.with_memory_space_constraint(a.array, pltpu.HBM) if isinstance(a, Kept) else a


def call(
    kernel, name, grid, in_specs, out_specs, out_shape, args, flops, scratch=(), aliases=None
):
    place, *args = args
    nbytes = sum(math.prod(a.shape) * a.dtype.itemsize for a in [*args, *out_shape])
    return pl.pallas_call(
        kernel,
        name=name,
        grid_spec=pltpu.PrefetchScalarGridSpec(
            num_scalar_prefetch=1,
            grid=grid,
            in_specs=in_specs,
            out_specs=out_specs,
            scratch_shapes=scratch,
        ),
        out_shape=[pltpu.HBM(s.shape, s.dtype) if isinstance(s, Kept) else s for s in out_shape],
        input_output_aliases=aliases or {},
        compiler_params=pltpu.CompilerParams(vmem_limit_bytes=16 << 20),
        cost_estimate=pl.CostEstimate(flops=flops, bytes_accessed=nbytes, transcendentals=0),
    )(place, *[in_hbm(a) for a in args])


def shape(dims, dtype=F32):
    return jax.ShapeDtypeStruct(dims, dtype)


def half_of(own, c_ref):
    return c_ref[0] if own else 1 - c_ref[0]


def wide(own, group=lambda i: i):
    return pl.BlockSpec((None, T, GW), lambda i, c: (0, 0, half_of(own, c) * HALF + group(i)))


def narrow(group=lambda i: i):
    return pl.BlockSpec((T, GW), lambda i, c: (0, group(i)))


def gain_block(own, group=lambda i: i):
    return pl.BlockSpec((1, GW), lambda i, c: (0, half_of(own, c) * HALF + group(i)))


def row_block(own, group=lambda i: i):
    return pl.BlockSpec((GH, T), lambda i, c: (half_of(own, c) * HALF + group(i), 0))


def gains_block(group=lambda i: i):
    return pl.BlockSpec((None, GH, HD), lambda i, c: (jnp.bitwise_xor(group(i), c[1] % 2), 0, 0))


def state_block(rows=HD, group=lambda i: i):
    return pl.BlockSpec((GH, rows, HD), lambda i, c: (group(i), 0, 0))


LOG_BLOCK = pl.BlockSpec((GH, 8, HD), lambda i, c: (i, 0, 0))
LOG_TAIL = pl.BlockSpec((GH, 8, HD), lambda i, c: (i, HD // 8, 0))
STAT_WHOLE = pl.BlockSpec((T, HD), lambda i, c: (0, 0))
ANY = pl.BlockSpec(memory_space=pl.ANY)
STATES = shape((NC, HD, HD))
LOGGED = shape((NC, HD + 8, HD))
LOGS = shape((NC, 8, HD))
HALF_F32 = shape((T, HALF * GW))
HALF_BF16 = shape((T, HALF * GW), BF16)
WHOLE_BF16 = shape((1, T, NG * GW), BF16)
STAT = shape((T, HD))
GAINS = shape((HALF, GH, HD))
MM = 2 * T * HD * HD * NC
SM = 2 * T * T * HD * NC


def swap_cores(values):
    return lax.ppermute(values, "core", [(0, 1), (1, 0)])


def chips_all_to_all(values):
    return lax.all_to_all(values, ("x", "y"), split_axis=0, concat_axis=0, tiled=True)


def scan_over_chips(upward, place, got, logs, gains=None):
    whole_m = pl.BlockSpec((NC, HD, HD), lambda i, c: (0, 0, 0))
    whole_l = pl.BlockSpec((NC, 8, HD), lambda i, c: (0, HD // 8 if upward else 0, 0))
    logs_out = pl.BlockSpec((NC, 8, HD), lambda i, c: (0, 0, 0))
    rows = HD if upward else HD + 8
    whole_t = pl.BlockSpec((rows, HD), lambda i, c: (0, 0))
    more = [] if upward else [gains]
    more_specs = [pl.BlockSpec((8, HD), lambda i, c: (0, 0))] * len(more)
    (total,) = call(
        functools.partial(total_kernel, upward), "half_total", (1,),
        [whole_m, whole_l] + more_specs, [whole_t], [shape((rows, HD))],
        (place, got, logs, *more), 0,
    )
    before = lax.ppermute(total, "zh", [(0, 1), (1, 0)])
    outs = [ANY] + [logs_out] * upward
    return call(
        functools.partial(scan_kernel, upward), "chip_scan", (1,),
        [whole_m, whole_l, whole_t] + more_specs, outs, [Kept(shape((NC, rows, HD))), LOGS][: len(outs)],
        (place, got, logs, before, *more), 0,
        scratch=[pltpu.VMEM((NC, rows, HD), F32), pltpu.SemaphoreType.DMA((NC,))],
    )


def per_device(queries, key_rows, value_rows, out_grad, log_decay, norm_gain):
    core = jnp.stack([lax.axis_index(a).astype(jnp.int32) for a in ("core", "dp", "zh", "y")])
    q, k, v, g = queries, key_rows, value_rows, out_grad
    gain = norm_gain.reshape(1, NG * GW)
    logs = jnp.transpose(log_decay[0])

    whole_rows = pl.BlockSpec((NG * GH, T), lambda i, c: (0, 0))
    sent, row = call(
        state_first_kernel, "states_other", (HALF,),
        [wide(False), wide(False), whole_rows], [state_block(HD + 8), whole_rows],
        [LOGGED, shape((NG * GH, T))], (core, Kept(k), Kept(v), Kept(logs)), MM,
    )
    got = swap_cores(sent)
    own, log_own = call(
        state_second_kernel, "states_own", (HALF,),
        [wide(True), wide(True), row_block(True)], [state_block(), LOG_BLOCK], [STATES, LOGS],
        (core, Kept(k), Kept(v), row), MM,
    )
    chip_total, kept_state, log_got = call(
        functools.partial(combine_kernel, True), "chip_total", (HALF,),
        [state_block(), state_block(), LOG_BLOCK, LOG_TAIL],
        [state_block(HD + 8), state_block(), LOG_BLOCK], [Kept(LOGGED), Kept(STATES), LOGS],
        (core, own, got, log_own, got), 0,
    )
    gathered = chips_all_to_all(chip_total)

    weights, inside = {}, {}
    for mine in (True, False):
        weights[mine], inside[mine] = call(
            forward_kernel, "forward_inside", (HALF,),
            [wide(mine), wide(mine), wide(mine), row_block(mine)],
            [pl.BlockSpec((GH, T, T), lambda i, c: (i, 0, 0)), narrow()],
            [Kept(shape((NC, T, T), BF16)), Kept(HALF_F32)],
            (core, Kept(q), Kept(k), Kept(v), row), 2 * SM,
        )

    gathered, inside[True], inside[False] = lax.optimization_barrier(
        (gathered, inside[True], inside[False])
    )
    before_chips, log_chips = scan_over_chips(True, core, gathered, gathered)
    scanned = chips_all_to_all(before_chips)
    onward, state_here = call(
        functools.partial(hand_on_kernel, True), "onward", (HALF,),
        [state_block()] * 2 + [LOG_BLOCK] * 2, [state_block()] * 2, [STATES] * 2,
        (core, scanned, kept_state, log_own, log_got), 0,
    )
    state_other = swap_cores(onward)
    att_own, squares, products = call(
        attend_own_kernel, "attend_own", (HALF,),
        [wide(True), wide(True), gain_block(True), row_block(True), narrow(), state_block()],
        [narrow(), STAT_WHOLE, STAT_WHOLE], [HALF_F32, STAT, STAT],
        (core, q, g, gain, row, inside[True], state_here), 2 * MM,
    )

    def turn(i):
        return jnp.where(i < HALF, i, 2 * HALF - 1 - i)

    def first(i):
        return jnp.minimum(i, HALF - 1)

    def second(i):
        return jnp.minimum(2 * HALF - 1 - i, HALF - 1)

    delta_other, moment_sent, gains_other, inverse, mean = call(
        attend_other_kernel, "attend_other", (2 * HALF,),
        [wide(False, turn), wide(False, turn), gain_block(False, turn), row_block(False, turn), narrow(first),
         state_block(HD, first), STAT_WHOLE, STAT_WHOLE],
        [narrow(second), state_block(HD, second), gains_block(second), STAT_WHOLE, STAT_WHOLE],
        [Kept(HALF_BF16), STATES, GAINS, STAT, STAT],
        (core, q, g, gain, row, inside[False], state_other, squares, products), 3 * MM,
        scratch=[pltpu.VMEM((HALF, T, GW), F32), pltpu.VMEM((T, HD), F32), pltpu.VMEM((T, HD), F32)],
    )
    moment_got = swap_cores(moment_sent)
    delta_own, moment_own, gains_own = call(
        delta_own_kernel, "delta_own", (HALF,),
        [wide(True), wide(True), gain_block(True), row_block(True), narrow(), STAT_WHOLE, STAT_WHOLE],
        [narrow(), state_block(), gains_block()], [Kept(HALF_BF16), STATES, GAINS],
        (core, q, g, gain, row, att_own, inverse, mean), MM,
    )
    chip_moment, kept_moment = call(
        functools.partial(combine_kernel, False), "chip_moment", (HALF,),
        [state_block(), state_block(), LOG_BLOCK, LOG_BLOCK], [state_block()] * 2, [Kept(STATES)] * 2,
        (core, moment_own, moment_got, log_own, log_got), 0,
    )
    gathered_back = chips_all_to_all(chip_moment)

    near = core[0] == core[1] // 2
    gains = [*jnp.where(near, gains_own, gains_other), *jnp.where(near, gains_other, gains_own)]
    collected = gains[0]
    for distance in range(1, NG):
        collected += lax.ppermute(gains[distance], "dp", [(i, i ^ distance) for i in range(NG)])

    delta = {True: delta_own, False: delta_other}
    state = {True: Kept(state_here), False: state_other}
    query_grad, key_inside, value_inside = (), {}, {}
    for mine in (True, False):
        *query_grad, key_inside[mine], value_inside[mine] = call(
            backward_kernel, "backward_inside", (HALF,),
            [narrow(), wide(mine), wide(mine), wide(mine),
             pl.BlockSpec((GH, T, T), lambda i, c: (i, 0, 0)), row_block(mine), state_block()]
            + [ANY] * len(query_grad),
            [wide(mine), narrow(), narrow()],
            [Kept(WHOLE_BF16), Kept(HALF_BF16), Kept(HALF_BF16)],
            (core, Kept(delta[mine]), Kept(q), Kept(k), Kept(v), Kept(weights[mine]), row, state[mine],
             *[Kept(a) for a in query_grad]),
            4 * SM + 2 * MM, aliases={8: 0} if query_grad else None,
        )

    gathered_back, key_inside[True] = lax.optimization_barrier((gathered_back, key_inside[True]))
    (after_chips,) = scan_over_chips(False, core, gathered_back, log_chips, collected)
    scanned_back = chips_all_to_all(after_chips)
    scanned_back, key_inside[False] = lax.optimization_barrier((scanned_back, key_inside[False]))
    onward_back, later_here, collected = call(
        functools.partial(hand_on_kernel, False), "onward_back", (HALF,),
        [state_block()] * 2 + [LOG_BLOCK] * 2 + [LOG_TAIL],
        [state_block(), state_block(), pl.BlockSpec((8, HD), lambda i, c: (0, 0))],
        [STATES, STATES, shape((8, HD))],
        (core, scanned_back, Kept(kept_moment), log_own, log_got, scanned_back), 0,
    )
    later_other = swap_cores(onward_back)
    pair = swap_cores(collected)
    inputs = [[wide(mine), wide(mine), row_block(mine), narrow(), narrow(), state_block()] for mine in (True, False)]
    small = pl.BlockSpec((8, HD), lambda i, c: (0, 0))
    grads = call(
        functools.partial(finish_kernel, True), "finish_own", (HALF,),
        inputs[0], [wide(True)] * 2, [Kept(WHOLE_BF16)] * 2,
        (core, Kept(k), Kept(v), row, Kept(key_inside[True]), Kept(value_inside[True]), later_here), 4 * MM,
    )
    key_grad, value_grad, gain_grad = call(
        functools.partial(finish_kernel, False), "finish_other", (HALF,),
        inputs[1] + [small, small, ANY, ANY],
        [wide(False)] * 2 + [pl.BlockSpec((1, 16), lambda i, c: (0, 0))],
        [Kept(WHOLE_BF16)] * 2 + [Kept(shape((1, 16)))],
        (core, Kept(k), Kept(v), row, Kept(key_inside[False]), Kept(value_inside[False]), later_other,
         collected, pair, *[Kept(a) for a in grads]), 4 * MM, aliases={9: 0, 10: 1},
    )
    return query_grad[0], key_grad, value_grad, gain_grad.reshape(16)


def solution(mesh):
    fine = Mesh(mesh.devices.reshape(4, 2, 4, 4, 2), ALL)
    rows = P("dp", ("zh", "x", "y", "core"), None)
    return jax.shard_map(
        per_device,
        mesh=fine,
        in_specs=(rows,) * 5 + (P(),),
        out_specs=(rows, rows, rows, P(ALL)),
        check_vma=False,
    )
```

```python
import functools
import math

import jax
import jax.numpy as jnp
from jax import lax
from jax.experimental import pallas as pl
from jax.experimental.pallas import tpu as pltpu
from jax.sharding import Mesh, PartitionSpec as P

EPSILON = 1e-06
HIGHEST = lax.Precision.HIGHEST
F32 = jnp.float32
BF16 = jnp.bfloat16
T = 192
HD = 128
GH = 8
GW = GH * HD
NG = 4
HALF = NG // 2
DEVICES = 256
NC = 16
ALL = ("dp", "zh", "x", "y", "core")


def dot(a, b, ca, cb):
    return lax.dot_general(a, b, (((ca,), (cb,)), ((), ())), preferred_element_type=F32)


def lanes(j):
    return slice(j * HD, (j + 1) * HD)


def split_state(state, axis):
    high = state.astype(BF16)
    low = (state - high.astype(F32)).astype(BF16)
    return jnp.concatenate([high, low], axis)


def rows_by_state(rows, state):
    return dot(jnp.concatenate([rows, rows], 1), split_state(state, 0), 1, 0)


def rows_by_state_t(rows, state):
    return dot(jnp.concatenate([rows, rows], 1), split_state(state, 1), 1, 1)


def columns(row_ref):
    return jnp.transpose(row_ref[...])


def decay_table(col, row):
    row_ids = lax.broadcasted_iota(jnp.int32, (T, T), 0)
    col_ids = lax.broadcasted_iota(jnp.int32, (T, T), 1)
    return jnp.exp(jnp.where(row_ids >= col_ids, col - row, -jnp.inf))


def scaled_columns(x, factors):
    return (jnp.transpose(x).astype(F32) * factors).astype(BF16)


def states_of(k_ref, v_ref, row_ref, store):
    rows = row_ref[...]
    last = rows[:, T - 1 : T]
    shrink = jnp.exp(last - rows)
    for j in range(GH):
        late = scaled_columns(k_ref[:, lanes(j)], shrink[j : j + 1, :])
        log = jnp.broadcast_to(last[j : j + 1, :], (8, HD))
        store(j, dot(late, v_ref[:, lanes(j)], 1, 0), log)


def state_first_kernel(c_ref, k_ref, v_ref, ld_ref, s_ref, row_ref):
    i = pl.program_id(0)

    @pl.when(i == 0)
    def _():
        upper = (
            lax.broadcasted_iota(jnp.int32, (T, T), 0) <= lax.broadcasted_iota(jnp.int32, (T, T), 1)
        ).astype(F32)
        logs = ld_ref[...]
        row_ref[...] = lax.dot_general(
            logs, upper, (((1,), (0,)), ((), ())), precision=HIGHEST, preferred_element_type=F32
        )

    def store(j, state, log):
        s_ref[j, :HD, :] = state
        s_ref[j, HD:, :] = log

    group = (1 - c_ref[0]) * HALF + i
    states_of(k_ref, v_ref, row_ref.at[pl.ds(pl.multiple_of(group * GH, GH), GH)], store)


def state_second_kernel(c_ref, k_ref, v_ref, row_ref, s_ref, l_ref):
    def store(j, state, log):
        s_ref[j] = state
        l_ref[j] = log

    states_of(k_ref, v_ref, row_ref, store)


def combine_kernel(upward, c_ref, own_ref, got_ref, lo_ref, lg_ref, p_ref, kept_ref, log_ref=None):
    first = c_ref[0] == 0 if upward else c_ref[0] == 1
    for j in range(GH):
        log_own, log_got = lo_ref[j, 0:1, :], lg_ref[j, 0:1, :]
        scale_own = jnp.where(first, jnp.exp(log_got), 1.0)
        scale_got = jnp.where(first, 1.0, jnp.exp(log_own))
        p_ref[j, :HD, :] = scale_own * own_ref[j] + scale_got * got_ref[j]
        kept_ref[j] = jnp.where(first, own_ref[j], got_ref[j])
        if upward:
            p_ref[j, HD:, :] = lo_ref[j] + lg_ref[j]
            log_ref[j] = lg_ref[j]


def total_kernel(upward, c_ref, m_ref, l_ref, *rest):
    run = jnp.zeros((HD, HD), F32)
    for i in range(NC) if upward else reversed(range(NC)):
        run = jnp.exp(l_ref[i, 0:1, :]) * run + m_ref[i]
    t_ref = rest[-1]
    t_ref[:HD, :] = run
    if not upward:
        t_ref[HD:, :] = rest[0][...]


def scan_kernel(upward, c_ref, m_ref, l_ref, t_ref, *rest):
    if upward:
        o_hbm, log_ref, o_buf, sem = rest
        log_ref[...] = l_ref[...]
    else:
        gain_ref, o_hbm, o_buf, sem = rest
        both = gain_ref[...] + t_ref[HD:, :]
    run = jnp.where(c_ref[2] == (1 if upward else 0), t_ref[:HD, :], 0.0)
    copies = [pltpu.make_async_copy(o_buf.at[i], o_hbm.at[i], sem.at[i]) for i in range(NC)]
    for i in range(NC) if upward else reversed(range(NC)):
        o_buf[i, :HD, :] = run
        if not upward:
            x = i // 4
            row = jnp.where(c_ref[2] == 0, both[x : x + 1, :], both[4 + x : 5 + x, :])
            o_buf[i, HD:, :] = jnp.broadcast_to(row, (8, HD))
        copies[i].start()
        run = jnp.exp(l_ref[i, 0:1, :]) * run + m_ref[i]
    for copy in copies:
        copy.wait()


def hand_on_kernel(upward, c_ref, d_ref, kept_ref, lo_ref, lg_ref, *rest):
    if upward:
        send_ref, state_ref = rest
    else:
        gains_ref, send_ref, state_ref, sum_ref = rest
        part = gains_ref[0]
        for j in range(1, GH):
            part += gains_ref[j]

        @pl.when(pl.program_id(0) == 0)
        def _():
            sum_ref[...] = part

        @pl.when(pl.program_id(0) > 0)
        def _():
            sum_ref[...] += part

    at_edge = c_ref[0] == (0 if upward else 1)
    for j in range(GH):
        edge = d_ref[j]
        passed = jnp.exp(jnp.where(at_edge, lo_ref[j, 0:1, :], lg_ref[j, 0:1, :])) * edge + kept_ref[j]
        send_ref[j] = jnp.where(at_edge, passed, edge)
        state_ref[j] = jnp.where(at_edge, edge, passed)


def forward_kernel(c_ref, q_ref, k_ref, v_ref, row_ref, *rest):
    fw_ref, in_ref = rest[-2:]
    if len(rest) > 2:
        rest[1][...] = rest[0][...]
    cum = columns(row_ref)
    for j in range(GH):
        decay = decay_table(cum[:, j : j + 1], row_ref[j : j + 1, :])
        scores = dot(q_ref[:, lanes(j)], k_ref[:, lanes(j)], 1, 1)
        weights = (scores * decay).astype(BF16)
        fw_ref[j] = jnp.transpose(weights)
        in_ref[:, lanes(j)] = dot(weights, v_ref[:, lanes(j)], 1, 0)


def attend_group(q_ref, g_ref, gain_ref, cum, in_ref, x_ref, att_ref, sq_ref, pr_ref):
    growth = jnp.exp(cum)
    squares = jnp.zeros((T, HD), F32)
    products = jnp.zeros((T, HD), F32)
    for j in range(GH):
        att = in_ref[:, lanes(j)] + growth[:, j : j + 1] * rows_by_state(q_ref[:, lanes(j)], x_ref[j])
        att_ref[:, lanes(j)] = att
        squares += att * att
        products += att * (gain_ref[:, lanes(j)] * g_ref[:, lanes(j)].astype(F32))
    sq_ref[...] += squares
    pr_ref[...] += products


def attend_own_kernel(
    c_ref, q_ref, g_ref, gain_ref, row_ref, in_ref, x_ref, att_ref, sq_ref, pr_ref
):
    @pl.when(pl.program_id(0) == 0)
    def _():
        sq_ref[...] = jnp.zeros_like(sq_ref)
        pr_ref[...] = jnp.zeros_like(pr_ref)

    attend_group(
        q_ref, g_ref, gain_ref, columns(row_ref), in_ref, x_ref, att_ref, sq_ref, pr_ref
    )


def delta_group(q_ref, g_ref, gain_ref, row_ref, att_ref, inverse, mean, od_ref, m_ref, gt_ref):
    growth = jnp.exp(row_ref[...])
    for j in range(GH):
        grad = g_ref[:, lanes(j)].astype(F32)
        normed = att_ref[:, lanes(j)] * inverse
        delta = (inverse * (gain_ref[:, lanes(j)] * grad - normed * mean)).astype(BF16)
        od_ref[:, lanes(j)] = delta
        gt_ref[j : j + 1, :] = jnp.sum(grad * normed, axis=0, keepdims=True)
        early = scaled_columns(q_ref[:, lanes(j)], growth[j : j + 1, :])
        m_ref[j] = dot(early, delta, 1, 0)


def attend_other_kernel(
    c_ref, q_ref, g_ref, gain_ref, row_ref, in_ref, i_ref, sq_in, pr_in,
    od_ref, m_ref, gt_ref, inv_ref, mean_ref, att_ref, sq_ref, pr_ref,
):
    step = pl.program_id(0)
    group = jnp.where(step < HALF, step, 2 * HALF - 1 - step)

    @pl.when(step == 0)
    def _():
        sq_ref[...] = sq_in[...]
        pr_ref[...] = pr_in[...]

    @pl.when(step < HALF)
    def _():
        attend_group(
            q_ref, g_ref, gain_ref, columns(row_ref), in_ref, i_ref, att_ref.at[group], sq_ref, pr_ref
        )

    @pl.when(step == HALF)
    def _():
        features = NG * GW
        inverse = lax.rsqrt(jnp.sum(sq_ref[...], axis=1, keepdims=True) * (1.0 / features) + EPSILON)
        mean = inverse * (jnp.sum(pr_ref[...], axis=1, keepdims=True) * (1.0 / features))
        inv_ref[...] = jnp.broadcast_to(inverse, (T, HD))
        mean_ref[...] = jnp.broadcast_to(mean, (T, HD))

    @pl.when(step >= HALF)
    def _():
        delta_group(
            q_ref, g_ref, gain_ref, row_ref, att_ref.at[group], inv_ref[...], mean_ref[...],
            od_ref, m_ref, gt_ref,
        )


def delta_own_kernel(
    c_ref, q_ref, g_ref, gain_ref, row_ref, att_ref, inv_ref, mean_ref, od_ref, m_ref, gt_ref
):
    delta_group(
        q_ref, g_ref, gain_ref, row_ref, att_ref, inv_ref[...], mean_ref[...], od_ref, m_ref, gt_ref
    )


def backward_kernel(
    c_ref, od_ref, q_ref, k_ref, v_ref, fw_ref, row_ref, i_ref, *rest
):
    qg_ref, ki_ref, vi_ref = rest[-3:]
    cum = columns(row_ref)
    growth = jnp.exp(cum)
    for j in range(GH):
        at = lanes(j)
        decay = decay_table(cum[:, j : j + 1], row_ref[j : j + 1, :])
        delta = od_ref[:, at]
        weights = (dot(delta, v_ref[:, at], 1, 1) * decay).astype(BF16)
        inter = growth[:, j : j + 1] * rows_by_state_t(delta, i_ref[j])
        qg_ref[:, at] = (dot(weights, k_ref[:, at], 1, 0) + inter).astype(BF16)
        ki_ref[:, at] = dot(weights, q_ref[:, at], 0, 0).astype(BF16)
        vi_ref[:, at] = dot(fw_ref[j], delta, 1, 0).astype(BF16)


def finish_kernel(own, c_ref, k_ref, v_ref, row_ref, ki_ref, vi_ref, x_ref, *rest):
    cum = columns(row_ref)
    shrink = jnp.exp(cum[T - 1 : T, :] - cum)
    if own:
        kg_ref, vg_ref = rest
    else:
        mine_ref, pair_ref, _, _, kg_ref, vg_ref, gain_ref = rest
        total = (mine_ref[...] + pair_ref[...]) * (1.0 / math.sqrt(T * DEVICES))
        at = c_ref[3] * 32 + c_ref[0] * 16
        gain_ref[...] = pltpu.roll(total, lax.rem(HD - at, HD), 1)[0:1, :16]
    for j in range(GH):
        at = lanes(j)
        scale = shrink[:, j : j + 1]
        kg_ref[:, at] = (ki_ref[:, at].astype(F32) + scale * rows_by_state_t(v_ref[:, at], x_ref[j])).astype(BF16)
        vg_ref[:, at] = (vi_ref[:, at].astype(F32) + scale * rows_by_state(k_ref[:, at], x_ref[j])).astype(BF16)


class Kept:
    def __init__(self, array):
        self.array = array
        self.shape, self.dtype = array.shape, array.dtype


def in_hbm(a):
    return pltpu.with_memory_space_constraint(a.array, pltpu.HBM) if isinstance(a, Kept) else a


def call(
    kernel, name, grid, in_specs, out_specs, out_shape, args, flops, scratch=(), aliases=None
):
    place, *args = args
    nbytes = sum(math.prod(a.shape) * a.dtype.itemsize for a in [*args, *out_shape])
    return pl.pallas_call(
        kernel,
        name=name,
        grid_spec=pltpu.PrefetchScalarGridSpec(
            num_scalar_prefetch=1,
            grid=grid,
            in_specs=in_specs,
            out_specs=out_specs,
            scratch_shapes=scratch,
        ),
        out_shape=[pltpu.HBM(s.shape, s.dtype) if isinstance(s, Kept) else s for s in out_shape],
        input_output_aliases=aliases or {},
        compiler_params=pltpu.CompilerParams(vmem_limit_bytes=16 << 20),
        cost_estimate=pl.CostEstimate(flops=flops, bytes_accessed=nbytes, transcendentals=0),
    )(place, *[in_hbm(a) for a in args])


def shape(dims, dtype=F32):
    return jax.ShapeDtypeStruct(dims, dtype)


def half_of(own, c_ref):
    return c_ref[0] if own else 1 - c_ref[0]


def wide(own, group=lambda i: i):
    return pl.BlockSpec((None, T, GW), lambda i, c: (0, 0, half_of(own, c) * HALF + group(i)))


def narrow(group=lambda i: i):
    return pl.BlockSpec((T, GW), lambda i, c: (0, group(i)))


def gain_block(own, group=lambda i: i):
    return pl.BlockSpec((1, GW), lambda i, c: (0, half_of(own, c) * HALF + group(i)))


def row_block(own, group=lambda i: i):
    return pl.BlockSpec((GH, T), lambda i, c: (half_of(own, c) * HALF + group(i), 0))


def gains_block(group=lambda i: i):
    return pl.BlockSpec((None, GH, HD), lambda i, c: (jnp.bitwise_xor(group(i), c[1] % 2), 0, 0))


def state_block(rows=HD, group=lambda i: i):
    return pl.BlockSpec((GH, rows, HD), lambda i, c: (group(i), 0, 0))


LOG_BLOCK = pl.BlockSpec((GH, 8, HD), lambda i, c: (i, 0, 0))
LOG_TAIL = pl.BlockSpec((GH, 8, HD), lambda i, c: (i, HD // 8, 0))
STAT_WHOLE = pl.BlockSpec((T, HD), lambda i, c: (0, 0))
ANY = pl.BlockSpec(memory_space=pl.ANY)
STATES = shape((NC, HD, HD))
LOGGED = shape((NC, HD + 8, HD))
LOGS = shape((NC, 8, HD))
HALF_F32 = shape((T, HALF * GW))
HALF_BF16 = shape((T, HALF * GW), BF16)
WHOLE_BF16 = shape((1, T, NG * GW), BF16)
STAT = shape((T, HD))
GAINS = shape((HALF, GH, HD))
MM = 2 * T * HD * HD * NC
SM = 2 * T * T * HD * NC


def swap_cores(values):
    return lax.ppermute(values, "core", [(0, 1), (1, 0)])


def chips_all_to_all(values):
    return lax.all_to_all(values, ("x", "y"), split_axis=0, concat_axis=0, tiled=True)


def scan_over_chips(upward, place, got, logs, gains=None):
    whole_m = pl.BlockSpec((NC, HD, HD), lambda i, c: (0, 0, 0))
    whole_l = pl.BlockSpec((NC, 8, HD), lambda i, c: (0, HD // 8 if upward else 0, 0))
    logs_out = pl.BlockSpec((NC, 8, HD), lambda i, c: (0, 0, 0))
    rows = HD if upward else HD + 8
    whole_t = pl.BlockSpec((rows, HD), lambda i, c: (0, 0))
    more = [] if upward else [gains]
    more_specs = [pl.BlockSpec((8, HD), lambda i, c: (0, 0))] * len(more)
    (total,) = call(
        functools.partial(total_kernel, upward), "half_total", (1,),
        [whole_m, whole_l] + more_specs, [whole_t], [shape((rows, HD))],
        (place, got, logs, *more), 0,
    )
    before = lax.ppermute(total, "zh", [(0, 1), (1, 0)])
    outs = [ANY] + [logs_out] * upward
    return call(
        functools.partial(scan_kernel, upward), "chip_scan", (1,),
        [whole_m, whole_l, whole_t] + more_specs, outs, [Kept(shape((NC, rows, HD))), LOGS][: len(outs)],
        (place, got, logs, before, *more), 0,
        scratch=[pltpu.VMEM((NC, rows, HD), F32), pltpu.SemaphoreType.DMA((NC,))],
    )


def per_device(queries, key_rows, value_rows, out_grad, log_decay, norm_gain):
    core = jnp.stack([lax.axis_index(a).astype(jnp.int32) for a in ("core", "dp", "zh", "y")])
    q, k, v, g = queries, key_rows, value_rows, out_grad
    gain = norm_gain.reshape(1, NG * GW)
    logs = jnp.transpose(log_decay[0])

    whole_rows = pl.BlockSpec((NG * GH, T), lambda i, c: (0, 0))
    sent, row = call(
        state_first_kernel, "states_other", (HALF,),
        [wide(False), wide(False), whole_rows], [state_block(HD + 8), whole_rows],
        [LOGGED, shape((NG * GH, T))], (core, Kept(k), Kept(v), Kept(logs)), MM,
    )
    got = swap_cores(sent)
    own, log_own = call(
        state_second_kernel, "states_own", (HALF,),
        [wide(True), wide(True), row_block(True)], [state_block(), LOG_BLOCK], [STATES, LOGS],
        (core, Kept(k), Kept(v), row), MM,
    )
    chip_total, kept_state, log_got = call(
        functools.partial(combine_kernel, True), "chip_total", (HALF,),
        [state_block(), state_block(), LOG_BLOCK, LOG_TAIL],
        [state_block(HD + 8), state_block(), LOG_BLOCK], [Kept(LOGGED), STATES, LOGS],
        (core, own, got, log_own, got), 0,
    )
    gathered = chips_all_to_all(chip_total)

    weights, inside = {}, {}
    for mine in (True, False):
        carried = [kept_state] if mine else []
        *moved, weights[mine], inside[mine] = call(
            forward_kernel, "forward_inside", (HALF,),
            [wide(mine), wide(mine), wide(mine), row_block(mine)] + [state_block()] * len(carried),
            [state_block()] * len(carried) + [pl.BlockSpec((GH, T, T), lambda i, c: (i, 0, 0)), narrow()],
            [Kept(STATES)] * len(carried) + [Kept(shape((NC, T, T), BF16)), Kept(HALF_F32)],
            (core, Kept(q), Kept(k), Kept(v), row, *carried), 2 * SM,
        )
        if mine:
            (kept_state,) = moved

    gathered, inside[True], inside[False] = lax.optimization_barrier(
        (gathered, inside[True], inside[False])
    )
    before_chips, log_chips = scan_over_chips(True, core, gathered, gathered)
    scanned = chips_all_to_all(before_chips)
    onward, state_here = call(
        functools.partial(hand_on_kernel, True), "onward", (HALF,),
        [state_block()] * 2 + [LOG_BLOCK] * 2, [state_block()] * 2, [STATES] * 2,
        (core, scanned, kept_state, log_own, log_got), 0,
    )
    state_other = swap_cores(onward)
    att_own, squares, products = call(
        attend_own_kernel, "attend_own", (HALF,),
        [wide(True), wide(True), gain_block(True), row_block(True), narrow(), state_block()],
        [narrow(), STAT_WHOLE, STAT_WHOLE], [HALF_F32, STAT, STAT],
        (core, q, g, gain, row, inside[True], state_here), 2 * MM,
    )

    def turn(i):
        return jnp.where(i < HALF, i, 2 * HALF - 1 - i)

    def first(i):
        return jnp.minimum(i, HALF - 1)

    def second(i):
        return jnp.minimum(2 * HALF - 1 - i, HALF - 1)

    delta_other, moment_sent, gains_other, inverse, mean = call(
        attend_other_kernel, "attend_other", (2 * HALF,),
        [wide(False, turn), wide(False, turn), gain_block(False, turn), row_block(False, turn), narrow(first),
         state_block(HD, first), STAT_WHOLE, STAT_WHOLE],
        [narrow(second), state_block(HD, second), gains_block(second), STAT_WHOLE, STAT_WHOLE],
        [Kept(HALF_BF16), STATES, GAINS, STAT, STAT],
        (core, q, g, gain, row, inside[False], state_other, squares, products), 3 * MM,
        scratch=[pltpu.VMEM((HALF, T, GW), F32), pltpu.VMEM((T, HD), F32), pltpu.VMEM((T, HD), F32)],
    )
    moment_got = swap_cores(moment_sent)
    delta_own, moment_own, gains_own = call(
        delta_own_kernel, "delta_own", (HALF,),
        [wide(True), wide(True), gain_block(True), row_block(True), narrow(), STAT_WHOLE, STAT_WHOLE],
        [narrow(), state_block(), gains_block()], [Kept(HALF_BF16), STATES, GAINS],
        (core, q, g, gain, row, att_own, inverse, mean), MM,
    )
    chip_moment, kept_moment = call(
        functools.partial(combine_kernel, False), "chip_moment", (HALF,),
        [state_block(), state_block(), LOG_BLOCK, LOG_BLOCK], [state_block()] * 2, [Kept(STATES)] * 2,
        (core, moment_own, moment_got, log_own, log_got), 0,
    )
    gathered_back = chips_all_to_all(chip_moment)

    near = core[0] == core[1] // 2
    gains = [*jnp.where(near, gains_own, gains_other), *jnp.where(near, gains_other, gains_own)]
    collected = gains[0]
    for distance in range(1, NG):
        collected += lax.ppermute(gains[distance], "dp", [(i, i ^ distance) for i in range(NG)])

    delta = {True: delta_own, False: delta_other}
    state = {True: Kept(state_here), False: state_other}
    query_grad, key_inside, value_inside = (), {}, {}
    for mine in (True, False):
        *query_grad, key_inside[mine], value_inside[mine] = call(
            backward_kernel, "backward_inside", (HALF,),
            [narrow(), wide(mine), wide(mine), wide(mine),
             pl.BlockSpec((GH, T, T), lambda i, c: (i, 0, 0)), row_block(mine), state_block()]
            + [ANY] * len(query_grad),
            [wide(mine), narrow(), narrow()],
            [Kept(WHOLE_BF16), Kept(HALF_BF16), Kept(HALF_BF16)],
            (core, Kept(delta[mine]), Kept(q), Kept(k), Kept(v), Kept(weights[mine]), row, state[mine],
             *[Kept(a) for a in query_grad]),
            4 * SM + 2 * MM, aliases={8: 0} if query_grad else None,
        )

    gathered_back, key_inside[True] = lax.optimization_barrier((gathered_back, key_inside[True]))
    (after_chips,) = scan_over_chips(False, core, gathered_back, log_chips, collected)
    scanned_back = chips_all_to_all(after_chips)
    scanned_back, key_inside[False] = lax.optimization_barrier((scanned_back, key_inside[False]))
    onward_back, later_here, collected = call(
        functools.partial(hand_on_kernel, False), "onward_back", (HALF,),
        [state_block()] * 2 + [LOG_BLOCK] * 2 + [LOG_TAIL],
        [state_block(), state_block(), pl.BlockSpec((8, HD), lambda i, c: (0, 0))],
        [STATES, STATES, shape((8, HD))],
        (core, scanned_back, Kept(kept_moment), log_own, log_got, scanned_back), 0,
    )
    later_other = swap_cores(onward_back)
    pair = swap_cores(collected)
    inputs = [[wide(mine), wide(mine), row_block(mine), narrow(), narrow(), state_block()] for mine in (True, False)]
    small = pl.BlockSpec((8, HD), lambda i, c: (0, 0))
    grads = call(
        functools.partial(finish_kernel, True), "finish_own", (HALF,),
        inputs[0], [wide(True)] * 2, [Kept(WHOLE_BF16)] * 2,
        (core, Kept(k), Kept(v), row, Kept(key_inside[True]), Kept(value_inside[True]), later_here), 4 * MM,
    )
    key_grad, value_grad, gain_grad = call(
        functools.partial(finish_kernel, False), "finish_other", (HALF,),
        inputs[1] + [small, small, ANY, ANY],
        [wide(False)] * 2 + [pl.BlockSpec((1, 16), lambda i, c: (0, 0))],
        [Kept(WHOLE_BF16)] * 2 + [Kept(shape((1, 16)))],
        (core, Kept(k), Kept(v), row, key_inside[False], value_inside[False], later_other,
         collected, pair, *[Kept(a) for a in grads]), 4 * MM, aliases={9: 0, 10: 1},
    )
    return query_grad[0], key_grad, value_grad, gain_grad.reshape(16)


def solution(mesh):
    fine = Mesh(mesh.devices.reshape(4, 2, 4, 4, 2), ALL)
    rows = P("dp", ("zh", "x", "y", "core"), None)
    return jax.shard_map(
        per_device,
        mesh=fine,
        in_specs=(rows,) * 5 + (P(),),
        out_specs=(rows, rows, rows, P(ALL)),
        check_vma=False,
    )
```

```python
import functools
import math

import jax
import jax.numpy as jnp
from jax import lax
from jax.experimental import pallas as pl
from jax.experimental.pallas import tpu as pltpu
from jax.sharding import Mesh, PartitionSpec as P

EPSILON = 1e-06
HIGHEST = lax.Precision.HIGHEST
F32 = jnp.float32
BF16 = jnp.bfloat16
T = 192
HD = 128
GH = 8
GW = GH * HD
NG = 4
HALF = NG // 2
DEVICES = 256
NC = 16
ALL = ("dp", "zh", "x", "y", "core")


def dot(a, b, ca, cb):
    return lax.dot_general(a, b, (((ca,), (cb,)), ((), ())), preferred_element_type=F32)


def lanes(j):
    return slice(j * HD, (j + 1) * HD)


def split_state(state, axis):
    high = state.astype(BF16)
    low = (state - high.astype(F32)).astype(BF16)
    return jnp.concatenate([high, low], axis)


def rows_by_state(rows, state):
    return dot(jnp.concatenate([rows, rows], 1), split_state(state, 0), 1, 0)


def rows_by_state_t(rows, state):
    return dot(jnp.concatenate([rows, rows], 1), split_state(state, 1), 1, 1)


def columns(row_ref):
    return jnp.transpose(row_ref[...])


def decay_table(col, row):
    row_ids = lax.broadcasted_iota(jnp.int32, (T, T), 0)
    col_ids = lax.broadcasted_iota(jnp.int32, (T, T), 1)
    return jnp.exp(jnp.where(row_ids >= col_ids, col - row, -jnp.inf))


def scaled_columns(x, factors):
    return (jnp.transpose(x).astype(F32) * factors).astype(BF16)


def states_of(k_ref, v_ref, row_ref, store):
    rows = row_ref[...]
    last = rows[:, T - 1 : T]
    shrink = jnp.exp(last - rows)
    for j in range(GH):
        late = scaled_columns(k_ref[:, lanes(j)], shrink[j : j + 1, :])
        log = jnp.broadcast_to(last[j : j + 1, :], (8, HD))
        store(j, dot(late, v_ref[:, lanes(j)], 1, 0), log)


def state_first_kernel(c_ref, k_ref, v_ref, ld_ref, s_ref, row_ref):
    i = pl.program_id(0)

    @pl.when(i == 0)
    def _():
        upper = (
            lax.broadcasted_iota(jnp.int32, (T, T), 0) <= lax.broadcasted_iota(jnp.int32, (T, T), 1)
        ).astype(F32)
        logs = ld_ref[...]
        row_ref[...] = lax.dot_general(
            logs, upper, (((1,), (0,)), ((), ())), precision=HIGHEST, preferred_element_type=F32
        )

    def store(j, state, log):
        s_ref[j, :HD, :] = state
        s_ref[j, HD:, :] = log

    group = (1 - c_ref[0]) * HALF + i
    states_of(k_ref, v_ref, row_ref.at[pl.ds(pl.multiple_of(group * GH, GH), GH)], store)


def state_second_kernel(c_ref, k_ref, v_ref, row_ref, s_ref, l_ref):
    def store(j, state, log):
        s_ref[j] = state
        l_ref[j] = log

    states_of(k_ref, v_ref, row_ref, store)


def combine_kernel(upward, c_ref, own_ref, got_ref, lo_ref, lg_ref, p_ref, kept_ref, log_ref=None):
    first = c_ref[0] == 0 if upward else c_ref[0] == 1
    for j in range(GH):
        log_own, log_got = lo_ref[j, 0:1, :], lg_ref[j, 0:1, :]
        scale_own = jnp.where(first, jnp.exp(log_got), 1.0)
        scale_got = jnp.where(first, 1.0, jnp.exp(log_own))
        p_ref[j, :HD, :] = scale_own * own_ref[j] + scale_got * got_ref[j]
        kept_ref[j] = jnp.where(first, own_ref[j], got_ref[j])
        if upward:
            p_ref[j, HD:, :] = lo_ref[j] + lg_ref[j]
            log_ref[j] = lg_ref[j]


def total_kernel(upward, c_ref, m_ref, l_ref, *rest):
    run = jnp.zeros((HD, HD), F32)
    for i in range(NC) if upward else reversed(range(NC)):
        run = jnp.exp(l_ref[i, 0:1, :]) * run + m_ref[i]
    t_ref = rest[-1]
    t_ref[:HD, :] = run
    if not upward:
        t_ref[HD:, :] = rest[0][...]


def scan_kernel(upward, c_ref, m_ref, l_ref, t_ref, *rest):
    if upward:
        o_ref, log_ref = rest
        log_ref[...] = l_ref[...]
    else:
        gain_ref, o_ref = rest
        both = gain_ref[...] + t_ref[HD:, :]
    run = jnp.where(c_ref[2] == (1 if upward else 0), t_ref[:HD, :], 0.0)
    for i in range(NC) if upward else reversed(range(NC)):
        o_ref[i, :HD, :] = run
        if not upward:
            x = i // 4
            row = jnp.where(c_ref[2] == 0, both[x : x + 1, :], both[4 + x : 5 + x, :])
            o_ref[i, HD:, :] = jnp.broadcast_to(row, (8, HD))
        run = jnp.exp(l_ref[i, 0:1, :]) * run + m_ref[i]


def hand_on_kernel(upward, c_ref, d_ref, kept_ref, lo_ref, lg_ref, *rest):
    if upward:
        send_ref, state_ref = rest
    else:
        gains_ref, send_ref, state_ref, sum_ref = rest
        part = gains_ref[0]
        for j in range(1, GH):
            part += gains_ref[j]

        @pl.when(pl.program_id(0) == 0)
        def _():
            sum_ref[...] = part

        @pl.when(pl.program_id(0) > 0)
        def _():
            sum_ref[...] += part

    at_edge = c_ref[0] == (0 if upward else 1)
    for j in range(GH):
        edge = d_ref[j]
        passed = jnp.exp(jnp.where(at_edge, lo_ref[j, 0:1, :], lg_ref[j, 0:1, :])) * edge + kept_ref[j]
        send_ref[j] = jnp.where(at_edge, passed, edge)
        state_ref[j] = jnp.where(at_edge, edge, passed)


def forward_kernel(c_ref, q_ref, k_ref, v_ref, row_ref, *rest):
    fw_ref, in_ref = rest[-2:]
    if len(rest) > 2:
        rest[1][...] = rest[0][...]
    cum = columns(row_ref)
    for j in range(GH):
        decay = decay_table(cum[:, j : j + 1], row_ref[j : j + 1, :])
        scores = dot(q_ref[:, lanes(j)], k_ref[:, lanes(j)], 1, 1)
        weights = (scores * decay).astype(BF16)
        fw_ref[j] = jnp.transpose(weights)
        in_ref[:, lanes(j)] = dot(weights, v_ref[:, lanes(j)], 1, 0)


def attend_group(q_ref, g_ref, gain_ref, cum, in_ref, x_ref, att_ref, sq_ref, pr_ref):
    growth = jnp.exp(cum)
    squares = jnp.zeros((T, HD), F32)
    products = jnp.zeros((T, HD), F32)
    for j in range(GH):
        att = in_ref[:, lanes(j)] + growth[:, j : j + 1] * rows_by_state(q_ref[:, lanes(j)], x_ref[j])
        att_ref[:, lanes(j)] = att
        squares += att * att
        products += att * (gain_ref[:, lanes(j)] * g_ref[:, lanes(j)].astype(F32))
    sq_ref[...] += squares
    pr_ref[...] += products


def attend_own_kernel(
    c_ref, q_ref, g_ref, gain_ref, row_ref, in_ref, x_ref, att_ref, sq_ref, pr_ref
):
    @pl.when(pl.program_id(0) == 0)
    def _():
        sq_ref[...] = jnp.zeros_like(sq_ref)
        pr_ref[...] = jnp.zeros_like(pr_ref)

    attend_group(
        q_ref, g_ref, gain_ref, columns(row_ref), in_ref, x_ref, att_ref, sq_ref, pr_ref
    )


def delta_group(q_ref, g_ref, gain_ref, row_ref, att_ref, inverse, mean, od_ref, m_ref, gt_ref):
    growth = jnp.exp(row_ref[...])
    for j in range(GH):
        grad = g_ref[:, lanes(j)].astype(F32)
        normed = att_ref[:, lanes(j)] * inverse
        delta = (inverse * (gain_ref[:, lanes(j)] * grad - normed * mean)).astype(BF16)
        od_ref[:, lanes(j)] = delta
        gt_ref[j : j + 1, :] = jnp.sum(grad * normed, axis=0, keepdims=True)
        early = scaled_columns(q_ref[:, lanes(j)], growth[j : j + 1, :])
        m_ref[j] = dot(early, delta, 1, 0)


def attend_other_kernel(
    c_ref, q_ref, g_ref, gain_ref, row_ref, in_ref, i_ref, sq_in, pr_in,
    od_ref, m_ref, gt_ref, inv_ref, mean_ref, att_ref, sq_ref, pr_ref,
):
    step = pl.program_id(0)
    group = jnp.where(step < HALF, step, 2 * HALF - 1 - step)

    @pl.when(step == 0)
    def _():
        sq_ref[...] = sq_in[...]
        pr_ref[...] = pr_in[...]

    @pl.when(step < HALF)
    def _():
        attend_group(
            q_ref, g_ref, gain_ref, columns(row_ref), in_ref, i_ref, att_ref.at[group], sq_ref, pr_ref
        )

    @pl.when(step == HALF)
    def _():
        features = NG * GW
        inverse = lax.rsqrt(jnp.sum(sq_ref[...], axis=1, keepdims=True) * (1.0 / features) + EPSILON)
        mean = inverse * (jnp.sum(pr_ref[...], axis=1, keepdims=True) * (1.0 / features))
        inv_ref[...] = jnp.broadcast_to(inverse, (T, HD))
        mean_ref[...] = jnp.broadcast_to(mean, (T, HD))

    @pl.when(step >= HALF)
    def _():
        delta_group(
            q_ref, g_ref, gain_ref, row_ref, att_ref.at[group], inv_ref[...], mean_ref[...],
            od_ref, m_ref, gt_ref,
        )


def delta_own_kernel(
    c_ref, q_ref, g_ref, gain_ref, row_ref, att_ref, inv_ref, mean_ref, od_ref, m_ref, gt_ref
):
    delta_group(
        q_ref, g_ref, gain_ref, row_ref, att_ref, inv_ref[...], mean_ref[...], od_ref, m_ref, gt_ref
    )


def backward_kernel(
    c_ref, od_ref, q_ref, k_ref, v_ref, fw_ref, row_ref, i_ref, *rest
):
    qg_ref, ki_ref, vi_ref = rest[-3:]
    cum = columns(row_ref)
    growth = jnp.exp(cum)
    for j in range(GH):
        at = lanes(j)
        decay = decay_table(cum[:, j : j + 1], row_ref[j : j + 1, :])
        delta = od_ref[:, at]
        weights = (dot(delta, v_ref[:, at], 1, 1) * decay).astype(BF16)
        inter = growth[:, j : j + 1] * rows_by_state_t(delta, i_ref[j])
        qg_ref[:, at] = (dot(weights, k_ref[:, at], 1, 0) + inter).astype(BF16)
        ki_ref[:, at] = dot(weights, q_ref[:, at], 0, 0).astype(BF16)
        vi_ref[:, at] = dot(fw_ref[j], delta, 1, 0).astype(BF16)


def finish_kernel(own, c_ref, k_ref, v_ref, row_ref, ki_ref, vi_ref, x_ref, *rest):
    cum = columns(row_ref)
    shrink = jnp.exp(cum[T - 1 : T, :] - cum)
    if own:
        kg_ref, vg_ref = rest
    else:
        mine_ref, pair_ref, _, _, kg_ref, vg_ref, gain_ref = rest
        total = (mine_ref[...] + pair_ref[...]) * (1.0 / math.sqrt(T * DEVICES))
        at = c_ref[3] * 32 + c_ref[0] * 16
        gain_ref[...] = pltpu.roll(total, lax.rem(HD - at, HD), 1)[0:1, :16]
    for j in range(GH):
        at = lanes(j)
        scale = shrink[:, j : j + 1]
        kg_ref[:, at] = (ki_ref[:, at].astype(F32) + scale * rows_by_state_t(v_ref[:, at], x_ref[j])).astype(BF16)
        vg_ref[:, at] = (vi_ref[:, at].astype(F32) + scale * rows_by_state(k_ref[:, at], x_ref[j])).astype(BF16)


class Kept:
    def __init__(self, array):
        self.array = array
        self.shape, self.dtype = array.shape, array.dtype


def in_hbm(a):
    return pltpu.with_memory_space_constraint(a.array, pltpu.HBM) if isinstance(a, Kept) else a


def call(
    kernel, name, grid, in_specs, out_specs, out_shape, args, flops, scratch=(), aliases=None
):
    place, *args = args
    nbytes = sum(math.prod(a.shape) * a.dtype.itemsize for a in [*args, *out_shape])
    return pl.pallas_call(
        kernel,
        name=name,
        grid_spec=pltpu.PrefetchScalarGridSpec(
            num_scalar_prefetch=1,
            grid=grid,
            in_specs=in_specs,
            out_specs=out_specs,
            scratch_shapes=scratch,
        ),
        out_shape=[pltpu.HBM(s.shape, s.dtype) if isinstance(s, Kept) else s for s in out_shape],
        input_output_aliases=aliases or {},
        compiler_params=pltpu.CompilerParams(vmem_limit_bytes=16 << 20),
        cost_estimate=pl.CostEstimate(flops=flops, bytes_accessed=nbytes, transcendentals=0),
    )(place, *[in_hbm(a) for a in args])


def shape(dims, dtype=F32):
    return jax.ShapeDtypeStruct(dims, dtype)


def half_of(own, c_ref):
    return c_ref[0] if own else 1 - c_ref[0]


def wide(own, group=lambda i: i):
    return pl.BlockSpec((None, T, GW), lambda i, c: (0, 0, half_of(own, c) * HALF + group(i)))


def narrow(group=lambda i: i):
    return pl.BlockSpec((T, GW), lambda i, c: (0, group(i)))


def gain_block(own, group=lambda i: i):
    return pl.BlockSpec((1, GW), lambda i, c: (0, half_of(own, c) * HALF + group(i)))


def row_block(own, group=lambda i: i):
    return pl.BlockSpec((GH, T), lambda i, c: (half_of(own, c) * HALF + group(i), 0))


def gains_block(group=lambda i: i):
    return pl.BlockSpec((None, GH, HD), lambda i, c: (jnp.bitwise_xor(group(i), c[1] % 2), 0, 0))


def state_block(rows=HD, group=lambda i: i):
    return pl.BlockSpec((GH, rows, HD), lambda i, c: (group(i), 0, 0))


LOG_BLOCK = pl.BlockSpec((GH, 8, HD), lambda i, c: (i, 0, 0))
LOG_TAIL = pl.BlockSpec((GH, 8, HD), lambda i, c: (i, HD // 8, 0))
STAT_WHOLE = pl.BlockSpec((T, HD), lambda i, c: (0, 0))
ANY = pl.BlockSpec(memory_space=pl.ANY)
STATES = shape((NC, HD, HD))
LOGGED = shape((NC, HD + 8, HD))
LOGS = shape((NC, 8, HD))
HALF_F32 = shape((T, HALF * GW))
HALF_BF16 = shape((T, HALF * GW), BF16)
WHOLE_BF16 = shape((1, T, NG * GW), BF16)
STAT = shape((T, HD))
GAINS = shape((HALF, GH, HD))
MM = 2 * T * HD * HD * NC
SM = 2 * T * T * HD * NC


def swap_cores(values):
    return lax.ppermute(values, "core", [(0, 1), (1, 0)])


def chips_all_to_all(values):
    return lax.all_to_all(values, ("x", "y"), split_axis=0, concat_axis=0, tiled=True)


def scan_over_chips(upward, place, got, logs, gains=None):
    whole_m = pl.BlockSpec((NC, HD, HD), lambda i, c: (0, 0, 0))
    whole_l = pl.BlockSpec((NC, 8, HD), lambda i, c: (0, HD // 8 if upward else 0, 0))
    logs_out = pl.BlockSpec((NC, 8, HD), lambda i, c: (0, 0, 0))
    rows = HD if upward else HD + 8
    whole_t = pl.BlockSpec((rows, HD), lambda i, c: (0, 0))
    more = [] if upward else [gains]
    more_specs = [pl.BlockSpec((8, HD), lambda i, c: (0, 0))] * len(more)
    (total,) = call(
        functools.partial(total_kernel, upward), "half_total", (1,),
        [whole_m, whole_l] + more_specs, [whole_t], [shape((rows, HD))],
        (place, got, logs, *more), 0,
    )
    before = lax.ppermute(total, "zh", [(0, 1), (1, 0)])
    outs = [pl.BlockSpec((NC, rows, HD), lambda i, c: (0, 0, 0))] + [logs_out] * upward
    scanned = shape((NC, rows, HD))
    return call(
        functools.partial(scan_kernel, upward), "chip_scan", (1,),
        [whole_m, whole_l, whole_t] + more_specs, outs, [scanned, LOGS] if upward else [Kept(scanned)],
        (place, got, logs, before, *more), 0,
    )


def per_device(queries, key_rows, value_rows, out_grad, log_decay, norm_gain):
    core = jnp.stack([lax.axis_index(a).astype(jnp.int32) for a in ("core", "dp", "zh", "y")])
    q, k, v, g = queries, key_rows, value_rows, out_grad
    gain = norm_gain.reshape(1, NG * GW)
    logs = jnp.transpose(log_decay[0])

    whole_rows = pl.BlockSpec((NG * GH, T), lambda i, c: (0, 0))
    sent, row = call(
        state_first_kernel, "states_other", (HALF,),
        [wide(False), wide(False), whole_rows], [state_block(HD + 8), whole_rows],
        [LOGGED, shape((NG * GH, T))], (core, Kept(k), Kept(v), Kept(logs)), MM,
    )
    got = swap_cores(sent)
    own, log_own = call(
        state_second_kernel, "states_own", (HALF,),
        [wide(True), wide(True), row_block(True)], [state_block(), LOG_BLOCK], [STATES, LOGS],
        (core, Kept(k), Kept(v), row), MM,
    )
    chip_total, kept_state, log_got = call(
        functools.partial(combine_kernel, True), "chip_total", (HALF,),
        [state_block(), state_block(), LOG_BLOCK, LOG_TAIL],
        [state_block(HD + 8), state_block(), LOG_BLOCK], [Kept(LOGGED), STATES, LOGS],
        (core, own, got, log_own, got), 0,
    )
    gathered = chips_all_to_all(chip_total)

    weights, inside = {}, {}
    for mine in (True, False):
        carried = [kept_state] if mine else []
        *moved, weights[mine], inside[mine] = call(
            forward_kernel, "forward_inside", (HALF,),
            [wide(mine), wide(mine), wide(mine), row_block(mine)] + [state_block()] * len(carried),
            [state_block()] * len(carried) + [pl.BlockSpec((GH, T, T), lambda i, c: (i, 0, 0)), narrow()],
            [Kept(STATES)] * len(carried) + [Kept(shape((NC, T, T), BF16)), Kept(HALF_F32)],
            (core, Kept(q), Kept(k), Kept(v), row, *carried), 2 * SM,
        )
        if mine:
            (kept_state,) = moved

    gathered, inside[True], inside[False] = lax.optimization_barrier(
        (gathered, inside[True], inside[False])
    )
    before_chips, log_chips = scan_over_chips(True, core, gathered, gathered)
    scanned = chips_all_to_all(before_chips)
    onward, state_here = call(
        functools.partial(hand_on_kernel, True), "onward", (HALF,),
        [state_block()] * 2 + [LOG_BLOCK] * 2, [state_block()] * 2, [STATES] * 2,
        (core, scanned, kept_state, log_own, log_got), 0,
    )
    state_other = swap_cores(onward)
    att_own, squares, products = call(
        attend_own_kernel, "attend_own", (HALF,),
        [wide(True), wide(True), gain_block(True), row_block(True), narrow(), state_block()],
        [narrow(), STAT_WHOLE, STAT_WHOLE], [HALF_F32, STAT, STAT],
        (core, q, g, gain, row, inside[True], state_here), 2 * MM,
    )

    def turn(i):
        return jnp.where(i < HALF, i, 2 * HALF - 1 - i)

    def first(i):
        return jnp.minimum(i, HALF - 1)

    def second(i):
        return jnp.minimum(2 * HALF - 1 - i, HALF - 1)

    delta_other, moment_sent, gains_other, inverse, mean = call(
        attend_other_kernel, "attend_other", (2 * HALF,),
        [wide(False, turn), wide(False, turn), gain_block(False, turn), row_block(False, turn), narrow(first),
         state_block(HD, first), STAT_WHOLE, STAT_WHOLE],
        [narrow(second), state_block(HD, second), gains_block(second), STAT_WHOLE, STAT_WHOLE],
        [Kept(HALF_BF16), STATES, GAINS, STAT, STAT],
        (core, q, g, gain, row, inside[False], state_other, squares, products), 3 * MM,
        scratch=[pltpu.VMEM((HALF, T, GW), F32), pltpu.VMEM((T, HD), F32), pltpu.VMEM((T, HD), F32)],
    )
    moment_got = swap_cores(moment_sent)
    delta_own, moment_own, gains_own = call(
        delta_own_kernel, "delta_own", (HALF,),
        [wide(True), wide(True), gain_block(True), row_block(True), narrow(), STAT_WHOLE, STAT_WHOLE],
        [narrow(), state_block(), gains_block()], [Kept(HALF_BF16), STATES, GAINS],
        (core, q, g, gain, row, att_own, inverse, mean), MM,
    )
    chip_moment, kept_moment = call(
        functools.partial(combine_kernel, False), "chip_moment", (HALF,),
        [state_block(), state_block(), LOG_BLOCK, LOG_BLOCK], [state_block()] * 2, [Kept(STATES)] * 2,
        (core, moment_own, moment_got, log_own, log_got), 0,
    )
    gathered_back = chips_all_to_all(chip_moment)

    near = core[0] == core[1] // 2
    gains = [*jnp.where(near, gains_own, gains_other), *jnp.where(near, gains_other, gains_own)]
    collected = gains[0]
    for distance in range(1, NG):
        collected += lax.ppermute(gains[distance], "dp", [(i, i ^ distance) for i in range(NG)])

    delta = {True: delta_own, False: delta_other}
    state = {True: Kept(state_here), False: state_other}
    query_grad, key_inside, value_inside = (), {}, {}
    for mine in (True, False):
        *query_grad, key_inside[mine], value_inside[mine] = call(
            backward_kernel, "backward_inside", (HALF,),
            [narrow(), wide(mine), wide(mine), wide(mine),
             pl.BlockSpec((GH, T, T), lambda i, c: (i, 0, 0)), row_block(mine), state_block()]
            + [ANY] * len(query_grad),
            [wide(mine), narrow(), narrow()],
            [Kept(WHOLE_BF16), Kept(HALF_BF16), Kept(HALF_BF16)],
            (core, Kept(delta[mine]), Kept(q), Kept(k), Kept(v), Kept(weights[mine]), row, state[mine],
             *[Kept(a) for a in query_grad]),
            4 * SM + 2 * MM, aliases={8: 0} if query_grad else None,
        )

    gathered_back, key_inside[True] = lax.optimization_barrier((gathered_back, key_inside[True]))
    (after_chips,) = scan_over_chips(False, core, gathered_back, log_chips, collected)
    scanned_back = chips_all_to_all(after_chips)
    scanned_back, key_inside[False] = lax.optimization_barrier((scanned_back, key_inside[False]))
    onward_back, later_here, collected = call(
        functools.partial(hand_on_kernel, False), "onward_back", (HALF,),
        [state_block()] * 2 + [LOG_BLOCK] * 2 + [LOG_TAIL],
        [state_block(), state_block(), pl.BlockSpec((8, HD), lambda i, c: (0, 0))],
        [STATES, STATES, shape((8, HD))],
        (core, scanned_back, Kept(kept_moment), log_own, log_got, scanned_back), 0,
    )
    later_other = swap_cores(onward_back)
    pair = swap_cores(collected)
    inputs = [[wide(mine), wide(mine), row_block(mine), narrow(), narrow(), state_block()] for mine in (True, False)]
    small = pl.BlockSpec((8, HD), lambda i, c: (0, 0))
    grads = call(
        functools.partial(finish_kernel, True), "finish_own", (HALF,),
        inputs[0], [wide(True)] * 2, [Kept(WHOLE_BF16)] * 2,
        (core, Kept(k), Kept(v), row, Kept(key_inside[True]), Kept(value_inside[True]), later_here), 4 * MM,
    )
    key_grad, value_grad, gain_grad = call(
        functools.partial(finish_kernel, False), "finish_other", (HALF,),
        inputs[1] + [small, small, ANY, ANY],
        [wide(False)] * 2 + [pl.BlockSpec((1, 16), lambda i, c: (0, 0))],
        [Kept(WHOLE_BF16)] * 2 + [Kept(shape((1, 16)))],
        (core, Kept(k), Kept(v), row, key_inside[False], value_inside[False], later_other,
         collected, pair, *[Kept(a) for a in grads]), 4 * MM, aliases={9: 0, 10: 1},
    )
    return query_grad[0], key_grad, value_grad, gain_grad.reshape(16)


def solution(mesh):
    fine = Mesh(mesh.devices.reshape(4, 2, 4, 4, 2), ALL)
    rows = P("dp", ("zh", "x", "y", "core"), None)
    return jax.shard_map(
        per_device,
        mesh=fine,
        in_specs=(rows,) * 5 + (P(),),
        out_specs=(rows, rows, rows, P(ALL)),
        check_vma=False,
    )
```
